256 devices in a mesh: spec: 16 (over y, x), grid: 16 (over z, core).
Axes of the slice: x: 4, y: 4, z: 8, core: 2. Of those that a mesh axis runs over, the one named last changes fastest.
Arguments:
- spectrum: float32 [1296, 64, 4096], P('spec', None, 'grid'), may hold values from 0.05 to 1
- group_speed: float32 [36], replicated, may hold values from 0.3 to 0.9
- depth_factor: float32 [64, 4096], P(None, 'grid'), may hold values from 0.4 to 1
- sea_mask: int32 [64, 4096], P(None, 'grid'), may hold values 0 or 1
- interaction: bfloat16 [1296, 1296], replicated, may hold values from -0.15625 to 0.15625
- wind_speed: float32 [64, 4096], P('spec', 'grid'), may hold values from 0.5 to 1.5
- wind_dir: float32 [64, 4096], P('spec', 'grid'), may hold values from -3.140625 to 3.140625
- nest_owner: int32 [32768, 1], P(('spec', 'grid')), may hold values from 0 to 15; in each aligned block of 128 rows (0 to 127, 128 to 255, ...) at most 16 rows name the same one
- nest_point: int32 [32768], P(('spec', 'grid')), may hold values from 0 to 127
- nest_cell: int32 [32768], P(('spec', 'grid')), may hold values from 0 to 1023
- weight_index: int32 [32768], P(('spec', 'grid')), may hold values from 0 to 63
- weight_table: float32 [64], replicated, may hold values from 0.2 to 1
Outputs:
- spectrum_out: float32 [1296, 64, 4096], P(None, 'spec', 'grid')
- nest_spectra: float32 [1296, 32768], P(None, ('spec', 'grid'))
The draws below stay inside these ranges and needn't reach their ends.
Inputs may be any that keep to these rules, and one draw needn't show every extreme that they name: `nest_owner`: among the 128 entries of one device no owner is named by more than 16 entries, a bound that some block reaches.
All inputs are finite; a program needn't handle non-finite values. No bound on the sum of `sea_mask` on one device may be relied on, other than what follows from the above.
Results may differ from the reference program's by a relative error of at most 0.0035.
Values may be sent and summed in bfloat16 or wider, within the bound.
A program may use at most 128 MiB of HBM per device.

```python
import math
import jax
import jax.numpy as jnp
import numpy as np
from jax import lax

NDIR = 36
NFREQ = 36
LAT = 64
LON_DEV = 256
SOURCE_STEPS = 4
NE = 128
NB_OWN = 128
NWT = 64
CAP = 16
LON = 4096
ROWS_DEV = 4
CELLS_DEV = 1024
ENTRIES = 32768
NBP = 32768
N_GRID = 16


def place_ends(drawn, stream_key, smallest, high):
    longest = drawn.shape.index(max(drawn.shape))
    spots = []
    for shift in (0, 1):
        where = [jax.random.randint(jax.random.fold_in(stream_key, axis), (), 0, length) for axis, length in enumerate(drawn.shape)]
        where[longest] = (where[longest] + shift) % drawn.shape[longest]
        spots.append(tuple(where))
    return drawn.at[spots[0]].set(smallest).at[spots[1]].set(high)


def block_scale(rng, shape, shards, least, high):
    def one(axis_at, shards_of):
        steps = jax.random.uniform(jax.random.fold_in(jax.random.fold_in(rng, 6), axis_at), (shards_of,), jnp.float32, least / len(shards), high / len(shards))
        return jnp.repeat(jnp.exp(steps), shape[axis_at] // shards_of).reshape((-1,) + (1,) * (len(shape) - axis_at - 1))

    factor_of = one(*shards[0])
    for cut in shards[1:]:
        factor_of = factor_of * one(*cut)
    return factor_of


def assign_block(key, own, number, rows, number_of, top, reach, lean):
    ranking = jax.random.permutation(key, number_of)
    packed, usual = portions_of(number_of, rows * top, reach, lean, True), portions_of(number_of, rows * top, reach, lean, False)
    places = jnp.arange(number_of)

    def named(lengths, rotation):
        used = int((lengths > 0).sum())
        fixed = max(1, used // 4)
        moved = fixed + (places - fixed + rotation * (used - fixed)) % max(1, number_of - fixed)
        return jnp.zeros((number_of,), jnp.int32).at[ranking[jnp.where(places < fixed, places, moved)]].set(jnp.asarray(lengths, jnp.int32))

    lengths = jnp.where(number % 4 == 0, named(packed, number // 4), named(usual, number - number // 4 - 1))
    mixed = jax.random.permutation(jax.random.fold_in(own, 3), number_of)
    source_of, sink = mixed[0:number_of // 2 * 2:2], mixed[1:number_of // 2 * 2:2]
    slack = jnp.minimum(lengths[source_of] - 1, reach - lengths[sink]) // 2
    slack = jnp.where((source_of == ranking[0]) | (sink == ranking[0]) | (lengths[sink] == 0), 0, jnp.maximum(slack, 0))
    moved = jax.random.randint(jax.random.fold_in(own, 4), (number_of // 2,), 0, 1 << 20) % (slack + 1)
    lengths = lengths.at[source_of].add(-moved).at[sink].add(moved)
    items = jnp.searchsorted(jnp.cumsum(lengths), jnp.arange(rows * top), side="right").astype(jnp.int32)
    table = items.reshape(top, rows).T
    table = table[jax.random.permutation(jax.random.fold_in(own, 1), rows)]
    rotation = jax.random.randint(jax.random.fold_in(own, 2), (rows, 1), 0, top)
    return jnp.take_along_axis(table, (jnp.arange(top)[None, :] + rotation) % top, axis=1)


def portions_of(number_of, total, reach, skew, full):
    weights = [(1 << 20) // math.isqrt(grade ** skew) + 1 for grade in range(1, number_of + 1)]
    largest = reach if full else min(reach, max(-(-total // number_of), total * weights[0] // sum(weights)))
    least = 1 if total - largest >= number_of - 1 else 0
    given, rest = [largest] + [least] * (number_of - 1), total - largest - least * (number_of - 1)
    while rest > 0:
        free = [i for i in range(1, number_of) if given[i] < largest] or [i for i in range(1, number_of) if given[i] < reach]
        whole, budget = sum([weights[i] for i in free]), rest
        for i in free:
            extra = min(reach - given[i], max(1, budget * weights[i] // whole), rest)
            given[i] = given[i] + extra
            rest = rest - extra
    return np.array(given)


def bell_draw(key, shape, deviation, reach, kind=jnp.bfloat16):
    values = deviation * jax.random.normal(key, shape, jnp.float32)
    return jnp.clip(values, min=-reach, max=reach).astype(kind)


def setup_inputs(seed: int = 0) -> dict:
    splits = jax.random.split(jax.random.key(seed), 13)
    spectrum = jnp.clip(jnp.exp(math.log(1.0) - 2.9957323 * jax.random.uniform(splits[0], (NDIR * NFREQ, LAT, LON), jnp.float32) ** block_scale(splits[0], (NDIR * NFREQ, LAT, LON), ((0, 16), (2, 16)), -0.2, 0.2)), 0.05, 1.0)
    group_speed = jnp.clip(jax.random.uniform(splits[1], (NFREQ,), jnp.float32, 0.3, 0.9), 0.3, 0.9)
    depth_factor = jnp.clip(0.4 + 0.6 * jax.random.uniform(splits[2], (LAT, LON), jnp.float32) ** block_scale(splits[2], (LAT, LON), ((1, 16),), -0.2, 0.2), 0.4, 1.0)
    sea_mask = place_ends((jax.random.randint(splits[3], (LAT, LON), 0, 10) < 7).astype(jnp.int32), jax.random.fold_in(splits[3], 1), 0, 1)
    interaction = bell_draw(splits[4], (NDIR * NFREQ, NDIR * NFREQ), (NDIR * NFREQ) ** -0.5, 0.15625)
    wind_speed = jnp.clip(0.5 + 1.0 * jax.random.uniform(splits[5], (LAT, LON), jnp.float32) ** block_scale(splits[5], (LAT, LON), ((0, 16), (1, 16)), -0.2, 0.2), 0.5, 1.5)
    wind_dir = jnp.clip(jax.random.uniform(splits[6], (LAT, LON), jnp.float32, -3.140625, 3.140625), -3.140625, 3.140625)
    nest_owner_keys = jax.random.split(jax.random.fold_in(splits[7], 1), ENTRIES // NE)
    nest_owner_turns = jax.random.permutation(jax.random.fold_in(splits[7], 3), ENTRIES // NE)
    nest_owner = jax.vmap(lambda own, number: assign_block(jax.random.fold_in(splits[7], 2), own, number, NE, N_GRID, 1, CAP, 2))(nest_owner_keys, nest_owner_turns).reshape((ENTRIES, 1))
    nest_point = place_ends(jax.random.randint(splits[8], (ENTRIES,), 0, NB_OWN), jax.random.fold_in(splits[8], 1), 0, NB_OWN - 1).astype(jnp.int32)
    nest_cell = place_ends(jax.random.randint(splits[9], (ENTRIES,), 0, CELLS_DEV), jax.random.fold_in(splits[9], 1), 0, CELLS_DEV - 1).astype(jnp.int32)
    weight_index = place_ends(jax.random.randint(splits[10], (ENTRIES,), 0, NWT), jax.random.fold_in(splits[10], 1), 0, NWT - 1).astype(jnp.int32)
    weight_table = jnp.clip(jax.random.uniform(splits[11], (NWT,), jnp.float32, 0.2, 1.0), 0.2, 1.0)
    return {"spectrum": spectrum, "group_speed": group_speed, "depth_factor": depth_factor, "sea_mask": sea_mask, "interaction": interaction, "wind_speed": wind_speed, "wind_dir": wind_dir, "nest_owner": nest_owner, "nest_point": nest_point, "nest_cell": nest_cell, "weight_index": weight_index, "weight_table": weight_table}


TWO_PI = 2.0 * math.pi
RATE = 0.2
WIND_GAIN = 0.8
WHITECAP = 1.0
EPSILON = 1e-06

def headings(number, freq_count, dir_count):
    component = jnp.arange(number, dtype=jnp.int32)
    heading = TWO_PI * ((component // freq_count).astype(jnp.float32) + 0.5) / dir_count
    return (heading, component % freq_count)

def north_south(part, rate_y, factor, sea_float):
    flux_y = rate_y[:, None, None] * factor[None] * part
    zero_row = jnp.zeros_like(flux_y[:, :1])
    before = jnp.concatenate([zero_row, flux_y[:, :-1]], axis=1)
    beyond = jnp.concatenate([flux_y[:, 1:], zero_row], axis=1)
    change = jnp.where(rate_y[:, None, None] > 0, flux_y - before, beyond - flux_y)
    return (sea_float[None] * (part - change)).astype(jnp.bfloat16)

def wind_term(heading, freq_index, freq_count, speed_flat, direction_flat):
    alignment = jnp.cos(heading)[:, None] * jnp.cos(direction_flat)[None] + jnp.sin(heading)[:, None] * jnp.sin(direction_flat)[None]
    scale_freq = (freq_index + 1).astype(jnp.float32) / freq_count
    return WIND_GAIN * scale_freq[:, None] * speed_flat[None] * jnp.maximum(alignment, 0.0)

def reference(spectrum, group_speed, depth_factor, sea_mask, interaction, wind_speed, wind_dir, nest_owner, nest_point, nest_cell, weight_index, weight_table):
    comp_total = NDIR * NFREQ
    heading, freq_index = headings(comp_total, NFREQ, NDIR)
    group_rate = group_speed[freq_index]
    rate_x = group_rate * jnp.cos(heading)
    rate_y = group_rate * jnp.sin(heading)
    sea_float = sea_mask.astype(jnp.float32)
    factor = depth_factor * sea_float
    flux_x = rate_x[:, None, None] * factor[None] * spectrum
    west_flux = jnp.roll(flux_x, 1, axis=2)
    east_flux = jnp.roll(flux_x, -1, axis=2)
    change = jnp.where(rate_x[:, None, None] > 0, flux_x - west_flux, east_flux - flux_x)
    after_x = sea_float[None] * (spectrum - change)
    propagated = lax.optimization_barrier(north_south(after_x, rate_y, factor, sea_float))
    spectra_now = propagated.astype(jnp.float32).reshape(comp_total, LAT * LON)
    sea_cells = sea_float.reshape(-1)
    wind_gain = wind_term(heading, freq_index, NFREQ, wind_speed.reshape(-1), wind_dir.reshape(-1))
    interaction_wide = interaction.astype(jnp.float32)
    for step_number in range(SOURCE_STEPS):
        spread = jnp.sqrt(lax.optimization_barrier(jnp.mean(spectra_now * spectra_now, axis=0)) + EPSILON)
        rounded = lax.optimization_barrier(spectra_now.astype(jnp.bfloat16)).astype(jnp.float32)
        transfer = jnp.dot(interaction_wide, rounded, precision=lax.Precision.HIGHEST, preferred_element_type=jnp.float32)
        spectra_now = sea_cells[None] * (spectra_now + RATE * (wind_gain * spectra_now + spectra_now * transfer / spread[None])) / (1.0 + RATE * WHITECAP * spread[None])
    final = spectra_now.reshape(comp_total, LAT, LON)
    device = jnp.arange(ENTRIES, dtype=jnp.int32) // NE
    spec_index = device // N_GRID
    grid_index = device % N_GRID
    row_index = spec_index * ROWS_DEV + nest_cell // LON_DEV
    lon_index = grid_index * LON_DEV + nest_cell % LON_DEV
    weights = weight_table[weight_index]
    values = final[:, row_index, lon_index] * weights[None]
    column = (spec_index * N_GRID + nest_owner[:, 0]) * NB_OWN + nest_point
    nest_spectra = jax.ops.segment_sum(values.T, column, num_segments=NBP).T
    return (final, nest_spectra)
```

```python
import functools
import math

import jax
import jax.numpy as jnp
from jax import lax
from jax.experimental import pallas as pl
from jax.experimental.pallas import tpu as pltpu
from jax.sharding import PartitionSpec as P

SOURCE_STEPS = 4
NB_OWN = 128
CAP = 16


TWO_PI = 2.0 * math.pi
RATE = 0.2
WIND_GAIN = 0.8
WHITECAP = 1.0
EPSILON = 1e-06
HIGHEST = lax.Precision.HIGHEST


def headings(offset, number, freq_count, dir_count):
    component = offset + jnp.arange(number, dtype=jnp.int32)
    heading = TWO_PI * ((component // freq_count).astype(jnp.float32) + 0.5) / dir_count
    return (heading, component % freq_count)


def wind_term(heading, freq_index, freq_count, speed_flat, direction_flat):
    alignment = (
        jnp.cos(heading)[:, None] * jnp.cos(direction_flat)[None]
        + jnp.sin(heading)[:, None] * jnp.sin(direction_flat)[None]
    )
    scale_freq = (freq_index + 1).astype(jnp.float32) / freq_count
    return WIND_GAIN * scale_freq[:, None] * speed_flat[None] * jnp.maximum(alignment, 0.0)


def propagate_kernel(block, rx_ref, ry_ref, spec_ref, factor_ref, sea_ref, west_ref, east_ref, out_ref):
    base = pl.program_id(0) * block
    factor = factor_ref[...]
    sea = sea_ref[...]
    rows, lons = factor.shape
    lane = lax.broadcasted_iota(jnp.int32, (rows, lons), 1)
    row = lax.broadcasted_iota(jnp.int32, (rows, lons), 0)

    def one(kk, carry):
        rx = rx_ref[base + kk]
        ry = ry_ref[base + kk]
        s = spec_ref[kk]
        fx = rx * factor * s
        west = jnp.where(lane == 0, west_ref[kk], pltpu.roll(fx, 1, 1))
        east = jnp.where(lane == lons - 1, east_ref[kk], pltpu.roll(fx, lons - 1, 1))
        change = jnp.where(rx > 0, fx - west, east - fx)
        ax = sea * (s - change)
        fy = ry * factor * ax
        south = jnp.where(row == 0, 0.0, pltpu.roll(fy, 1, 0))
        north = jnp.where(row == rows - 1, 0.0, pltpu.roll(fy, rows - 1, 0))
        change_y = jnp.where(ry > 0, fy - south, north - fy)
        out_ref[kk] = (sea * (ax - change_y)).astype(out_ref.dtype)
        return carry

    lax.fori_loop(0, block, one, 0)


def propagate(spectrum, rate_x, rate_y, factor, sea_float, west, east):
    comps, rows, lons = spectrum.shape
    block = 9 if comps % 9 == 0 else 1
    smem = pl.BlockSpec(memory_space=pltpu.SMEM)
    return pl.pallas_call(
        functools.partial(propagate_kernel, block),
        grid=(comps // block,),
        in_specs=[
            smem,
            smem,
            pl.BlockSpec((block, rows, lons), lambda b: (b, 0, 0)),
            pl.BlockSpec((rows, lons), lambda b: (0, 0)),
            pl.BlockSpec((rows, lons), lambda b: (0, 0)),
            pl.BlockSpec((block, rows, 1), lambda b: (b, 0, 0)),
            pl.BlockSpec((block, rows, 1), lambda b: (b, 0, 0)),
        ],
        out_specs=pl.BlockSpec((block, rows, lons), lambda b: (b, 0, 0)),
        out_shape=jax.ShapeDtypeStruct((comps, rows, lons), jnp.bfloat16),
        compiler_params=pltpu.CompilerParams(dimension_semantics=("arbitrary",)),
        cost_estimate=pl.CostEstimate(
            flops=20 * comps * rows * lons, bytes_accessed=6 * comps * rows * lons, transcendentals=0
        ),
    )(rate_x, rate_y, spectrum, factor, sea_float, west, east)


def local(
    spectrum,
    group_speed,
    depth_factor,
    sea_mask,
    interaction,
    wind_speed,
    wind_dir,
    nest_owner,
    nest_point,
    nest_cell,
    weight_index,
    weight_table,
):
    comp_dev = spectrum.shape[0]
    freq_count = group_speed.shape[0]
    comp_total = interaction.shape[0]
    dir_count = comp_total // freq_count
    spec_count = lax.axis_size("spec")
    grid_count = lax.axis_size("grid")
    heading, freq_index = headings(
        lax.axis_index("spec") * comp_dev, comp_dev, freq_count, dir_count
    )
    group_rate = jnp.take(group_speed, freq_index)
    rate_x = group_rate * jnp.cos(heading)
    rate_y = group_rate * jnp.sin(heading)
    sea_float = sea_mask.astype(jnp.float32)
    factor = depth_factor * sea_float
    lon_count = spectrum.shape[2]
    last_flux = rate_x[:, None, None] * factor[None, :, lon_count - 1 :] * spectrum[:, :, lon_count - 1 :]
    first_flux = rate_x[:, None, None] * factor[None, :, :1] * spectrum[:, :, :1]
    up = [(i, (i + 1) % grid_count) for i in range(grid_count)]
    down = [(j, i) for i, j in up]
    west = lax.ppermute(last_flux, "grid", up)
    east = lax.ppermute(first_flux, "grid", down)
    propagated = propagate(spectrum, rate_x, rate_y, factor, sea_float, west, east)

    row_count = spectrum.shape[1] // spec_count
    received = lax.all_to_all(propagated, "spec", split_axis=1, concat_axis=0, tiled=True)
    cell_count = row_count * lon_count
    spectra_now = received.astype(jnp.float32).reshape(comp_total, cell_count)
    sea_rows = lax.dynamic_slice_in_dim(sea_float, lax.axis_index("spec") * row_count, row_count, 0)
    sea_cells = sea_rows.reshape(-1)
    all_heading, all_freq = headings(0, comp_total, freq_count, dir_count)
    wind_gain = wind_term(
        all_heading, all_freq, freq_count, wind_speed.reshape(-1), wind_dir.reshape(-1)
    )
    for step_number in range(SOURCE_STEPS):
        spread = jnp.sqrt(jnp.mean(spectra_now * spectra_now, axis=0) + EPSILON)
        rounded = spectra_now.astype(jnp.bfloat16)
        transfer = jnp.dot(interaction, rounded, preferred_element_type=jnp.float32)
        spectra_now = (
            sea_cells[None]
            * (
                spectra_now
                + RATE * (wind_gain * spectra_now + spectra_now * transfer / spread[None])
            )
            / (1.0 + RATE * WHITECAP * spread[None])
        )

    slots = grid_count * CAP
    owners = nest_owner[:, 0]
    member = (owners[:, None] == jnp.arange(grid_count, dtype=jnp.int32)[None]).astype(jnp.int32)
    slot_rank = jnp.sum((jnp.cumsum(member, axis=0) - member) * member, axis=1)
    column = owners * CAP + slot_rank
    weights = jnp.take(weight_table, weight_index)
    pick_slot = (column[:, None] == jnp.arange(slots, dtype=jnp.int32)[None]).astype(jnp.float32)
    pick_cell = (nest_cell[:, None] == jnp.arange(cell_count, dtype=jnp.int32)[None]).astype(jnp.float32)
    slot_cell = jnp.dot(pick_slot.T, pick_cell, precision=HIGHEST, preferred_element_type=jnp.float32)
    slot_weight = jnp.dot(pick_slot.T, weights, precision=HIGHEST, preferred_element_type=jnp.float32)
    slot_label = jnp.dot(
        pick_slot.T, nest_point.astype(jnp.float32) + 1.0, precision=HIGHEST,
        preferred_element_type=jnp.float32,
    ) - 1.0
    gathered = lax.dot_general(
        slot_cell, spectra_now, (((1,), (1,)), ((), ())), precision=HIGHEST,
        preferred_element_type=jnp.float32,
    )
    send = jnp.concatenate([gathered * slot_weight[:, None], slot_label[:, None]], axis=1)
    send = send.reshape(grid_count, CAP, comp_total + 1)
    arrived = lax.all_to_all(send, "grid", split_axis=0, concat_axis=0, tiled=True)
    arrived = arrived.reshape(slots, comp_total + 1)
    select = (arrived[:, comp_total][:, None] == jnp.arange(NB_OWN, dtype=jnp.float32)[None]).astype(
        jnp.float32
    )
    nest_spectra = lax.dot_general(
        arrived[:, :comp_total], select, (((0,), (0,)), ((), ())), precision=HIGHEST,
        preferred_element_type=jnp.float32,
    )
    return (spectra_now.reshape(comp_total, row_count, lon_count), nest_spectra)


def solution(mesh):
    in_specs = (
        P("spec", None, "grid"),
        P(),
        P(None, "grid"),
        P(None, "grid"),
        P(),
        P("spec", "grid"),
        P("spec", "grid"),
        P(("spec", "grid"), None),
        P(("spec", "grid")),
        P(("spec", "grid")),
        P(("spec", "grid")),
        P(),
    )
    out_specs = (P(None, "spec", "grid"), P(None, ("spec", "grid")))
    return jax.shard_map(local, mesh=mesh, in_specs=in_specs, out_specs=out_specs, check_vma=False)
```

```python
import functools
import math

import jax
import jax.numpy as jnp
from jax import lax
from jax.experimental import pallas as pl
from jax.experimental.pallas import tpu as pltpu
from jax.sharding import PartitionSpec as P

SOURCE_STEPS = 4
NB_OWN = 128
CAP = 16


TWO_PI = 2.0 * math.pi
RATE = 0.2
WIND_GAIN = 0.8
WHITECAP = 1.0
EPSILON = 1e-06
HIGHEST = lax.Precision.HIGHEST


def headings(offset, number, freq_count, dir_count):
    component = offset + jnp.arange(number, dtype=jnp.int32)
    heading = TWO_PI * ((component // freq_count).astype(jnp.float32) + 0.5) / dir_count
    return (heading, component % freq_count)


def wind_term(heading, freq_index, freq_count, speed_flat, direction_flat):
    alignment = (
        jnp.cos(heading)[:, None] * jnp.cos(direction_flat)[None]
        + jnp.sin(heading)[:, None] * jnp.sin(direction_flat)[None]
    )
    scale_freq = (freq_index + 1).astype(jnp.float32) / freq_count
    return WIND_GAIN * scale_freq[:, None] * speed_flat[None] * jnp.maximum(alignment, 0.0)


def propagate_kernel(
    rx_ref, ry_ref, spec_ref, factor_ref, sea_ref, out_ref,
    send_first, send_last, recv_west, recv_east, send_sem, recv_sem,
):
    comps, rows, lons = spec_ref.shape
    grid_count = lax.axis_size("grid")
    me = lax.axis_index("grid")
    spec = lax.axis_index("spec")
    right = lax.rem(me + 1, grid_count)
    left = lax.rem(me + grid_count - 1, grid_count)
    barrier = pltpu.get_barrier_semaphore()
    for neighbour in (left, right):
        pl.semaphore_signal(barrier, inc=1, device_id=(spec, neighbour), device_id_type=pl.DeviceIdType.MESH)
    pl.semaphore_wait(barrier, 2)

    factor = factor_ref[...]
    sea = sea_ref[...]
    edge_lane = lax.broadcasted_iota(jnp.int32, (rows, 128), 1)
    factor_first = factor[:, 0:1]
    factor_last = factor[:, lons - 1 : lons]

    def edges(kk, carry):
        first, last = carry
        rx = rx_ref[kk]
        s_first = spec_ref[kk, :, 0:128][:, 0:1]
        s_last = spec_ref[kk, :, lons - 128 : lons][:, 127:128]
        first = jnp.where(edge_lane == kk, rx * factor_first * s_first, first)
        last = jnp.where(edge_lane == kk, rx * factor_last * s_last, last)
        return first, last

    zero = jnp.zeros((rows, 128), jnp.float32)
    first, last = lax.fori_loop(0, comps, edges, (zero, zero))
    send_first[...] = first
    send_last[...] = last
    to_right = pltpu.make_async_remote_copy(
        src_ref=send_last, dst_ref=recv_west, send_sem=send_sem.at[0], recv_sem=recv_sem.at[0],
        device_id=(spec, right), device_id_type=pl.DeviceIdType.MESH,
    )
    to_left = pltpu.make_async_remote_copy(
        src_ref=send_first, dst_ref=recv_east, send_sem=send_sem.at[1], recv_sem=recv_sem.at[1],
        device_id=(spec, left), device_id_type=pl.DeviceIdType.MESH,
    )
    to_right.start()
    to_left.start()
    to_right.wait()
    to_left.wait()

    lane = lax.broadcasted_iota(jnp.int32, (rows, lons), 1)
    row = lax.broadcasted_iota(jnp.int32, (rows, lons), 0)

    def one(kk, carry):
        rx = rx_ref[kk]
        ry = ry_ref[kk]
        s = spec_ref[kk]
        west_col = jnp.sum(jnp.where(edge_lane == kk, recv_west[...], 0.0), axis=1, keepdims=True)
        east_col = jnp.sum(jnp.where(edge_lane == kk, recv_east[...], 0.0), axis=1, keepdims=True)
        fx = rx * factor * s
        west = jnp.where(lane == 0, west_col, pltpu.roll(fx, 1, 1))
        east = jnp.where(lane == lons - 1, east_col, pltpu.roll(fx, lons - 1, 1))
        change = jnp.where(rx > 0, fx - west, east - fx)
        ax = sea * (s - change)
        fy = ry * factor * ax
        south = jnp.where(row == 0, 0.0, pltpu.roll(fy, 1, 0))
        north = jnp.where(row == rows - 1, 0.0, pltpu.roll(fy, rows - 1, 0))
        change_y = jnp.where(ry > 0, fy - south, north - fy)
        out_ref[kk] = (sea * (ax - change_y)).astype(out_ref.dtype)
        return carry

    lax.fori_loop(0, comps, one, 0)


def propagate(spectrum, rate_x, rate_y, factor, sea_float):
    comps, rows, lons = spectrum.shape
    smem = pl.BlockSpec(memory_space=pltpu.SMEM)
    vmem = pl.BlockSpec(memory_space=pltpu.VMEM)
    return pl.pallas_call(
        propagate_kernel,
        in_specs=[smem, smem, vmem, vmem, vmem],
        out_specs=vmem,
        out_shape=jax.ShapeDtypeStruct((comps, rows, lons), jnp.bfloat16),
        scratch_shapes=[
            pltpu.VMEM((rows, 128), jnp.float32),
            pltpu.VMEM((rows, 128), jnp.float32),
            pltpu.VMEM((rows, 128), jnp.float32),
            pltpu.VMEM((rows, 128), jnp.float32),
            pltpu.SemaphoreType.DMA((2,)),
            pltpu.SemaphoreType.DMA((2,)),
        ],
        compiler_params=pltpu.CompilerParams(
            collective_id=0, has_side_effects=True, vmem_limit_bytes=48 * 1024 * 1024
        ),
        cost_estimate=pl.CostEstimate(
            flops=30 * comps * rows * lons, bytes_accessed=6 * comps * rows * lons, transcendentals=0
        ),
    )(rate_x, rate_y, spectrum, factor, sea_float)


def local(
    spectrum,
    group_speed,
    depth_factor,
    sea_mask,
    interaction,
    wind_speed,
    wind_dir,
    nest_owner,
    nest_point,
    nest_cell,
    weight_index,
    weight_table,
):
    comp_dev = spectrum.shape[0]
    freq_count = group_speed.shape[0]
    comp_total = interaction.shape[0]
    dir_count = comp_total // freq_count
    spec_count = lax.axis_size("spec")
    grid_count = lax.axis_size("grid")
    heading, freq_index = headings(
        lax.axis_index("spec") * comp_dev, comp_dev, freq_count, dir_count
    )
    group_rate = jnp.take(group_speed, freq_index)
    rate_x = group_rate * jnp.cos(heading)
    rate_y = group_rate * jnp.sin(heading)
    sea_float = sea_mask.astype(jnp.float32)
    factor = depth_factor * sea_float
    lon_count = spectrum.shape[2]
    propagated = propagate(spectrum, rate_x, rate_y, factor, sea_float)

    row_count = spectrum.shape[1] // spec_count
    received = lax.all_to_all(propagated, "spec", split_axis=1, concat_axis=0, tiled=True)
    cell_count = row_count * lon_count
    spectra_now = received.astype(jnp.float32).reshape(comp_total, cell_count)
    sea_rows = lax.dynamic_slice_in_dim(sea_float, lax.axis_index("spec") * row_count, row_count, 0)
    sea_cells = sea_rows.reshape(-1)
    all_heading, all_freq = headings(0, comp_total, freq_count, dir_count)
    wind_gain = wind_term(
        all_heading, all_freq, freq_count, wind_speed.reshape(-1), wind_dir.reshape(-1)
    )
    for step_number in range(SOURCE_STEPS):
        spread = jnp.sqrt(jnp.mean(spectra_now * spectra_now, axis=0) + EPSILON)
        rounded = spectra_now.astype(jnp.bfloat16)
        transfer = jnp.dot(interaction, rounded, preferred_element_type=jnp.float32)
        spectra_now = (
            sea_cells[None]
            * (
                spectra_now
                + RATE * (wind_gain * spectra_now + spectra_now * transfer / spread[None])
            )
            / (1.0 + RATE * WHITECAP * spread[None])
        )

    slots = grid_count * CAP
    owners = nest_owner[:, 0]
    member = (owners[:, None] == jnp.arange(grid_count, dtype=jnp.int32)[None]).astype(jnp.int32)
    slot_rank = jnp.sum((jnp.cumsum(member, axis=0) - member) * member, axis=1)
    column = owners * CAP + slot_rank
    weights = jnp.take(weight_table, weight_index)
    pick_slot = (column[:, None] == jnp.arange(slots, dtype=jnp.int32)[None]).astype(jnp.float32)
    pick_cell = (nest_cell[:, None] == jnp.arange(cell_count, dtype=jnp.int32)[None]).astype(jnp.float32)
    slot_cell = jnp.dot(pick_slot.T, pick_cell, precision=HIGHEST, preferred_element_type=jnp.float32)
    slot_weight = jnp.dot(pick_slot.T, weights, precision=HIGHEST, preferred_element_type=jnp.float32)
    slot_label = jnp.dot(
        pick_slot.T, nest_point.astype(jnp.float32) + 1.0, precision=HIGHEST,
        preferred_element_type=jnp.float32,
    ) - 1.0
    gathered = lax.dot_general(
        slot_cell, spectra_now, (((1,), (1,)), ((), ())), precision=HIGHEST,
        preferred_element_type=jnp.float32,
    )
    send = jnp.concatenate([gathered * slot_weight[:, None], slot_label[:, None]], axis=1)
    send = send.astype(jnp.bfloat16).reshape(grid_count, CAP, comp_total + 1)
    arrived = lax.all_to_all(send, "grid", split_axis=0, concat_axis=0, tiled=True)
    arrived = arrived.reshape(slots, comp_total + 1)
    select = (arrived[:, comp_total][:, None] == jnp.arange(NB_OWN, dtype=jnp.bfloat16)[None]).astype(
        jnp.bfloat16
    )
    nest_spectra = lax.dot_general(
        arrived[:, :comp_total], select, (((0,), (0,)), ((), ())),
        preferred_element_type=jnp.float32,
    )
    return (spectra_now.reshape(comp_total, row_count, lon_count), nest_spectra)


def solution(mesh):
    in_specs = (
        P("spec", None, "grid"),
        P(),
        P(None, "grid"),
        P(None, "grid"),
        P(),
        P("spec", "grid"),
        P("spec", "grid"),
        P(("spec", "grid"), None),
        P(("spec", "grid")),
        P(("spec", "grid")),
        P(("spec", "grid")),
        P(),
    )
    out_specs = (P(None, "spec", "grid"), P(None, ("spec", "grid")))
    return jax.shard_map(local, mesh=mesh, in_specs=in_specs, out_specs=out_specs, check_vma=False)
```

```python
import functools
import math

import jax
import jax.numpy as jnp
from jax import lax
from jax.experimental import pallas as pl
from jax.experimental.pallas import tpu as pltpu
from jax.sharding import PartitionSpec as P

SOURCE_STEPS = 4
NB_OWN = 128
CAP = 16


TWO_PI = 2.0 * math.pi
RATE = 0.2
WIND_GAIN = 0.8
WHITECAP = 1.0
EPSILON = 1e-06
HIGHEST = lax.Precision.HIGHEST


def headings(offset, number, freq_count, dir_count):
    component = offset + jnp.arange(number, dtype=jnp.int32)
    heading = TWO_PI * ((component // freq_count).astype(jnp.float32) + 0.5) / dir_count
    return (heading, component % freq_count)


def wind_term(heading, freq_index, freq_count, speed_flat, direction_flat):
    alignment = (
        jnp.cos(heading)[:, None] * jnp.cos(direction_flat)[None]
        + jnp.sin(heading)[:, None] * jnp.sin(direction_flat)[None]
    )
    scale_freq = (freq_index + 1).astype(jnp.float32) / freq_count
    return WIND_GAIN * scale_freq[:, None] * speed_flat[None] * jnp.maximum(alignment, 0.0)


def propagate_kernel(
    rx_ref, ry_ref, spec_ref, factor_ref, sea_ref, out_ref,
    send_first, send_last, recv_west, recv_east, send_sem, recv_sem, result_lo, result_hi,
):
    comps, rows, lons = spec_ref.shape
    grid_count = lax.axis_size("grid")
    me = lax.axis_index("grid")
    spec = lax.axis_index("spec")
    right = lax.rem(me + 1, grid_count)
    left = lax.rem(me + grid_count - 1, grid_count)
    barrier = pltpu.get_barrier_semaphore()
    for neighbour in (left, right):
        pl.semaphore_signal(barrier, inc=1, device_id=(spec, neighbour), device_id_type=pl.DeviceIdType.MESH)
    pl.semaphore_wait(barrier, 2)

    factor = factor_ref[...]
    sea = sea_ref[...]
    edge_lane = lax.broadcasted_iota(jnp.int32, (rows, 128), 1)
    factor_first = factor[:, 0:1]
    factor_last = factor[:, lons - 1 : lons]

    def edges(kk, carry):
        first, last = carry
        rx = rx_ref[kk]
        s_first = spec_ref[kk, :, 0:128][:, 0:1]
        s_last = spec_ref[kk, :, lons - 128 : lons][:, 127:128]
        first = jnp.where(edge_lane == kk, rx * factor_first * s_first, first)
        last = jnp.where(edge_lane == kk, rx * factor_last * s_last, last)
        return first, last

    zero = jnp.zeros((rows, 128), jnp.float32)
    first, last = lax.fori_loop(0, comps, edges, (zero, zero), unroll=3)
    send_first[...] = first
    send_last[...] = last
    to_right = pltpu.make_async_remote_copy(
        src_ref=send_last, dst_ref=recv_west, send_sem=send_sem.at[0], recv_sem=recv_sem.at[0],
        device_id=(spec, right), device_id_type=pl.DeviceIdType.MESH,
    )
    to_left = pltpu.make_async_remote_copy(
        src_ref=send_first, dst_ref=recv_east, send_sem=send_sem.at[1], recv_sem=recv_sem.at[1],
        device_id=(spec, left), device_id_type=pl.DeviceIdType.MESH,
    )
    to_right.start()
    to_left.start()
    to_right.wait()
    to_left.wait()

    lane = lax.broadcasted_iota(jnp.int32, (rows, lons), 1)
    row = lax.broadcasted_iota(jnp.int32, (rows, lons), 0)

    def one(kk, carry):
        rx = rx_ref[kk]
        ry = ry_ref[kk]
        s = spec_ref[kk]
        west_col = jnp.sum(jnp.where(edge_lane == kk, recv_west[...], 0.0), axis=1, keepdims=True)
        east_col = jnp.sum(jnp.where(edge_lane == kk, recv_east[...], 0.0), axis=1, keepdims=True)
        fx = rx * factor * s
        west = jnp.where(lane == 0, west_col, pltpu.roll(fx, 1, 1))
        east = jnp.where(lane == lons - 1, east_col, pltpu.roll(fx, lons - 1, 1))
        change = jnp.where(rx > 0, fx - west, east - fx)
        ax = sea * (s - change)
        fy = ry * factor * ax
        south = jnp.where(row == 0, 0.0, pltpu.roll(fy, 1, 0))
        north = jnp.where(row == rows - 1, 0.0, pltpu.roll(fy, rows - 1, 0))
        change_y = jnp.where(ry > 0, fy - south, north - fy)
        res = sea * (ax - change_y)
        place = pl.ds(pl.multiple_of(kk * rows, rows), rows)
        result_lo[place, :] = res[:, :128]
        result_hi[place, :] = res[:, 128:]
        return carry

    lax.fori_loop(0, comps, one, 0, unroll=3)

    chunks = out_ref.shape[0]

    def regroup(i, carry):
        out_ref[i % chunks, i // chunks, :, 0:128] = result_lo[pl.ds(i, comps, stride=rows), :].astype(out_ref.dtype)
        out_ref[i % chunks, i // chunks, :, 128:256] = result_hi[pl.ds(i, comps, stride=rows), :].astype(out_ref.dtype)
        return carry

    lax.fori_loop(0, rows, regroup, 0, unroll=4)


def propagate(spectrum, rate_x, rate_y, factor, sea_float, chunks):
    comps, rows, lons = spectrum.shape
    smem = pl.BlockSpec(memory_space=pltpu.SMEM)
    vmem = pl.BlockSpec(memory_space=pltpu.VMEM)
    return pl.pallas_call(
        propagate_kernel,
        in_specs=[smem, smem, vmem, vmem, vmem],
        out_specs=vmem,
        out_shape=jax.ShapeDtypeStruct((chunks, rows // chunks, comps, lons), jnp.bfloat16),
        scratch_shapes=[
            pltpu.VMEM((rows, 128), jnp.float32),
            pltpu.VMEM((rows, 128), jnp.float32),
            pltpu.VMEM((rows, 128), jnp.float32),
            pltpu.VMEM((rows, 128), jnp.float32),
            pltpu.SemaphoreType.DMA((2,)),
            pltpu.SemaphoreType.DMA((2,)),
            pltpu.VMEM((comps * rows, 128), jnp.float32),
            pltpu.VMEM((comps * rows, 128), jnp.float32),
        ],
        compiler_params=pltpu.CompilerParams(
            collective_id=0, has_side_effects=True, vmem_limit_bytes=48 * 1024 * 1024
        ),
        cost_estimate=pl.CostEstimate(
            flops=30 * comps * rows * lons, bytes_accessed=6 * comps * rows * lons, transcendentals=0
        ),
    )(rate_x, rate_y, spectrum, factor, sea_float)


def local(
    spectrum,
    group_speed,
    depth_factor,
    sea_mask,
    interaction,
    wind_speed,
    wind_dir,
    nest_owner,
    nest_point,
    nest_cell,
    weight_index,
    weight_table,
):
    comp_dev = spectrum.shape[0]
    freq_count = group_speed.shape[0]
    comp_total = interaction.shape[0]
    dir_count = comp_total // freq_count
    spec_count = lax.axis_size("spec")
    grid_count = lax.axis_size("grid")
    heading, freq_index = headings(
        lax.axis_index("spec") * comp_dev, comp_dev, freq_count, dir_count
    )
    group_rate = jnp.take(group_speed, freq_index)
    rate_x = group_rate * jnp.cos(heading)
    rate_y = group_rate * jnp.sin(heading)
    sea_float = sea_mask.astype(jnp.float32)
    factor = depth_factor * sea_float
    lon_count = spectrum.shape[2]
    row_count = spectrum.shape[1] // spec_count
    propagated = propagate(spectrum, rate_x, rate_y, factor, sea_float, row_count)
    sea_rows = lax.dynamic_slice_in_dim(sea_float, lax.axis_index("spec") * row_count, row_count, 0)
    all_heading, all_freq = headings(0, comp_total, freq_count, dir_count)
    cell_count = row_count * lon_count
    finals = []
    for r in range(row_count):
        received = lax.all_to_all(propagated[r], "spec", split_axis=0, concat_axis=0, tiled=True)
        state = received.astype(jnp.float32).reshape(comp_total, lon_count)
        sea_cells = sea_rows[r]
        wind_gain = wind_term(all_heading, all_freq, freq_count, wind_speed[r], wind_dir[r])
        for step_number in range(SOURCE_STEPS):
            spread = jnp.sqrt(jnp.mean(state * state, axis=0) + EPSILON)
            rounded = state.astype(jnp.bfloat16)
            transfer = jnp.dot(interaction, rounded, preferred_element_type=jnp.float32)
            state = (
                sea_cells[None]
                * (state + RATE * (wind_gain * state + state * transfer / spread[None]))
                / (1.0 + RATE * WHITECAP * spread[None])
            )
        finals.append(state)
    spectra_now = jnp.stack(finals, axis=1)

    slots = grid_count * CAP
    owners = nest_owner[:, 0]
    member = (owners[:, None] == jnp.arange(grid_count, dtype=jnp.int32)[None]).astype(jnp.int32)
    slot_rank = jnp.sum((jnp.cumsum(member, axis=0) - member) * member, axis=1)
    column = owners * CAP + slot_rank
    weights = jnp.take(weight_table, weight_index)
    pick_slot = (column[:, None] == jnp.arange(slots, dtype=jnp.int32)[None]).astype(jnp.float32)
    pick_cell = (nest_cell[:, None] == jnp.arange(cell_count, dtype=jnp.int32)[None]).astype(jnp.float32)
    slot_cell = jnp.dot(pick_slot.T, pick_cell, precision=HIGHEST, preferred_element_type=jnp.float32)
    slot_weight = jnp.dot(pick_slot.T, weights, precision=HIGHEST, preferred_element_type=jnp.float32)
    slot_label = jnp.dot(
        pick_slot.T, nest_point.astype(jnp.float32) + 1.0, precision=HIGHEST,
        preferred_element_type=jnp.float32,
    ) - 1.0
    gathered = sum(
        lax.dot_general(
            slot_cell[:, r * lon_count : (r + 1) * lon_count], finals[r], (((1,), (1,)), ((), ())),
            precision=HIGHEST, preferred_element_type=jnp.float32,
        )
        for r in range(row_count)
    )
    send = jnp.concatenate([gathered * slot_weight[:, None], slot_label[:, None]], axis=1)
    send = send.astype(jnp.bfloat16).reshape(grid_count, CAP, comp_total + 1)
    arrived = lax.all_to_all(send, "grid", split_axis=0, concat_axis=0, tiled=True)
    arrived = arrived.reshape(slots, comp_total + 1)
    select = (arrived[:, comp_total][:, None] == jnp.arange(NB_OWN, dtype=jnp.bfloat16)[None]).astype(
        jnp.bfloat16
    )
    nest_spectra = lax.dot_general(
        arrived[:, :comp_total], select, (((0,), (0,)), ((), ())),
        preferred_element_type=jnp.float32,
    )
    return (spectra_now, nest_spectra)


def solution(mesh):
    in_specs = (
        P("spec", None, "grid"),
        P(),
        P(None, "grid"),
        P(None, "grid"),
        P(),
        P("spec", "grid"),
        P("spec", "grid"),
        P(("spec", "grid"), None),
        P(("spec", "grid")),
        P(("spec", "grid")),
        P(("spec", "grid")),
        P(),
    )
    out_specs = (P(None, "spec", "grid"), P(None, ("spec", "grid")))
    return jax.shard_map(local, mesh=mesh, in_specs=in_specs, out_specs=out_specs, check_vma=False)
```

```python
import functools
import math

import jax
import jax.numpy as jnp
from jax import lax
from jax.experimental import pallas as pl
from jax.experimental.pallas import tpu as pltpu
from jax.sharding import PartitionSpec as P

SOURCE_STEPS = 4
NB_OWN = 128
CAP = 16


TWO_PI = 2.0 * math.pi
RATE = 0.2
WIND_GAIN = 0.8
WHITECAP = 1.0
EPSILON = 1e-06
HIGHEST = lax.Precision.HIGHEST


def headings(offset, number, freq_count, dir_count):
    component = offset + jnp.arange(number, dtype=jnp.int32)
    heading = TWO_PI * ((component // freq_count).astype(jnp.float32) + 0.5) / dir_count
    return (heading, component % freq_count)


def wind_term(heading, freq_index, freq_count, speed_flat, direction_flat):
    alignment = (
        jnp.cos(heading)[:, None] * jnp.cos(direction_flat)[None]
        + jnp.sin(heading)[:, None] * jnp.sin(direction_flat)[None]
    )
    scale_freq = (freq_index + 1).astype(jnp.float32) / freq_count
    return WIND_GAIN * scale_freq[:, None] * speed_flat[None] * jnp.maximum(alignment, 0.0)


def propagate_kernel(
    rx_ref, ry_ref, spec_ref, factor_ref, sea_ref, out_ref,
    send_first, send_last, recv_west, recv_east, send_sem, recv_sem,
    result_lo, result_hi, send_buf, a2a_send, a2a_recv,
):
    comps, rows, lons = spec_ref.shape
    spec_count = lax.axis_size("spec")
    grid_count = lax.axis_size("grid")
    chunk = rows // spec_count
    me = lax.axis_index("grid")
    spec = lax.axis_index("spec")
    right = lax.rem(me + 1, grid_count)
    left = lax.rem(me + grid_count - 1, grid_count)
    barrier = pltpu.get_barrier_semaphore()
    for neighbour in (left, right):
        pl.semaphore_signal(barrier, inc=1, device_id=(spec, neighbour), device_id_type=pl.DeviceIdType.MESH)

    def greet(d, carry):
        @pl.when(d != spec)
        def _():
            pl.semaphore_signal(barrier, inc=1, device_id=(d, me), device_id_type=pl.DeviceIdType.MESH)
        return carry

    lax.fori_loop(0, spec_count, greet, 0)
    pl.semaphore_wait(barrier, 2 + spec_count - 1)

    factor = factor_ref[...]
    sea = sea_ref[...]
    edge_lane = lax.broadcasted_iota(jnp.int32, (rows, 128), 1)
    factor_first = factor[:, 0:1]
    factor_last = factor[:, lons - 1 : lons]

    def edges(kk, carry):
        first, last = carry
        rx = rx_ref[kk]
        s_first = spec_ref[kk, :, 0:128][:, 0:1]
        s_last = spec_ref[kk, :, lons - 128 : lons][:, 127:128]
        first = jnp.where(edge_lane == kk, rx * factor_first * s_first, first)
        last = jnp.where(edge_lane == kk, rx * factor_last * s_last, last)
        return first, last

    zero = jnp.zeros((rows, 128), jnp.float32)
    first, last = lax.fori_loop(0, comps, edges, (zero, zero), unroll=3)
    send_first[...] = first
    send_last[...] = last
    to_right = pltpu.make_async_remote_copy(
        src_ref=send_last, dst_ref=recv_west, send_sem=send_sem.at[0], recv_sem=recv_sem.at[0],
        device_id=(spec, right), device_id_type=pl.DeviceIdType.MESH,
    )
    to_left = pltpu.make_async_remote_copy(
        src_ref=send_first, dst_ref=recv_east, send_sem=send_sem.at[1], recv_sem=recv_sem.at[1],
        device_id=(spec, left), device_id_type=pl.DeviceIdType.MESH,
    )
    to_right.start()
    to_left.start()
    to_right.wait()
    to_left.wait()

    lane = lax.broadcasted_iota(jnp.int32, (rows, lons), 1)
    row = lax.broadcasted_iota(jnp.int32, (rows, lons), 0)

    def one(kk, carry):
        rx = rx_ref[kk]
        ry = ry_ref[kk]
        s = spec_ref[kk]
        west_col = jnp.sum(jnp.where(edge_lane == kk, recv_west[...], 0.0), axis=1, keepdims=True)
        east_col = jnp.sum(jnp.where(edge_lane == kk, recv_east[...], 0.0), axis=1, keepdims=True)
        fx = rx * factor * s
        west = jnp.where(lane == 0, west_col, pltpu.roll(fx, 1, 1))
        east = jnp.where(lane == lons - 1, east_col, pltpu.roll(fx, lons - 1, 1))
        change = jnp.where(rx > 0, fx - west, east - fx)
        ax = sea * (s - change)
        fy = ry * factor * ax
        south = jnp.where(row == 0, 0.0, pltpu.roll(fy, 1, 0))
        north = jnp.where(row == rows - 1, 0.0, pltpu.roll(fy, rows - 1, 0))
        change_y = jnp.where(ry > 0, fy - south, north - fy)
        res = sea * (ax - change_y)
        place = pl.ds(pl.multiple_of(kk * rows, rows), rows)
        result_lo[place, :] = res[:, :128]
        result_hi[place, :] = res[:, 128:]
        return carry

    lax.fori_loop(0, comps, one, 0, unroll=3)

    def copy_to(d, slot):
        return pltpu.make_async_remote_copy(
            src_ref=send_buf.at[d], dst_ref=out_ref.at[slot], send_sem=a2a_send.at[d],
            recv_sem=a2a_recv.at[slot], device_id=(d, me), device_id_type=pl.DeviceIdType.MESH,
        )

    def regroup(d, carry):
        for r in range(chunk):
            i = d * chunk + r
            for half, part in ((0, result_lo), (1, result_hi)):
                at = r * lons + half * 128
                send_buf[d, :, at : at + 128] = part[pl.ds(i, comps, stride=rows), :].astype(send_buf.dtype)

        @pl.when(d != spec)
        def _():
            copy_to(d, spec).start()

        @pl.when(d == spec)
        def _():
            out_ref[d] = send_buf[d]

        return carry

    lax.fori_loop(0, spec_count, regroup, 0)

    def finish(d, carry):
        @pl.when(d != spec)
        def _():
            copy_to(d, d).wait_send()
            copy_to(d, d).wait_recv()

        return carry

    lax.fori_loop(0, spec_count, finish, 0)


def propagate(spectrum, rate_x, rate_y, factor, sea_float, spec_count):
    comps, rows, lons = spectrum.shape
    chunk = rows // spec_count
    smem = pl.BlockSpec(memory_space=pltpu.SMEM)
    vmem = pl.BlockSpec(memory_space=pltpu.VMEM)
    return pl.pallas_call(
        propagate_kernel,
        in_specs=[smem, smem, vmem, vmem, vmem],
        out_specs=vmem,
        out_shape=jax.ShapeDtypeStruct((spec_count, comps, chunk * lons), jnp.bfloat16),
        scratch_shapes=[
            pltpu.VMEM((rows, 128), jnp.float32),
            pltpu.VMEM((rows, 128), jnp.float32),
            pltpu.VMEM((rows, 128), jnp.float32),
            pltpu.VMEM((rows, 128), jnp.float32),
            pltpu.SemaphoreType.DMA((2,)),
            pltpu.SemaphoreType.DMA((2,)),
            pltpu.VMEM((comps * rows, 128), jnp.float32),
            pltpu.VMEM((comps * rows, 128), jnp.float32),
            pltpu.VMEM((spec_count, comps, chunk * lons), jnp.bfloat16),
            pltpu.SemaphoreType.DMA((spec_count,)),
            pltpu.SemaphoreType.DMA((spec_count,)),
        ],
        compiler_params=pltpu.CompilerParams(
            collective_id=0, has_side_effects=True, vmem_limit_bytes=56 * 1024 * 1024
        ),
        cost_estimate=pl.CostEstimate(
            flops=30 * comps * rows * lons, bytes_accessed=6 * comps * rows * lons, transcendentals=0
        ),
    )(rate_x, rate_y, spectrum, factor, sea_float)


def local(
    spectrum,
    group_speed,
    depth_factor,
    sea_mask,
    interaction,
    wind_speed,
    wind_dir,
    nest_owner,
    nest_point,
    nest_cell,
    weight_index,
    weight_table,
):
    comp_dev = spectrum.shape[0]
    freq_count = group_speed.shape[0]
    comp_total = interaction.shape[0]
    dir_count = comp_total // freq_count
    spec_count = lax.axis_size("spec")
    grid_count = lax.axis_size("grid")
    heading, freq_index = headings(
        lax.axis_index("spec") * comp_dev, comp_dev, freq_count, dir_count
    )
    group_rate = jnp.take(group_speed, freq_index)
    rate_x = group_rate * jnp.cos(heading)
    rate_y = group_rate * jnp.sin(heading)
    sea_float = sea_mask.astype(jnp.float32)
    factor = depth_factor * sea_float
    lon_count = spectrum.shape[2]
    received = propagate(spectrum, rate_x, rate_y, factor, sea_float, spec_count)
    row_count = spectrum.shape[1] // spec_count
    cell_count = row_count * lon_count
    spectra_now = received.astype(jnp.float32).reshape(comp_total, cell_count)
    sea_rows = lax.dynamic_slice_in_dim(sea_float, lax.axis_index("spec") * row_count, row_count, 0)
    sea_cells = sea_rows.reshape(-1)
    all_heading, all_freq = headings(0, comp_total, freq_count, dir_count)
    wind_gain = wind_term(
        all_heading, all_freq, freq_count, wind_speed.reshape(-1), wind_dir.reshape(-1)
    )
    for step_number in range(SOURCE_STEPS):
        spread = jnp.sqrt(jnp.mean(spectra_now * spectra_now, axis=0) + EPSILON)
        rounded = spectra_now.astype(jnp.bfloat16)
        transfer = jnp.dot(interaction, rounded, preferred_element_type=jnp.float32)
        spectra_now = (
            sea_cells[None]
            * (
                spectra_now
                + RATE * (wind_gain * spectra_now + spectra_now * transfer / spread[None])
            )
            / (1.0 + RATE * WHITECAP * spread[None])
        )

    slots = grid_count * CAP
    owners = nest_owner[:, 0]
    member = (owners[:, None] == jnp.arange(grid_count, dtype=jnp.int32)[None]).astype(jnp.int32)
    slot_rank = jnp.sum((jnp.cumsum(member, axis=0) - member) * member, axis=1)
    column = owners * CAP + slot_rank
    weights = jnp.take(weight_table, weight_index)
    pick_slot = (column[:, None] == jnp.arange(slots, dtype=jnp.int32)[None]).astype(jnp.float32)
    pick_cell = (nest_cell[:, None] == jnp.arange(cell_count, dtype=jnp.int32)[None]).astype(jnp.float32)
    slot_cell = jnp.dot(pick_slot.T, pick_cell, precision=HIGHEST, preferred_element_type=jnp.float32)
    slot_weight = jnp.dot(pick_slot.T, weights, precision=HIGHEST, preferred_element_type=jnp.float32)
    slot_label = jnp.dot(
        pick_slot.T, nest_point.astype(jnp.float32) + 1.0, precision=HIGHEST,
        preferred_element_type=jnp.float32,
    ) - 1.0
    gathered = lax.dot_general(
        slot_cell, spectra_now, (((1,), (1,)), ((), ())), precision=HIGHEST,
        preferred_element_type=jnp.float32,
    )
    send = jnp.concatenate([gathered * slot_weight[:, None], slot_label[:, None]], axis=1)
    send = send.astype(jnp.bfloat16).reshape(grid_count, CAP, comp_total + 1)
    arrived = lax.all_to_all(send, "grid", split_axis=0, concat_axis=0, tiled=True)
    arrived = arrived.reshape(slots, comp_total + 1)
    select = (arrived[:, comp_total][:, None] == jnp.arange(NB_OWN, dtype=jnp.bfloat16)[None]).astype(
        jnp.bfloat16
    )
    nest_spectra = lax.dot_general(
        arrived[:, :comp_total], select, (((0,), (0,)), ((), ())),
        preferred_element_type=jnp.float32,
    )
    return (spectra_now.reshape(comp_total, row_count, lon_count), nest_spectra)


def solution(mesh):
    in_specs = (
        P("spec", None, "grid"),
        P(),
        P(None, "grid"),
        P(None, "grid"),
        P(),
        P("spec", "grid"),
        P("spec", "grid"),
        P(("spec", "grid"), None),
        P(("spec", "grid")),
        P(("spec", "grid")),
        P(("spec", "grid")),
        P(),
    )
    out_specs = (P(None, "spec", "grid"), P(None, ("spec", "grid")))
    return jax.shard_map(local, mesh=mesh, in_specs=in_specs, out_specs=out_specs, check_vma=False)
```

```python
import functools
import math

import jax
import jax.numpy as jnp
from jax import lax
from jax.experimental import pallas as pl
from jax.experimental.pallas import tpu as pltpu
from jax.sharding import PartitionSpec as P

SOURCE_STEPS = 4
NB_OWN = 128
CAP = 16


TWO_PI = 2.0 * math.pi
RATE = 0.2
WIND_GAIN = 0.8
WHITECAP = 1.0
EPSILON = 1e-06
HIGHEST = lax.Precision.HIGHEST


def headings(offset, number, freq_count, dir_count):
    component = offset + jnp.arange(number, dtype=jnp.int32)
    heading = TWO_PI * ((component // freq_count).astype(jnp.float32) + 0.5) / dir_count
    return (heading, component % freq_count)


def wind_term(heading, freq_index, freq_count, speed_flat, direction_flat):
    alignment = (
        jnp.cos(heading)[:, None] * jnp.cos(direction_flat)[None]
        + jnp.sin(heading)[:, None] * jnp.sin(direction_flat)[None]
    )
    scale_freq = (freq_index + 1).astype(jnp.float32) / freq_count
    return WIND_GAIN * scale_freq[:, None] * speed_flat[None] * jnp.maximum(alignment, 0.0)


def propagate_kernel(
    rx_ref, ry_ref, spec_ref, factor_ref, sea_ref, out_ref,
    send_first, send_last, recv_west, recv_east, send_sem, recv_sem,
    result_lo, result_hi, send_buf, a2a_send, a2a_recv,
):
    comps, rows, lons = spec_ref.shape
    spec_count = lax.axis_size("spec")
    grid_count = lax.axis_size("grid")
    chunk = rows // spec_count
    me = lax.axis_index("grid")
    spec = lax.axis_index("spec")
    right = lax.rem(me + 1, grid_count)
    left = lax.rem(me + grid_count - 1, grid_count)
    barrier = pltpu.get_barrier_semaphore()
    for neighbour in (left, right):
        pl.semaphore_signal(barrier, inc=1, device_id=(spec, neighbour), device_id_type=pl.DeviceIdType.MESH)

    def greet(d, carry):
        @pl.when(d != spec)
        def _():
            pl.semaphore_signal(barrier, inc=1, device_id=(d, me), device_id_type=pl.DeviceIdType.MESH)
        return carry

    lax.fori_loop(0, spec_count, greet, 0)
    pl.semaphore_wait(barrier, 2 + spec_count - 1)

    factor = factor_ref[...]
    sea = sea_ref[...]
    edge_lane = lax.broadcasted_iota(jnp.int32, (rows, 128), 1)
    factor_first = factor[:, 0:1]
    factor_last = factor[:, lons - 1 : lons]

    def edges(kk, carry):
        first, last = carry
        rx = rx_ref[kk]
        s_first = spec_ref[kk, :, 0:128][:, 0:1]
        s_last = spec_ref[kk, :, lons - 128 : lons][:, 127:128]
        first = jnp.where(edge_lane == kk, rx * factor_first * s_first, first)
        last = jnp.where(edge_lane == kk, rx * factor_last * s_last, last)
        return first, last

    zero = jnp.zeros((rows, 128), jnp.float32)
    first, last = lax.fori_loop(0, comps, edges, (zero, zero), unroll=3)
    send_first[...] = first
    send_last[...] = last
    to_right = pltpu.make_async_remote_copy(
        src_ref=send_last, dst_ref=recv_west, send_sem=send_sem.at[0], recv_sem=recv_sem.at[0],
        device_id=(spec, right), device_id_type=pl.DeviceIdType.MESH,
    )
    to_left = pltpu.make_async_remote_copy(
        src_ref=send_first, dst_ref=recv_east, send_sem=send_sem.at[1], recv_sem=recv_sem.at[1],
        device_id=(spec, left), device_id_type=pl.DeviceIdType.MESH,
    )
    to_right.start()
    to_left.start()
    to_right.wait()
    to_left.wait()

    lane = lax.broadcasted_iota(jnp.int32, (rows, lons), 1)
    row = lax.broadcasted_iota(jnp.int32, (rows, lons), 0)

    def one(kk, carry):
        rx = rx_ref[kk]
        ry = ry_ref[kk]
        s = spec_ref[kk]
        west_col = jnp.sum(jnp.where(edge_lane == kk, recv_west[...], 0.0), axis=1, keepdims=True)
        east_col = jnp.sum(jnp.where(edge_lane == kk, recv_east[...], 0.0), axis=1, keepdims=True)
        fx = rx * factor * s
        west = jnp.where(lane == 0, west_col, pltpu.roll(fx, 1, 1))
        east = jnp.where(lane == lons - 1, east_col, pltpu.roll(fx, lons - 1, 1))
        change = jnp.where(rx > 0, fx - west, east - fx)
        ax = sea * (s - change)
        fy = ry * factor * ax
        south = jnp.where(row == 0, 0.0, pltpu.roll(fy, 1, 0))
        north = jnp.where(row == rows - 1, 0.0, pltpu.roll(fy, rows - 1, 0))
        change_y = jnp.where(ry > 0, fy - south, north - fy)
        res = sea * (ax - change_y)
        place = pl.ds(pl.multiple_of(kk * rows, rows), rows)
        result_lo[place, :] = res[:, :128]
        result_hi[place, :] = res[:, 128:]
        return carry

    def copy_to(d, slot, start, size):
        return pltpu.make_async_remote_copy(
            src_ref=send_buf.at[d, pl.ds(start, size)], dst_ref=out_ref.at[slot, pl.ds(start, size)],
            send_sem=a2a_send.at[d], recv_sem=a2a_recv.at[slot], device_id=(d, me),
            device_id_type=pl.DeviceIdType.MESH,
        )

    tile = 16
    count = comps // tile
    blocks = [(tile * b, tile) for b in range(count - 1)]
    blocks.append((tile * (count - 1), comps - tile * (count - 1)))
    for start, size in blocks:
        lax.fori_loop(start, start + size, one, 0)

        def regroup(d, carry, start=start, size=size):
            for r in range(chunk):
                i = start * rows + d * chunk + r
                for half, part in ((0, result_lo), (1, result_hi)):
                    at = r * lons + half * 128
                    send_buf[d, pl.ds(start, size), at : at + 128] = part[
                        pl.ds(i, size, stride=rows), :
                    ].astype(send_buf.dtype)

            @pl.when(d != spec)
            def _():
                copy_to(d, spec, start, size).start()

            @pl.when(d == spec)
            def _():
                out_ref[d, pl.ds(start, size), :] = send_buf[d, pl.ds(start, size), :]

            return carry

        lax.fori_loop(0, spec_count, regroup, 0)

    def finish(d, carry):
        @pl.when(d != spec)
        def _():
            copy_to(d, d, 0, comps).wait_send()
            copy_to(d, d, 0, comps).wait_recv()

        return carry

    lax.fori_loop(0, spec_count, finish, 0)


def propagate(spectrum, rate_x, rate_y, factor, sea_float, spec_count):
    comps, rows, lons = spectrum.shape
    chunk = rows // spec_count
    smem = pl.BlockSpec(memory_space=pltpu.SMEM)
    vmem = pl.BlockSpec(memory_space=pltpu.VMEM)
    return pl.pallas_call(
        propagate_kernel,
        in_specs=[smem, smem, vmem, vmem, vmem],
        out_specs=vmem,
        out_shape=jax.ShapeDtypeStruct((spec_count, comps, chunk * lons), jnp.bfloat16),
        scratch_shapes=[
            pltpu.VMEM((rows, 128), jnp.float32),
            pltpu.VMEM((rows, 128), jnp.float32),
            pltpu.VMEM((rows, 128), jnp.float32),
            pltpu.VMEM((rows, 128), jnp.float32),
            pltpu.SemaphoreType.DMA((2,)),
            pltpu.SemaphoreType.DMA((2,)),
            pltpu.VMEM((comps * rows, 128), jnp.float32),
            pltpu.VMEM((comps * rows, 128), jnp.float32),
            pltpu.VMEM((spec_count, comps, chunk * lons), jnp.bfloat16),
            pltpu.SemaphoreType.DMA((spec_count,)),
            pltpu.SemaphoreType.DMA((spec_count,)),
        ],
        compiler_params=pltpu.CompilerParams(
            collective_id=0, has_side_effects=True, vmem_limit_bytes=56 * 1024 * 1024
        ),
        cost_estimate=pl.CostEstimate(
            flops=30 * comps * rows * lons, bytes_accessed=6 * comps * rows * lons, transcendentals=0
        ),
    )(rate_x, rate_y, spectrum, factor, sea_float)


def local(
    spectrum,
    group_speed,
    depth_factor,
    sea_mask,
    interaction,
    wind_speed,
    wind_dir,
    nest_owner,
    nest_point,
    nest_cell,
    weight_index,
    weight_table,
):
    comp_dev = spectrum.shape[0]
    freq_count = group_speed.shape[0]
    comp_total = interaction.shape[0]
    dir_count = comp_total // freq_count
    spec_count = lax.axis_size("spec")
    grid_count = lax.axis_size("grid")
    heading, freq_index = headings(
        lax.axis_index("spec") * comp_dev, comp_dev, freq_count, dir_count
    )
    group_rate = jnp.take(group_speed, freq_index)
    rate_x = group_rate * jnp.cos(heading)
    rate_y = group_rate * jnp.sin(heading)
    sea_float = sea_mask.astype(jnp.float32)
    factor = depth_factor * sea_float
    lon_count = spectrum.shape[2]
    received = propagate(spectrum, rate_x, rate_y, factor, sea_float, spec_count)
    row_count = spectrum.shape[1] // spec_count
    cell_count = row_count * lon_count
    spectra_now = received.astype(jnp.float32).reshape(comp_total, cell_count)
    sea_rows = lax.dynamic_slice_in_dim(sea_float, lax.axis_index("spec") * row_count, row_count, 0)
    sea_cells = sea_rows.reshape(-1)
    all_heading, all_freq = headings(0, comp_total, freq_count, dir_count)
    wind_gain = wind_term(
        all_heading, all_freq, freq_count, wind_speed.reshape(-1), wind_dir.reshape(-1)
    )
    for step_number in range(SOURCE_STEPS):
        spread = jnp.sqrt(jnp.mean(spectra_now * spectra_now, axis=0) + EPSILON)
        rounded = spectra_now.astype(jnp.bfloat16)
        transfer = jnp.dot(interaction, rounded, preferred_element_type=jnp.float32)
        spectra_now = (
            sea_cells[None]
            * (
                spectra_now
                + RATE * (wind_gain * spectra_now + spectra_now * transfer / spread[None])
            )
            / (1.0 + RATE * WHITECAP * spread[None])
        )

    slots = grid_count * CAP
    owners = nest_owner[:, 0]
    member = (owners[:, None] == jnp.arange(grid_count, dtype=jnp.int32)[None]).astype(jnp.int32)
    slot_rank = jnp.sum((jnp.cumsum(member, axis=0) - member) * member, axis=1)
    column = owners * CAP + slot_rank
    weights = jnp.take(weight_table, weight_index)
    pick_slot = (column[:, None] == jnp.arange(slots, dtype=jnp.int32)[None]).astype(jnp.float32)
    pick_cell = (nest_cell[:, None] == jnp.arange(cell_count, dtype=jnp.int32)[None]).astype(jnp.float32)
    slot_cell = jnp.dot(pick_slot.T, pick_cell, precision=HIGHEST, preferred_element_type=jnp.float32)
    slot_weight = jnp.dot(pick_slot.T, weights, precision=HIGHEST, preferred_element_type=jnp.float32)
    slot_label = jnp.dot(
        pick_slot.T, nest_point.astype(jnp.float32) + 1.0, precision=HIGHEST,
        preferred_element_type=jnp.float32,
    ) - 1.0
    gathered = lax.dot_general(
        slot_cell, spectra_now, (((1,), (1,)), ((), ())), precision=HIGHEST,
        preferred_element_type=jnp.float32,
    )
    send = jnp.concatenate([gathered * slot_weight[:, None], slot_label[:, None]], axis=1)
    send = send.astype(jnp.bfloat16).reshape(grid_count, CAP, comp_total + 1)
    arrived = lax.all_to_all(send, "grid", split_axis=0, concat_axis=0, tiled=True)
    arrived = arrived.reshape(slots, comp_total + 1)
    select = (arrived[:, comp_total][:, None] == jnp.arange(NB_OWN, dtype=jnp.bfloat16)[None]).astype(
        jnp.bfloat16
    )
    nest_spectra = lax.dot_general(
        arrived[:, :comp_total], select, (((0,), (0,)), ((), ())),
        preferred_element_type=jnp.float32,
    )
    return (spectra_now.reshape(comp_total, row_count, lon_count), nest_spectra)


def solution(mesh):
    in_specs = (
        P("spec", None, "grid"),
        P(),
        P(None, "grid"),
        P(None, "grid"),
        P(),
        P("spec", "grid"),
        P("spec", "grid"),
        P(("spec", "grid"), None),
        P(("spec", "grid")),
        P(("spec", "grid")),
        P(("spec", "grid")),
        P(),
    )
    out_specs = (P(None, "spec", "grid"), P(None, ("spec", "grid")))
    return jax.shard_map(local, mesh=mesh, in_specs=in_specs, out_specs=out_specs, check_vma=False)
```

```python
import functools
import math

import jax
import jax.numpy as jnp
from jax import lax
from jax.experimental import pallas as pl
from jax.experimental.pallas import tpu as pltpu
from jax.sharding import PartitionSpec as P

SOURCE_STEPS = 4
NB_OWN = 128
CAP = 16


TWO_PI = 2.0 * math.pi
RATE = 0.2
WIND_GAIN = 0.8
WHITECAP = 1.0
EPSILON = 1e-06
HIGHEST = lax.Precision.HIGHEST


def headings(offset, number, freq_count, dir_count):
    component = offset + jnp.arange(number, dtype=jnp.int32)
    heading = TWO_PI * ((component // freq_count).astype(jnp.float32) + 0.5) / dir_count
    return (heading, component % freq_count)


def wind_term(heading, freq_index, freq_count, speed_flat, direction_flat):
    alignment = (
        jnp.cos(heading)[:, None] * jnp.cos(direction_flat)[None]
        + jnp.sin(heading)[:, None] * jnp.sin(direction_flat)[None]
    )
    scale_freq = (freq_index + 1).astype(jnp.float32) / freq_count
    return WIND_GAIN * scale_freq[:, None] * speed_flat[None] * jnp.maximum(alignment, 0.0)


def propagate_kernel(
    rx_ref, ry_ref, spec_ref, factor_ref, sea_ref, out_ref,
    send_first, send_last, recv_west, recv_east, send_sem, recv_sem,
    result_lo, result_hi, send_buf, a2a_send, a2a_recv,
):
    comps, rows, lons = spec_ref.shape
    spec_count = lax.axis_size("spec")
    grid_count = lax.axis_size("grid")
    chunk = rows // spec_count
    me = lax.axis_index("grid")
    spec = lax.axis_index("spec")
    right = lax.rem(me + 1, grid_count)
    left = lax.rem(me + grid_count - 1, grid_count)
    barrier = pltpu.get_barrier_semaphore()
    for neighbour in (left, right):
        pl.semaphore_signal(barrier, inc=1, device_id=(spec, neighbour), device_id_type=pl.DeviceIdType.MESH)

    def greet(d, carry):
        @pl.when(d != spec)
        def _():
            pl.semaphore_signal(barrier, inc=1, device_id=(d, me), device_id_type=pl.DeviceIdType.MESH)
        return carry

    lax.fori_loop(0, spec_count, greet, 0)
    pl.semaphore_wait(barrier, 2 + spec_count - 1)

    factor = factor_ref[...]
    sea = sea_ref[...]
    edge_lane = lax.broadcasted_iota(jnp.int32, (rows, 128), 1)
    factor_first = factor[:, 0:1]
    factor_last = factor[:, lons - 1 : lons]

    def edges(kk, carry):
        first, last = carry
        rx = rx_ref[kk]
        s_first = spec_ref[kk, :, 0:128][:, 0:1]
        s_last = spec_ref[kk, :, lons - 128 : lons][:, 127:128]
        first = jnp.where(edge_lane == kk, rx * factor_first * s_first, first)
        last = jnp.where(edge_lane == kk, rx * factor_last * s_last, last)
        return first, last

    zero = jnp.zeros((rows, 128), jnp.float32)
    first, last = lax.fori_loop(0, comps, edges, (zero, zero), unroll=3)
    send_first[...] = first
    send_last[...] = last
    to_right = pltpu.make_async_remote_copy(
        src_ref=send_last, dst_ref=recv_west, send_sem=send_sem.at[0], recv_sem=recv_sem.at[0],
        device_id=(spec, right), device_id_type=pl.DeviceIdType.MESH,
    )
    to_left = pltpu.make_async_remote_copy(
        src_ref=send_first, dst_ref=recv_east, send_sem=send_sem.at[1], recv_sem=recv_sem.at[1],
        device_id=(spec, left), device_id_type=pl.DeviceIdType.MESH,
    )
    to_right.start()
    to_left.start()
    to_right.wait()
    to_left.wait()

    lane = lax.broadcasted_iota(jnp.int32, (rows, lons), 1)
    row = lax.broadcasted_iota(jnp.int32, (rows, lons), 0)

    def one(kk, carry):
        rx = rx_ref[kk]
        ry = ry_ref[kk]
        s = spec_ref[kk]
        west_col = jnp.sum(jnp.where(edge_lane == kk, recv_west[...], 0.0), axis=1, keepdims=True)
        east_col = jnp.sum(jnp.where(edge_lane == kk, recv_east[...], 0.0), axis=1, keepdims=True)
        fx = rx * factor * s
        west = jnp.where(lane == 0, west_col, pltpu.roll(fx, 1, 1))
        east = jnp.where(lane == lons - 1, east_col, pltpu.roll(fx, lons - 1, 1))
        change = jnp.where(rx > 0, fx - west, east - fx)
        ax = sea * (s - change)
        fy = ry * factor * ax
        south = jnp.where(row == 0, 0.0, pltpu.roll(fy, 1, 0))
        north = jnp.where(row == rows - 1, 0.0, pltpu.roll(fy, rows - 1, 0))
        change_y = jnp.where(ry > 0, fy - south, north - fy)
        res = sea * (ax - change_y)
        place = pl.ds(pl.multiple_of(kk * rows, rows), rows)
        result_lo[place, :] = res[:, :128]
        result_hi[place, :] = res[:, 128:]
        return carry

    def copy_to(d, slot, start, size):
        return pltpu.make_async_remote_copy(
            src_ref=send_buf.at[d, pl.ds(start, size)], dst_ref=out_ref.at[slot, pl.ds(start, size)],
            send_sem=a2a_send.at[d], recv_sem=a2a_recv.at[slot], device_id=(d, me),
            device_id_type=pl.DeviceIdType.MESH,
        )

    tile = 16
    count = comps // tile
    blocks = [(tile * b, tile) for b in range(count - 1)]
    blocks.append((tile * (count - 1), comps - tile * (count - 1)))
    for start, size in blocks:
        lax.fori_loop(start, start + size, one, 0)

        def regroup(d, carry, start=start, size=size):
            for r in range(chunk):
                i = start * rows + d * chunk + r
                for half, part in ((0, result_lo), (1, result_hi)):
                    at = r * lons + half * 128
                    send_buf[d, pl.ds(start, size), at : at + 128] = part[
                        pl.ds(i, size, stride=rows), :
                    ].astype(send_buf.dtype)

            @pl.when(d != spec)
            def _():
                copy_to(d, spec, start, size).start()

            @pl.when(d == spec)
            def _():
                out_ref[d, pl.ds(start, size), :] = send_buf[d, pl.ds(start, size), :]

            return carry

        lax.fori_loop(0, spec_count, regroup, 0)

    def finish(d, carry):
        @pl.when(d != spec)
        def _():
            copy_to(d, d, 0, comps).wait_send()
            copy_to(d, d, 0, comps).wait_recv()

        return carry

    lax.fori_loop(0, spec_count, finish, 0)


def propagate(spectrum, rate_x, rate_y, factor, sea_float, spec_count):
    comps, rows, lons = spectrum.shape
    chunk = rows // spec_count
    smem = pl.BlockSpec(memory_space=pltpu.SMEM)
    vmem = pl.BlockSpec(memory_space=pltpu.VMEM)
    return pl.pallas_call(
        propagate_kernel,
        in_specs=[smem, smem, vmem, vmem, vmem],
        out_specs=vmem,
        out_shape=jax.ShapeDtypeStruct((spec_count, comps, chunk * lons), jnp.bfloat16),
        scratch_shapes=[
            pltpu.VMEM((rows, 128), jnp.float32),
            pltpu.VMEM((rows, 128), jnp.float32),
            pltpu.VMEM((rows, 128), jnp.float32),
            pltpu.VMEM((rows, 128), jnp.float32),
            pltpu.SemaphoreType.DMA((2,)),
            pltpu.SemaphoreType.DMA((2,)),
            pltpu.VMEM((comps * rows, 128), jnp.float32),
            pltpu.VMEM((comps * rows, 128), jnp.float32),
            pltpu.VMEM((spec_count, comps, chunk * lons), jnp.bfloat16),
            pltpu.SemaphoreType.DMA((spec_count,)),
            pltpu.SemaphoreType.DMA((spec_count,)),
        ],
        compiler_params=pltpu.CompilerParams(
            collective_id=0, has_side_effects=True, vmem_limit_bytes=56 * 1024 * 1024
        ),
        cost_estimate=pl.CostEstimate(
            flops=30 * comps * rows * lons, bytes_accessed=6 * comps * rows * lons, transcendentals=0
        ),
    )(rate_x, rate_y, spectrum, factor, sea_float)


def source_kernel(state_ref, inter_ref, colv_ref, rowv_ref, out_ref, gain, current):
    cols = colv_ref[...]
    rowv = rowv_ref[...]
    speed, cos_w, sin_w, sea = rowv[0:1], rowv[1:2], rowv[2:3], rowv[3:4]
    scale, cos_h, sin_h = cols[:, 0:1], cols[:, 1:2], cols[:, 2:3]
    gain[...] = scale * speed * jnp.maximum(cos_h * cos_w + sin_h * sin_w, 0.0)
    current[...] = state_ref[...]
    comps = current.shape[0]
    for step_number in range(SOURCE_STEPS):
        state = current[...]
        spread = jnp.sqrt(jnp.sum(state * state, axis=0, keepdims=True) / comps + EPSILON)
        transfer = jnp.dot(inter_ref[...], state.astype(jnp.bfloat16), preferred_element_type=jnp.float32)
        current[...] = (
            sea
            * (state + RATE * (gain[...] * state + state * transfer / spread))
            / (1.0 + RATE * WHITECAP * spread)
        )
    out_ref[...] = current[...]


def source_steps(state, interaction, colv, rowv):
    comps, cells = state.shape
    block = 256
    return pl.pallas_call(
        source_kernel,
        grid=(cells // block,),
        in_specs=[
            pl.BlockSpec((comps, block), lambda j: (0, j)),
            pl.BlockSpec((comps, comps), lambda j: (0, 0)),
            pl.BlockSpec((comps, 128), lambda j: (0, 0)),
            pl.BlockSpec((8, block), lambda j: (0, j)),
        ],
        out_specs=pl.BlockSpec((comps, block), lambda j: (0, j)),
        out_shape=jax.ShapeDtypeStruct((comps, cells), jnp.float32),
        scratch_shapes=[
            pltpu.VMEM((comps, block), jnp.float32),
            pltpu.VMEM((comps, block), jnp.float32),
        ],
        compiler_params=pltpu.CompilerParams(
            dimension_semantics=("arbitrary",), vmem_limit_bytes=56 * 1024 * 1024
        ),
        cost_estimate=pl.CostEstimate(
            flops=SOURCE_STEPS * 2 * comps * comps * cells, bytes_accessed=8 * comps * cells,
            transcendentals=SOURCE_STEPS * cells,
        ),
    )(state, interaction, colv, rowv)


def local(
    spectrum,
    group_speed,
    depth_factor,
    sea_mask,
    interaction,
    wind_speed,
    wind_dir,
    nest_owner,
    nest_point,
    nest_cell,
    weight_index,
    weight_table,
):
    comp_dev = spectrum.shape[0]
    freq_count = group_speed.shape[0]
    comp_total = interaction.shape[0]
    dir_count = comp_total // freq_count
    spec_count = lax.axis_size("spec")
    grid_count = lax.axis_size("grid")
    heading, freq_index = headings(
        lax.axis_index("spec") * comp_dev, comp_dev, freq_count, dir_count
    )
    group_rate = jnp.take(group_speed, freq_index)
    rate_x = group_rate * jnp.cos(heading)
    rate_y = group_rate * jnp.sin(heading)
    sea_float = sea_mask.astype(jnp.float32)
    factor = depth_factor * sea_float
    lon_count = spectrum.shape[2]
    received = propagate(spectrum, rate_x, rate_y, factor, sea_float, spec_count)
    row_count = spectrum.shape[1] // spec_count
    cell_count = row_count * lon_count
    spectra_now = received.astype(jnp.float32).reshape(comp_total, cell_count)
    sea_rows = lax.dynamic_slice_in_dim(sea_float, lax.axis_index("spec") * row_count, row_count, 0)
    sea_cells = sea_rows.reshape(-1)
    all_heading, all_freq = headings(0, comp_total, freq_count, dir_count)
    scale_freq = (all_freq + 1).astype(jnp.float32) / freq_count
    colv = jnp.zeros((comp_total, 128), jnp.float32)
    colv = colv.at[:, 0].set(WIND_GAIN * scale_freq).at[:, 1].set(jnp.cos(all_heading)).at[:, 2].set(jnp.sin(all_heading))
    direction = wind_dir.reshape(-1)
    rowv = jnp.zeros((8, cell_count), jnp.float32)
    rowv = (
        rowv.at[0].set(wind_speed.reshape(-1)).at[1].set(jnp.cos(direction))
        .at[2].set(jnp.sin(direction)).at[3].set(sea_cells)
    )
    spectra_now = source_steps(spectra_now, interaction, colv, rowv)

    slots = grid_count * CAP
    owners = nest_owner[:, 0]
    member = (owners[:, None] == jnp.arange(grid_count, dtype=jnp.int32)[None]).astype(jnp.int32)
    slot_rank = jnp.sum((jnp.cumsum(member, axis=0) - member) * member, axis=1)
    column = owners * CAP + slot_rank
    weights = jnp.take(weight_table, weight_index)
    pick_slot = (column[:, None] == jnp.arange(slots, dtype=jnp.int32)[None]).astype(jnp.float32)
    pick_cell = (nest_cell[:, None] == jnp.arange(cell_count, dtype=jnp.int32)[None]).astype(jnp.float32)
    slot_cell = jnp.dot(pick_slot.T, pick_cell, precision=HIGHEST, preferred_element_type=jnp.float32)
    slot_weight = jnp.dot(pick_slot.T, weights, precision=HIGHEST, preferred_element_type=jnp.float32)
    slot_label = jnp.dot(
        pick_slot.T, nest_point.astype(jnp.float32) + 1.0, precision=HIGHEST,
        preferred_element_type=jnp.float32,
    ) - 1.0
    gathered = lax.dot_general(
        slot_cell, spectra_now, (((1,), (1,)), ((), ())), precision=HIGHEST,
        preferred_element_type=jnp.float32,
    )
    send = jnp.concatenate([gathered * slot_weight[:, None], slot_label[:, None]], axis=1)
    send = send.astype(jnp.bfloat16).reshape(grid_count, CAP, comp_total + 1)
    arrived = lax.all_to_all(send, "grid", split_axis=0, concat_axis=0, tiled=True)
    arrived = arrived.reshape(slots, comp_total + 1)
    select = (arrived[:, comp_total][:, None] == jnp.arange(NB_OWN, dtype=jnp.bfloat16)[None]).astype(
        jnp.bfloat16
    )
    nest_spectra = lax.dot_general(
        arrived[:, :comp_total], select, (((0,), (0,)), ((), ())),
        preferred_element_type=jnp.float32,
    )
    return (spectra_now.reshape(comp_total, row_count, lon_count), nest_spectra)


def solution(mesh):
    in_specs = (
        P("spec", None, "grid"),
        P(),
        P(None, "grid"),
        P(None, "grid"),
        P(),
        P("spec", "grid"),
        P("spec", "grid"),
        P(("spec", "grid"), None),
        P(("spec", "grid")),
        P(("spec", "grid")),
        P(("spec", "grid")),
        P(),
    )
    out_specs = (P(None, "spec", "grid"), P(None, ("spec", "grid")))
    return jax.shard_map(local, mesh=mesh, in_specs=in_specs, out_specs=out_specs, check_vma=False)
```

```python
import functools
import math

import jax
import jax.numpy as jnp
from jax import lax
from jax.experimental import pallas as pl
from jax.experimental.pallas import tpu as pltpu
from jax.sharding import PartitionSpec as P

SOURCE_STEPS = 4
NB_OWN = 128
CAP = 16


TWO_PI = 2.0 * math.pi
RATE = 0.2
WIND_GAIN = 0.8
WHITECAP = 1.0
EPSILON = 1e-06
HIGHEST = lax.Precision.HIGHEST


def headings(offset, number, freq_count, dir_count):
    component = offset + jnp.arange(number, dtype=jnp.int32)
    heading = TWO_PI * ((component // freq_count).astype(jnp.float32) + 0.5) / dir_count
    return (heading, component % freq_count)


def wind_term(heading, freq_index, freq_count, speed_flat, direction_flat):
    alignment = (
        jnp.cos(heading)[:, None] * jnp.cos(direction_flat)[None]
        + jnp.sin(heading)[:, None] * jnp.sin(direction_flat)[None]
    )
    scale_freq = (freq_index + 1).astype(jnp.float32) / freq_count
    return WIND_GAIN * scale_freq[:, None] * speed_flat[None] * jnp.maximum(alignment, 0.0)


def propagate_kernel(
    rx_ref, ry_ref, spec_ref, factor_ref, sea_ref, out_ref,
    send_first, send_last, recv_west, recv_east, send_sem, recv_sem,
    result_lo, result_hi, send_buf, a2a_send, a2a_recv,
):
    comps, rows, lons = spec_ref.shape
    spec_count = lax.axis_size("spec")
    grid_count = lax.axis_size("grid")
    chunk = rows // spec_count
    me = lax.axis_index("grid")
    spec = lax.axis_index("spec")
    right = lax.rem(me + 1, grid_count)
    left = lax.rem(me + grid_count - 1, grid_count)
    barrier = pltpu.get_barrier_semaphore()
    for neighbour in (left, right):
        pl.semaphore_signal(barrier, inc=1, device_id=(spec, neighbour), device_id_type=pl.DeviceIdType.MESH)

    def greet(d, carry):
        @pl.when(d != spec)
        def _():
            pl.semaphore_signal(barrier, inc=1, device_id=(d, me), device_id_type=pl.DeviceIdType.MESH)
        return carry

    lax.fori_loop(0, spec_count, greet, 0)
    pl.semaphore_wait(barrier, 2 + spec_count - 1)

    sea = sea_ref[...].astype(jnp.float32)
    factor = factor_ref[...] * sea
    edge_lane = lax.broadcasted_iota(jnp.int32, (rows, 128), 1)
    factor_first = factor[:, 0:1]
    factor_last = factor[:, lons - 1 : lons]

    def edges(kk, carry):
        first, last = carry
        rx = rx_ref[kk]
        s_first = spec_ref[kk, :, 0:128][:, 0:1]
        s_last = spec_ref[kk, :, lons - 128 : lons][:, 127:128]
        first = jnp.where(edge_lane == kk, rx * factor_first * s_first, first)
        last = jnp.where(edge_lane == kk, rx * factor_last * s_last, last)
        return first, last

    zero = jnp.zeros((rows, 128), jnp.float32)
    first, last = lax.fori_loop(0, comps, edges, (zero, zero), unroll=3)
    send_first[...] = first
    send_last[...] = last
    to_right = pltpu.make_async_remote_copy(
        src_ref=send_last, dst_ref=recv_west, send_sem=send_sem.at[0], recv_sem=recv_sem.at[0],
        device_id=(spec, right), device_id_type=pl.DeviceIdType.MESH,
    )
    to_left = pltpu.make_async_remote_copy(
        src_ref=send_first, dst_ref=recv_east, send_sem=send_sem.at[1], recv_sem=recv_sem.at[1],
        device_id=(spec, left), device_id_type=pl.DeviceIdType.MESH,
    )
    to_right.start()
    to_left.start()
    to_right.wait()
    to_left.wait()

    lane = lax.broadcasted_iota(jnp.int32, (rows, lons), 1)
    row = lax.broadcasted_iota(jnp.int32, (rows, lons), 0)

    def one(kk, carry):
        rx = rx_ref[kk]
        ry = ry_ref[kk]
        s = spec_ref[kk]
        west_col = jnp.sum(jnp.where(edge_lane == kk, recv_west[...], 0.0), axis=1, keepdims=True)
        east_col = jnp.sum(jnp.where(edge_lane == kk, recv_east[...], 0.0), axis=1, keepdims=True)
        fx = rx * factor * s
        west = jnp.where(lane == 0, west_col, pltpu.roll(fx, 1, 1))
        east = jnp.where(lane == lons - 1, east_col, pltpu.roll(fx, lons - 1, 1))
        change = jnp.where(rx > 0, fx - west, east - fx)
        ax = sea * (s - change)
        fy = ry * factor * ax
        south = jnp.where(row == 0, 0.0, pltpu.roll(fy, 1, 0))
        north = jnp.where(row == rows - 1, 0.0, pltpu.roll(fy, rows - 1, 0))
        change_y = jnp.where(ry > 0, fy - south, north - fy)
        res = sea * (ax - change_y)
        place = pl.ds(pl.multiple_of(kk * rows, rows), rows)
        result_lo[place, :] = res[:, :128]
        result_hi[place, :] = res[:, 128:]
        return carry

    def copy_to(d, slot, start, size):
        return pltpu.make_async_remote_copy(
            src_ref=send_buf.at[d, pl.ds(start, size)], dst_ref=out_ref.at[slot, pl.ds(start, size)],
            send_sem=a2a_send.at[d], recv_sem=a2a_recv.at[slot], device_id=(d, me),
            device_id_type=pl.DeviceIdType.MESH,
        )

    tile = 16
    count = comps // tile
    blocks = [(tile * b, tile) for b in range(count - 1)]
    blocks.append((tile * (count - 1), comps - tile * (count - 1)))
    for start, size in blocks:
        lax.fori_loop(start, start + size, one, 0)

        def regroup(t, carry, start=start, size=size):
            d = lax.rem(spec + t, spec_count)
            for r in range(chunk):
                i = start * rows + d * chunk + r
                for half, part in ((0, result_lo), (1, result_hi)):
                    at = r * lons + half * 128
                    send_buf[d, pl.ds(start, size), at : at + 128] = part[
                        pl.ds(i, size, stride=rows), :
                    ].astype(send_buf.dtype)

            @pl.when(d != spec)
            def _():
                copy_to(d, spec, start, size).start()

            @pl.when(d == spec)
            def _():
                out_ref[d, pl.ds(start, size), :] = send_buf[d, pl.ds(start, size), :]

            return carry

        lax.fori_loop(0, spec_count, regroup, 0)

    def finish(d, carry):
        @pl.when(d != spec)
        def _():
            copy_to(d, d, 0, comps).wait_send()
            copy_to(d, d, 0, comps).wait_recv()

        return carry

    lax.fori_loop(0, spec_count, finish, 0)


def propagate(spectrum, rate_x, rate_y, factor, sea_float, spec_count):
    comps, rows, lons = spectrum.shape
    chunk = rows // spec_count
    smem = pl.BlockSpec(memory_space=pltpu.SMEM)
    vmem = pl.BlockSpec(memory_space=pltpu.VMEM)
    return pl.pallas_call(
        propagate_kernel,
        in_specs=[smem, smem, vmem, vmem, vmem],
        out_specs=vmem,
        out_shape=jax.ShapeDtypeStruct((spec_count, comps, chunk * lons), jnp.bfloat16),
        scratch_shapes=[
            pltpu.VMEM((rows, 128), jnp.float32),
            pltpu.VMEM((rows, 128), jnp.float32),
            pltpu.VMEM((rows, 128), jnp.float32),
            pltpu.VMEM((rows, 128), jnp.float32),
            pltpu.SemaphoreType.DMA((2,)),
            pltpu.SemaphoreType.DMA((2,)),
            pltpu.VMEM((comps * rows, 128), jnp.float32),
            pltpu.VMEM((comps * rows, 128), jnp.float32),
            pltpu.VMEM((spec_count, comps, chunk * lons), jnp.bfloat16),
            pltpu.SemaphoreType.DMA((spec_count,)),
            pltpu.SemaphoreType.DMA((spec_count,)),
        ],
        compiler_params=pltpu.CompilerParams(
            collective_id=0, has_side_effects=True, vmem_limit_bytes=56 * 1024 * 1024
        ),
        cost_estimate=pl.CostEstimate(
            flops=30 * comps * rows * lons, bytes_accessed=6 * comps * rows * lons, transcendentals=0
        ),
    )(rate_x, rate_y, spectrum, factor, sea_float)


def local(
    spectrum,
    group_speed,
    depth_factor,
    sea_mask,
    interaction,
    wind_speed,
    wind_dir,
    nest_owner,
    nest_point,
    nest_cell,
    weight_index,
    weight_table,
):
    comp_dev = spectrum.shape[0]
    freq_count = group_speed.shape[0]
    comp_total = interaction.shape[0]
    dir_count = comp_total // freq_count
    spec_count = lax.axis_size("spec")
    grid_count = lax.axis_size("grid")
    heading, freq_index = headings(
        lax.axis_index("spec") * comp_dev, comp_dev, freq_count, dir_count
    )
    group_rate = jnp.take(group_speed, freq_index)
    rate_x = group_rate * jnp.cos(heading)
    rate_y = group_rate * jnp.sin(heading)
    sea_float = sea_mask.astype(jnp.float32)
    factor = depth_factor * sea_float
    lon_count = spectrum.shape[2]
    received = propagate(spectrum, rate_x, rate_y, depth_factor, sea_mask, spec_count)
    row_count = spectrum.shape[1] // spec_count
    cell_count = row_count * lon_count
    spectra_now = received.astype(jnp.float32).reshape(comp_total, cell_count)
    sea_rows = lax.dynamic_slice_in_dim(sea_float, lax.axis_index("spec") * row_count, row_count, 0)
    sea_cells = sea_rows.reshape(-1)
    all_heading, all_freq = headings(0, comp_total, freq_count, dir_count)
    wind_gain = wind_term(
        all_heading, all_freq, freq_count, wind_speed.reshape(-1), wind_dir.reshape(-1)
    )
    for step_number in range(SOURCE_STEPS):
        spread = jnp.sqrt(jnp.mean(spectra_now * spectra_now, axis=0) + EPSILON)
        rounded = spectra_now.astype(jnp.bfloat16)
        transfer = jnp.dot(interaction, rounded, preferred_element_type=jnp.float32)
        spectra_now = (
            sea_cells[None]
            * (
                spectra_now
                + RATE * (wind_gain * spectra_now + spectra_now * transfer / spread[None])
            )
            / (1.0 + RATE * WHITECAP * spread[None])
        )

    slots = grid_count * CAP
    owners = nest_owner[:, 0]
    member = (owners[:, None] == jnp.arange(grid_count, dtype=jnp.int32)[None]).astype(jnp.int32)
    slot_rank = jnp.sum((jnp.cumsum(member, axis=0) - member) * member, axis=1)
    column = owners * CAP + slot_rank
    weights = jnp.take(weight_table, weight_index)
    pick_slot = (column[:, None] == jnp.arange(slots, dtype=jnp.int32)[None]).astype(jnp.float32)
    pick_cell = (nest_cell[:, None] == jnp.arange(cell_count, dtype=jnp.int32)[None]).astype(jnp.float32)
    slot_cell = jnp.dot(pick_slot.T, pick_cell, precision=HIGHEST, preferred_element_type=jnp.float32)
    slot_weight = jnp.dot(pick_slot.T, weights, precision=HIGHEST, preferred_element_type=jnp.float32)
    slot_label = jnp.dot(
        pick_slot.T, nest_point.astype(jnp.float32) + 1.0, precision=HIGHEST,
        preferred_element_type=jnp.float32,
    ) - 1.0
    gathered = lax.dot_general(
        slot_cell, spectra_now, (((1,), (1,)), ((), ())), precision=lax.Precision.HIGH,
        preferred_element_type=jnp.float32,
    )
    send = jnp.concatenate([gathered * slot_weight[:, None], slot_label[:, None]], axis=1)
    send = send.astype(jnp.bfloat16).reshape(grid_count, CAP, comp_total + 1)
    arrived = lax.all_to_all(send, "grid", split_axis=0, concat_axis=0, tiled=True)
    arrived = arrived.reshape(slots, comp_total + 1)
    select = (arrived[:, comp_total][:, None] == jnp.arange(NB_OWN, dtype=jnp.bfloat16)[None]).astype(
        jnp.bfloat16
    )
    nest_spectra = lax.dot_general(
        arrived[:, :comp_total], select, (((0,), (0,)), ((), ())),
        preferred_element_type=jnp.float32,
    )
    return (spectra_now.reshape(comp_total, row_count, lon_count), nest_spectra)


def solution(mesh):
    in_specs = (
        P("spec", None, "grid"),
        P(),
        P(None, "grid"),
        P(None, "grid"),
        P(),
        P("spec", "grid"),
        P("spec", "grid"),
        P(("spec", "grid"), None),
        P(("spec", "grid")),
        P(("spec", "grid")),
        P(("spec", "grid")),
        P(),
    )
    out_specs = (P(None, "spec", "grid"), P(None, ("spec", "grid")))
    return jax.shard_map(local, mesh=mesh, in_specs=in_specs, out_specs=out_specs, check_vma=False)
```

```python
import functools
import math

import jax
import jax.numpy as jnp
from jax import lax
from jax.experimental import pallas as pl
from jax.experimental.pallas import tpu as pltpu
from jax.sharding import PartitionSpec as P

SOURCE_STEPS = 4
NB_OWN = 128
CAP = 16


TWO_PI = 2.0 * math.pi
RATE = 0.2
WIND_GAIN = 0.8
WHITECAP = 1.0
EPSILON = 1e-06
HIGHEST = lax.Precision.HIGHEST


def headings(offset, number, freq_count, dir_count):
    component = offset + jnp.arange(number, dtype=jnp.int32)
    heading = TWO_PI * ((component // freq_count).astype(jnp.float32) + 0.5) / dir_count
    return (heading, component % freq_count)


def wind_term(heading, freq_index, freq_count, speed_flat, direction_flat):
    alignment = (
        jnp.cos(heading)[:, None] * jnp.cos(direction_flat)[None]
        + jnp.sin(heading)[:, None] * jnp.sin(direction_flat)[None]
    )
    scale_freq = (freq_index + 1).astype(jnp.float32) / freq_count
    return WIND_GAIN * scale_freq[:, None] * speed_flat[None] * jnp.maximum(alignment, 0.0)


def propagate_kernel(
    rx_ref, ry_ref, spec_ref, factor_ref, sea_ref, out_ref,
    send_first, send_last, recv_west, recv_east, send_sem, recv_sem,
    result_lo, result_hi, send_buf, a2a_send, a2a_recv, recv_buf,
):
    comps, rows, lons = spec_ref.shape
    spec_count = lax.axis_size("spec")
    grid_count = lax.axis_size("grid")
    chunk = rows // spec_count
    me = lax.axis_index("grid")
    spec = lax.axis_index("spec")
    right = lax.rem(me + 1, grid_count)
    left = lax.rem(me + grid_count - 1, grid_count)
    barrier = pltpu.get_barrier_semaphore()
    for neighbour in (left, right):
        pl.semaphore_signal(barrier, inc=1, device_id=(spec, neighbour), device_id_type=pl.DeviceIdType.MESH)

    def greet(d, carry):
        @pl.when(d != spec)
        def _():
            pl.semaphore_signal(barrier, inc=1, device_id=(d, me), device_id_type=pl.DeviceIdType.MESH)
        return carry

    lax.fori_loop(0, spec_count, greet, 0)
    pl.semaphore_wait(barrier, 2 + spec_count - 1)

    sea = sea_ref[...].astype(jnp.float32)
    factor = factor_ref[...] * sea
    edge_lane = lax.broadcasted_iota(jnp.int32, (rows, 128), 1)
    factor_first = factor[:, 0:1]
    factor_last = factor[:, lons - 1 : lons]

    def edges(kk, carry):
        first, last = carry
        rx = rx_ref[kk]
        s_first = spec_ref[kk, :, 0:128][:, 0:1]
        s_last = spec_ref[kk, :, lons - 128 : lons][:, 127:128]
        first = jnp.where(edge_lane == kk, rx * factor_first * s_first, first)
        last = jnp.where(edge_lane == kk, rx * factor_last * s_last, last)
        return first, last

    zero = jnp.zeros((rows, 128), jnp.float32)
    first, last = lax.fori_loop(0, comps, edges, (zero, zero), unroll=3)
    send_first[...] = first
    send_last[...] = last
    to_right = pltpu.make_async_remote_copy(
        src_ref=send_last, dst_ref=recv_west, send_sem=send_sem.at[0], recv_sem=recv_sem.at[0],
        device_id=(spec, right), device_id_type=pl.DeviceIdType.MESH,
    )
    to_left = pltpu.make_async_remote_copy(
        src_ref=send_first, dst_ref=recv_east, send_sem=send_sem.at[1], recv_sem=recv_sem.at[1],
        device_id=(spec, left), device_id_type=pl.DeviceIdType.MESH,
    )
    to_right.start()
    to_left.start()
    to_right.wait()
    to_left.wait()

    lane = lax.broadcasted_iota(jnp.int32, (rows, lons), 1)
    row = lax.broadcasted_iota(jnp.int32, (rows, lons), 0)

    def one(kk, carry):
        rx = rx_ref[kk]
        ry = ry_ref[kk]
        s = spec_ref[kk]
        west_col = jnp.sum(jnp.where(edge_lane == kk, recv_west[...], 0.0), axis=1, keepdims=True)
        east_col = jnp.sum(jnp.where(edge_lane == kk, recv_east[...], 0.0), axis=1, keepdims=True)
        fx = rx * factor * s
        west = jnp.where(lane == 0, west_col, pltpu.roll(fx, 1, 1))
        east = jnp.where(lane == lons - 1, east_col, pltpu.roll(fx, lons - 1, 1))
        change = jnp.where(rx > 0, fx - west, east - fx)
        ax = sea * (s - change)
        fy = ry * factor * ax
        south = jnp.where(row == 0, 0.0, pltpu.roll(fy, 1, 0))
        north = jnp.where(row == rows - 1, 0.0, pltpu.roll(fy, rows - 1, 0))
        change_y = jnp.where(ry > 0, fy - south, north - fy)
        res = sea * (ax - change_y)
        place = pl.ds(pl.multiple_of(kk * rows, rows), rows)
        result_lo[place, :] = res[:, :128]
        result_hi[place, :] = res[:, 128:]
        return carry

    def copy_to(d, slot, start, size):
        return pltpu.make_async_remote_copy(
            src_ref=send_buf.at[d, pl.ds(start, size)], dst_ref=recv_buf.at[slot, pl.ds(start, size)],
            send_sem=a2a_send.at[d], recv_sem=a2a_recv.at[slot], device_id=(d, me),
            device_id_type=pl.DeviceIdType.MESH,
        )

    tile = 16
    count = comps // tile
    blocks = [(tile * b, tile) for b in range(count - 1)]
    blocks.append((tile * (count - 1), comps - tile * (count - 1)))
    for start, size in blocks:
        lax.fori_loop(start, start + size, one, 0)

        def regroup(t, carry, start=start, size=size):
            d = lax.rem(spec + t, spec_count)
            for r in range(chunk):
                i = start * rows + d * chunk + r
                for half, part in ((0, result_lo), (1, result_hi)):
                    at = r * lons + half * 128
                    send_buf[d, pl.ds(start, size), at : at + 128] = part[
                        pl.ds(i, size, stride=rows), :
                    ].astype(send_buf.dtype)

            @pl.when(d != spec)
            def _():
                copy_to(d, spec, start, size).start()

            @pl.when(d == spec)
            def _():
                recv_buf[d, pl.ds(start, size), :] = send_buf[d, pl.ds(start, size), :]

            return carry

        lax.fori_loop(0, spec_count, regroup, 0)

    def finish(d, carry):
        @pl.when(d != spec)
        def _():
            copy_to(d, d, 0, comps).wait_send()
            copy_to(d, d, 0, comps).wait_recv()

        return carry

    lax.fori_loop(0, spec_count, finish, 0)
    for s in range(spec_count):
        out_ref[s * comps : (s + 1) * comps, :] = recv_buf[s].astype(out_ref.dtype)


def propagate(spectrum, rate_x, rate_y, factor, sea_float, spec_count):
    comps, rows, lons = spectrum.shape
    chunk = rows // spec_count
    smem = pl.BlockSpec(memory_space=pltpu.SMEM)
    vmem = pl.BlockSpec(memory_space=pltpu.VMEM)
    return pl.pallas_call(
        propagate_kernel,
        in_specs=[smem, smem, vmem, vmem, vmem],
        out_specs=vmem,
        out_shape=jax.ShapeDtypeStruct((spec_count * comps, chunk * lons), jnp.float32),
        scratch_shapes=[
            pltpu.VMEM((rows, 128), jnp.float32),
            pltpu.VMEM((rows, 128), jnp.float32),
            pltpu.VMEM((rows, 128), jnp.float32),
            pltpu.VMEM((rows, 128), jnp.float32),
            pltpu.SemaphoreType.DMA((2,)),
            pltpu.SemaphoreType.DMA((2,)),
            pltpu.VMEM((comps * rows, 128), jnp.float32),
            pltpu.VMEM((comps * rows, 128), jnp.float32),
            pltpu.VMEM((spec_count, comps, chunk * lons), jnp.bfloat16),
            pltpu.SemaphoreType.DMA((spec_count,)),
            pltpu.SemaphoreType.DMA((spec_count,)),
            pltpu.VMEM((spec_count, comps, chunk * lons), jnp.bfloat16),
        ],
        compiler_params=pltpu.CompilerParams(
            collective_id=0, has_side_effects=True, vmem_limit_bytes=56 * 1024 * 1024
        ),
        cost_estimate=pl.CostEstimate(
            flops=30 * comps * rows * lons, bytes_accessed=6 * comps * rows * lons, transcendentals=0
        ),
    )(rate_x, rate_y, spectrum, factor, sea_float)


def local(
    spectrum,
    group_speed,
    depth_factor,
    sea_mask,
    interaction,
    wind_speed,
    wind_dir,
    nest_owner,
    nest_point,
    nest_cell,
    weight_index,
    weight_table,
):
    comp_dev = spectrum.shape[0]
    freq_count = group_speed.shape[0]
    comp_total = interaction.shape[0]
    dir_count = comp_total // freq_count
    spec_count = lax.axis_size("spec")
    grid_count = lax.axis_size("grid")
    heading, freq_index = headings(
        lax.axis_index("spec") * comp_dev, comp_dev, freq_count, dir_count
    )
    group_rate = jnp.take(group_speed, freq_index)
    rate_x = group_rate * jnp.cos(heading)
    rate_y = group_rate * jnp.sin(heading)
    sea_float = sea_mask.astype(jnp.float32)
    factor = depth_factor * sea_float
    lon_count = spectrum.shape[2]
    received = propagate(spectrum, rate_x, rate_y, depth_factor, sea_mask, spec_count)
    row_count = spectrum.shape[1] // spec_count
    cell_count = row_count * lon_count
    spectra_now = received
    sea_rows = lax.dynamic_slice_in_dim(sea_float, lax.axis_index("spec") * row_count, row_count, 0)
    sea_cells = sea_rows.reshape(-1)
    all_heading, all_freq = headings(0, comp_total, freq_count, dir_count)
    wind_gain = wind_term(
        all_heading, all_freq, freq_count, wind_speed.reshape(-1), wind_dir.reshape(-1)
    )
    for step_number in range(SOURCE_STEPS):
        spread = jnp.sqrt(jnp.mean(spectra_now * spectra_now, axis=0) + EPSILON)
        rounded = spectra_now.astype(jnp.bfloat16)
        transfer = jnp.dot(interaction, rounded, preferred_element_type=jnp.float32)
        spectra_now = (
            sea_cells[None]
            * (
                spectra_now
                + RATE * (wind_gain * spectra_now + spectra_now * transfer / spread[None])
            )
            / (1.0 + RATE * WHITECAP * spread[None])
        )

    slots = grid_count * CAP
    owners = nest_owner[:, 0]
    member = (owners[:, None] == jnp.arange(grid_count, dtype=jnp.int32)[None]).astype(jnp.int32)
    slot_rank = jnp.sum((jnp.cumsum(member, axis=0) - member) * member, axis=1)
    column = owners * CAP + slot_rank
    weights = jnp.take(weight_table, weight_index)
    pick_slot = (column[:, None] == jnp.arange(slots, dtype=jnp.int32)[None]).astype(jnp.float32)
    pick_cell = (nest_cell[:, None] == jnp.arange(cell_count, dtype=jnp.int32)[None]).astype(jnp.float32)
    slot_cell = jnp.dot(pick_slot.T, pick_cell, precision=HIGHEST, preferred_element_type=jnp.float32)
    slot_weight = jnp.dot(pick_slot.T, weights, precision=HIGHEST, preferred_element_type=jnp.float32)
    slot_label = jnp.dot(
        pick_slot.T, nest_point.astype(jnp.float32) + 1.0, precision=HIGHEST,
        preferred_element_type=jnp.float32,
    ) - 1.0
    gathered = lax.dot_general(
        slot_cell, spectra_now, (((1,), (1,)), ((), ())), precision=lax.Precision.HIGH,
        preferred_element_type=jnp.float32,
    )
    send = jnp.concatenate([gathered * slot_weight[:, None], slot_label[:, None]], axis=1)
    send = send.astype(jnp.bfloat16).reshape(grid_count, CAP, comp_total + 1)
    arrived = lax.all_to_all(send, "grid", split_axis=0, concat_axis=0, tiled=True)
    arrived = arrived.reshape(slots, comp_total + 1)
    select = (arrived[:, comp_total][:, None] == jnp.arange(NB_OWN, dtype=jnp.bfloat16)[None]).astype(
        jnp.bfloat16
    )
    nest_spectra = lax.dot_general(
        arrived[:, :comp_total], select, (((0,), (0,)), ((), ())),
        preferred_element_type=jnp.float32,
    )
    return (spectra_now.reshape(comp_total, row_count, lon_count), nest_spectra)


def solution(mesh):
    in_specs = (
        P("spec", None, "grid"),
        P(),
        P(None, "grid"),
        P(None, "grid"),
        P(),
        P("spec", "grid"),
        P("spec", "grid"),
        P(("spec", "grid"), None),
        P(("spec", "grid")),
        P(("spec", "grid")),
        P(("spec", "grid")),
        P(),
    )
    out_specs = (P(None, "spec", "grid"), P(None, ("spec", "grid")))
    return jax.shard_map(local, mesh=mesh, in_specs=in_specs, out_specs=out_specs, check_vma=False)
```

```python
import functools
import math

import jax
import jax.numpy as jnp
from jax import lax
from jax.experimental import pallas as pl
from jax.experimental.pallas import tpu as pltpu
from jax.sharding import PartitionSpec as P

SOURCE_STEPS = 4
NB_OWN = 128
CAP = 16


TWO_PI = 2.0 * math.pi
RATE = 0.2
WIND_GAIN = 0.8
WHITECAP = 1.0
EPSILON = 1e-06
HIGHEST = lax.Precision.HIGHEST


def headings(offset, number, freq_count, dir_count):
    component = offset + jnp.arange(number, dtype=jnp.int32)
    heading = TWO_PI * ((component // freq_count).astype(jnp.float32) + 0.5) / dir_count
    return (heading, component % freq_count)


def wind_term(heading, freq_index, freq_count, speed_flat, direction_flat):
    alignment = (
        jnp.cos(heading)[:, None] * jnp.cos(direction_flat)[None]
        + jnp.sin(heading)[:, None] * jnp.sin(direction_flat)[None]
    )
    scale_freq = (freq_index + 1).astype(jnp.float32) / freq_count
    return WIND_GAIN * scale_freq[:, None] * speed_flat[None] * jnp.maximum(alignment, 0.0)


def propagate_kernel(
    rx_ref, ry_ref, spec_ref, factor_ref, sea_ref, out_ref,
    send_first, send_last, recv_west, recv_east, send_sem, recv_sem,
    result_lo, result_hi, send_buf, a2a_send, a2a_recv, recv_buf,
):
    comps, rows, lons = spec_ref.shape
    spec_count = lax.axis_size("spec")
    grid_count = lax.axis_size("grid")
    chunk = rows // spec_count
    me = lax.axis_index("grid")
    spec = lax.axis_index("spec")
    right = lax.rem(me + 1, grid_count)
    left = lax.rem(me + grid_count - 1, grid_count)
    barrier = pltpu.get_barrier_semaphore()
    for neighbour in (left, right):
        pl.semaphore_signal(barrier, inc=1, device_id=(spec, neighbour), device_id_type=pl.DeviceIdType.MESH)

    def greet(d, carry):
        @pl.when(d != spec)
        def _():
            pl.semaphore_signal(barrier, inc=1, device_id=(d, me), device_id_type=pl.DeviceIdType.MESH)
        return carry

    lax.fori_loop(0, spec_count, greet, 0)
    pl.semaphore_wait(barrier, 2 + spec_count - 1)

    sea = sea_ref[...].astype(jnp.float32)
    factor = factor_ref[...] * sea
    edge_lane = lax.broadcasted_iota(jnp.int32, (rows, 128), 1)
    factor_first = factor[:, 0:1]
    factor_last = factor[:, lons - 1 : lons]

    def edges(kk, carry):
        first, last = carry
        rx = rx_ref[kk]
        s_first = spec_ref[kk, :, 0:128][:, 0:1]
        s_last = spec_ref[kk, :, lons - 128 : lons][:, 127:128]
        first = jnp.where(edge_lane == kk, rx * factor_first * s_first, first)
        last = jnp.where(edge_lane == kk, rx * factor_last * s_last, last)
        return first, last

    zero = jnp.zeros((rows, 128), jnp.float32)
    first, last = lax.fori_loop(0, comps, edges, (zero, zero), unroll=3)
    send_first[...] = first
    send_last[...] = last
    to_right = pltpu.make_async_remote_copy(
        src_ref=send_last, dst_ref=recv_west, send_sem=send_sem.at[0], recv_sem=recv_sem.at[0],
        device_id=(spec, right), device_id_type=pl.DeviceIdType.MESH,
    )
    to_left = pltpu.make_async_remote_copy(
        src_ref=send_first, dst_ref=recv_east, send_sem=send_sem.at[1], recv_sem=recv_sem.at[1],
        device_id=(spec, left), device_id_type=pl.DeviceIdType.MESH,
    )
    to_right.start()
    to_left.start()
    to_right.wait()
    to_left.wait()

    lane = lax.broadcasted_iota(jnp.int32, (rows, lons), 1)
    row = lax.broadcasted_iota(jnp.int32, (rows, lons), 0)

    def one(kk, carry):
        rx = rx_ref[kk]
        ry = ry_ref[kk]
        s = spec_ref[kk]
        west_col = jnp.sum(jnp.where(edge_lane == kk, recv_west[...], 0.0), axis=1, keepdims=True)
        east_col = jnp.sum(jnp.where(edge_lane == kk, recv_east[...], 0.0), axis=1, keepdims=True)
        fx = rx * factor * s
        west = jnp.where(lane == 0, west_col, pltpu.roll(fx, 1, 1))
        east = jnp.where(lane == lons - 1, east_col, pltpu.roll(fx, lons - 1, 1))
        change = jnp.where(rx > 0, fx - west, east - fx)
        ax = sea * (s - change)
        fy = ry * factor * ax
        south = jnp.where(row == 0, 0.0, pltpu.roll(fy, 1, 0))
        north = jnp.where(row == rows - 1, 0.0, pltpu.roll(fy, rows - 1, 0))
        change_y = jnp.where(ry > 0, fy - south, north - fy)
        res = sea * (ax - change_y)
        place = pl.ds(pl.multiple_of(kk * rows, rows), rows)
        result_lo[place, :] = res[:, :128]
        result_hi[place, :] = res[:, 128:]
        return carry

    def copy_to(d, slot, start, size):
        return pltpu.make_async_remote_copy(
            src_ref=send_buf.at[d, pl.ds(start, size)], dst_ref=recv_buf.at[slot, pl.ds(start, size)],
            send_sem=a2a_send.at[d], recv_sem=a2a_recv.at[slot], device_id=(d, me),
            device_id_type=pl.DeviceIdType.MESH,
        )

    tile = 16
    count = comps // tile
    blocks = [(tile * b, tile) for b in range(count - 1)]
    blocks.append((tile * (count - 1), comps - tile * (count - 1)))
    for start, size in blocks:
        lax.fori_loop(start, start + size, one, 0)

        def regroup(t, carry, start=start, size=size):
            d = lax.rem(spec + t, spec_count)
            for r in range(chunk):
                i = start * rows + d * chunk + r
                for half, part in ((0, result_lo), (1, result_hi)):
                    at = r * lons + half * 128
                    send_buf[d, pl.ds(start, size), at : at + 128] = part[
                        pl.ds(i, size, stride=rows), :
                    ].astype(send_buf.dtype)

            @pl.when(d != spec)
            def _():
                copy_to(d, spec, start, size).start()

            @pl.when(d == spec)
            def _():
                recv_buf[d, pl.ds(start, size), :] = send_buf[d, pl.ds(start, size), :]

            return carry

        lax.fori_loop(0, spec_count, regroup, 0)

    def finish(d, carry):
        @pl.when(d != spec)
        def _():
            copy_to(d, d, 0, comps).wait_send()
            copy_to(d, d, 0, comps).wait_recv()

        return carry

    lax.fori_loop(0, spec_count, finish, 0)
    for s in range(spec_count):
        out_ref[s * comps : (s + 1) * comps, :] = recv_buf[s].astype(out_ref.dtype)


def propagate(spectrum, rate_x, rate_y, factor, sea_float, spec_count):
    comps, rows, lons = spectrum.shape
    chunk = rows // spec_count
    smem = pl.BlockSpec(memory_space=pltpu.SMEM)
    vmem = pl.BlockSpec(memory_space=pltpu.VMEM)
    return pl.pallas_call(
        propagate_kernel,
        in_specs=[smem, smem, vmem, vmem, vmem],
        out_specs=vmem,
        out_shape=jax.ShapeDtypeStruct((spec_count * comps, chunk * lons), jnp.float32),
        scratch_shapes=[
            pltpu.VMEM((rows, 128), jnp.float32),
            pltpu.VMEM((rows, 128), jnp.float32),
            pltpu.VMEM((rows, 128), jnp.float32),
            pltpu.VMEM((rows, 128), jnp.float32),
            pltpu.SemaphoreType.DMA((2,)),
            pltpu.SemaphoreType.DMA((2,)),
            pltpu.VMEM((comps * rows, 128), jnp.float32),
            pltpu.VMEM((comps * rows, 128), jnp.float32),
            pltpu.VMEM((spec_count, comps, chunk * lons), jnp.bfloat16),
            pltpu.SemaphoreType.DMA((spec_count,)),
            pltpu.SemaphoreType.DMA((spec_count,)),
            pltpu.VMEM((spec_count, comps, chunk * lons), jnp.bfloat16),
        ],
        compiler_params=pltpu.CompilerParams(
            collective_id=0, has_side_effects=True, vmem_limit_bytes=56 * 1024 * 1024
        ),
        cost_estimate=pl.CostEstimate(
            flops=30 * comps * rows * lons, bytes_accessed=6 * comps * rows * lons, transcendentals=0
        ),
    )(rate_x, rate_y, spectrum, factor, sea_float)


def local(
    spectrum,
    group_speed,
    depth_factor,
    sea_mask,
    interaction,
    wind_speed,
    wind_dir,
    nest_owner,
    nest_point,
    nest_cell,
    weight_index,
    weight_table,
):
    comp_dev = spectrum.shape[0]
    freq_count = group_speed.shape[0]
    comp_total = interaction.shape[0]
    dir_count = comp_total // freq_count
    spec_count = lax.axis_size("spec")
    grid_count = lax.axis_size("grid")
    heading, freq_index = headings(
        lax.axis_index("spec") * comp_dev, comp_dev, freq_count, dir_count
    )
    group_rate = jnp.take(group_speed, freq_index)
    rate_x = group_rate * jnp.cos(heading)
    rate_y = group_rate * jnp.sin(heading)
    sea_float = sea_mask.astype(jnp.float32)
    factor = depth_factor * sea_float
    lon_count = spectrum.shape[2]
    received = propagate(spectrum, rate_x, rate_y, depth_factor, sea_mask, spec_count)
    row_count = spectrum.shape[1] // spec_count
    cell_count = row_count * lon_count
    spectra_now = received
    sea_rows = lax.dynamic_slice_in_dim(sea_float, lax.axis_index("spec") * row_count, row_count, 0)
    sea_cells = sea_rows.reshape(-1)
    all_heading, all_freq = headings(0, comp_total, freq_count, dir_count)
    wind_gain = wind_term(
        all_heading, all_freq, freq_count, wind_speed.reshape(-1), wind_dir.reshape(-1)
    )
    def source_step(step_number, state):
        spread = jnp.sqrt(jnp.mean(state * state, axis=0) + EPSILON)
        rounded = state.astype(jnp.bfloat16)
        transfer = jnp.dot(interaction, rounded, preferred_element_type=jnp.float32)
        return (
            sea_cells[None]
            * (state + RATE * (wind_gain * state + state * transfer / spread[None]))
            / (1.0 + RATE * WHITECAP * spread[None])
        )

    spectra_now = lax.fori_loop(0, SOURCE_STEPS, source_step, spectra_now)

    slots = grid_count * CAP
    owners = nest_owner[:, 0]
    member = (owners[:, None] == jnp.arange(grid_count, dtype=jnp.int32)[None]).astype(jnp.int32)
    slot_rank = jnp.sum((jnp.cumsum(member, axis=0) - member) * member, axis=1)
    column = owners * CAP + slot_rank
    weights = jnp.take(weight_table, weight_index)
    pick_slot = (column[:, None] == jnp.arange(slots, dtype=jnp.int32)[None]).astype(jnp.float32)
    pick_cell = (nest_cell[:, None] == jnp.arange(cell_count, dtype=jnp.int32)[None]).astype(jnp.float32)
    slot_cell = jnp.dot(pick_slot.T, pick_cell, precision=HIGHEST, preferred_element_type=jnp.float32)
    slot_weight = jnp.dot(pick_slot.T, weights, precision=HIGHEST, preferred_element_type=jnp.float32)
    slot_label = jnp.dot(
        pick_slot.T, nest_point.astype(jnp.float32) + 1.0, precision=HIGHEST,
        preferred_element_type=jnp.float32,
    ) - 1.0
    gathered = lax.dot_general(
        slot_cell, spectra_now, (((1,), (1,)), ((), ())), precision=lax.Precision.HIGH,
        preferred_element_type=jnp.float32,
    )
    send = jnp.concatenate([gathered * slot_weight[:, None], slot_label[:, None]], axis=1)
    send = send.astype(jnp.bfloat16).reshape(grid_count, CAP, comp_total + 1)
    arrived = lax.all_to_all(send, "grid", split_axis=0, concat_axis=0, tiled=True)
    arrived = arrived.reshape(slots, comp_total + 1)
    select = (arrived[:, comp_total][:, None] == jnp.arange(NB_OWN, dtype=jnp.bfloat16)[None]).astype(
        jnp.bfloat16
    )
    nest_spectra = lax.dot_general(
        arrived[:, :comp_total], select, (((0,), (0,)), ((), ())),
        preferred_element_type=jnp.float32,
    )
    return (spectra_now.reshape(comp_total, row_count, lon_count), nest_spectra)


def solution(mesh):
    in_specs = (
        P("spec", None, "grid"),
        P(),
        P(None, "grid"),
        P(None, "grid"),
        P(),
        P("spec", "grid"),
        P("spec", "grid"),
        P(("spec", "grid"), None),
        P(("spec", "grid")),
        P(("spec", "grid")),
        P(("spec", "grid")),
        P(),
    )
    out_specs = (P(None, "spec", "grid"), P(None, ("spec", "grid")))
    return jax.shard_map(local, mesh=mesh, in_specs=in_specs, out_specs=out_specs, check_vma=False)
```

```python
import functools
import math

import jax
import jax.numpy as jnp
from jax import lax
from jax.experimental import pallas as pl
from jax.experimental.pallas import tpu as pltpu
from jax.sharding import PartitionSpec as P

SOURCE_STEPS = 4
NB_OWN = 128
CAP = 16


TWO_PI = 2.0 * math.pi
RATE = 0.2
WIND_GAIN = 0.8
WHITECAP = 1.0
EPSILON = 1e-06
HIGHEST = lax.Precision.HIGHEST


def headings(offset, number, freq_count, dir_count):
    component = offset + jnp.arange(number, dtype=jnp.int32)
    heading = TWO_PI * ((component // freq_count).astype(jnp.float32) + 0.5) / dir_count
    return (heading, component % freq_count)


def wind_term(heading, freq_index, freq_count, speed_flat, direction_flat):
    alignment = (
        jnp.cos(heading)[:, None] * jnp.cos(direction_flat)[None]
        + jnp.sin(heading)[:, None] * jnp.sin(direction_flat)[None]
    )
    scale_freq = (freq_index + 1).astype(jnp.float32) / freq_count
    return WIND_GAIN * scale_freq[:, None] * speed_flat[None] * jnp.maximum(alignment, 0.0)


def propagate_kernel(
    rx_ref, ry_ref, spec_ref, factor_ref, sea_ref, out_ref, sumsq_ref,
    send_first, send_last, recv_west, recv_east, send_sem, recv_sem,
    result_lo, result_hi, send_buf, a2a_send, a2a_recv, recv_buf,
):
    comps, rows, lons = spec_ref.shape
    spec_count = lax.axis_size("spec")
    grid_count = lax.axis_size("grid")
    chunk = rows // spec_count
    me = lax.axis_index("grid")
    spec = lax.axis_index("spec")
    right = lax.rem(me + 1, grid_count)
    left = lax.rem(me + grid_count - 1, grid_count)
    barrier = pltpu.get_barrier_semaphore()
    for neighbour in (left, right):
        pl.semaphore_signal(barrier, inc=1, device_id=(spec, neighbour), device_id_type=pl.DeviceIdType.MESH)

    def greet(d, carry):
        @pl.when(d != spec)
        def _():
            pl.semaphore_signal(barrier, inc=1, device_id=(d, me), device_id_type=pl.DeviceIdType.MESH)
        return carry

    lax.fori_loop(0, spec_count, greet, 0)
    pl.semaphore_wait(barrier, 2 + spec_count - 1)

    sea = sea_ref[...].astype(jnp.float32)
    factor = factor_ref[...] * sea
    edge_lane = lax.broadcasted_iota(jnp.int32, (rows, 128), 1)
    factor_first = factor[:, 0:1]
    factor_last = factor[:, lons - 1 : lons]

    def edges(kk, carry):
        first, last = carry
        rx = rx_ref[kk]
        s_first = spec_ref[kk, :, 0:128][:, 0:1]
        s_last = spec_ref[kk, :, lons - 128 : lons][:, 127:128]
        first = jnp.where(edge_lane == kk, rx * factor_first * s_first, first)
        last = jnp.where(edge_lane == kk, rx * factor_last * s_last, last)
        return first, last

    zero = jnp.zeros((rows, 128), jnp.float32)
    first, last = lax.fori_loop(0, comps, edges, (zero, zero), unroll=3)
    send_first[...] = first
    send_last[...] = last
    to_right = pltpu.make_async_remote_copy(
        src_ref=send_last, dst_ref=recv_west, send_sem=send_sem.at[0], recv_sem=recv_sem.at[0],
        device_id=(spec, right), device_id_type=pl.DeviceIdType.MESH,
    )
    to_left = pltpu.make_async_remote_copy(
        src_ref=send_first, dst_ref=recv_east, send_sem=send_sem.at[1], recv_sem=recv_sem.at[1],
        device_id=(spec, left), device_id_type=pl.DeviceIdType.MESH,
    )
    to_right.start()
    to_left.start()
    to_right.wait()
    to_left.wait()

    lane = lax.broadcasted_iota(jnp.int32, (rows, lons), 1)
    row = lax.broadcasted_iota(jnp.int32, (rows, lons), 0)

    def one(kk, carry):
        rx = rx_ref[kk]
        ry = ry_ref[kk]
        s = spec_ref[kk]
        west_col = jnp.sum(jnp.where(edge_lane == kk, recv_west[...], 0.0), axis=1, keepdims=True)
        east_col = jnp.sum(jnp.where(edge_lane == kk, recv_east[...], 0.0), axis=1, keepdims=True)
        fx = rx * factor * s
        west = jnp.where(lane == 0, west_col, pltpu.roll(fx, 1, 1))
        east = jnp.where(lane == lons - 1, east_col, pltpu.roll(fx, lons - 1, 1))
        change = jnp.where(rx > 0, fx - west, east - fx)
        ax = sea * (s - change)
        fy = ry * factor * ax
        south = jnp.where(row == 0, 0.0, pltpu.roll(fy, 1, 0))
        north = jnp.where(row == rows - 1, 0.0, pltpu.roll(fy, rows - 1, 0))
        change_y = jnp.where(ry > 0, fy - south, north - fy)
        res = sea * (ax - change_y)
        place = pl.ds(pl.multiple_of(kk * rows, rows), rows)
        result_lo[place, :] = res[:, :128]
        result_hi[place, :] = res[:, 128:]
        return carry

    def copy_to(d, slot, start, size):
        return pltpu.make_async_remote_copy(
            src_ref=send_buf.at[d, pl.ds(start, size)], dst_ref=recv_buf.at[slot, pl.ds(start, size)],
            send_sem=a2a_send.at[d], recv_sem=a2a_recv.at[slot], device_id=(d, me),
            device_id_type=pl.DeviceIdType.MESH,
        )

    tile = 16
    count = comps // tile
    blocks = [(tile * b, tile) for b in range(count - 1)]
    blocks.append((tile * (count - 1), comps - tile * (count - 1)))
    for start, size in blocks:
        lax.fori_loop(start, start + size, one, 0)

        def regroup(t, carry, start=start, size=size):
            d = lax.rem(spec + t, spec_count)
            for r in range(chunk):
                i = start * rows + d * chunk + r
                for half, part in ((0, result_lo), (1, result_hi)):
                    at = r * lons + half * 128
                    send_buf[d, pl.ds(start, size), at : at + 128] = part[
                        pl.ds(i, size, stride=rows), :
                    ].astype(send_buf.dtype)

            @pl.when(d != spec)
            def _():
                copy_to(d, spec, start, size).start()

            @pl.when(d == spec)
            def _():
                recv_buf[d, pl.ds(start, size), :] = send_buf[d, pl.ds(start, size), :]

            return carry

        lax.fori_loop(0, spec_count, regroup, 0)

    def finish(d, carry):
        @pl.when(d != spec)
        def _():
            copy_to(d, d, 0, comps).wait_send()
            copy_to(d, d, 0, comps).wait_recv()

        return carry

    lax.fori_loop(0, spec_count, finish, 0)
    total = jnp.zeros(sumsq_ref.shape, jnp.float32)
    for s in range(spec_count):
        part = recv_buf[s].astype(out_ref.dtype)
        out_ref[s * comps : (s + 1) * comps, :] = part
        total = total + jnp.sum(part * part, axis=0, keepdims=True)
    sumsq_ref[...] = total


def propagate(spectrum, rate_x, rate_y, factor, sea_float, spec_count):
    comps, rows, lons = spectrum.shape
    chunk = rows // spec_count
    smem = pl.BlockSpec(memory_space=pltpu.SMEM)
    vmem = pl.BlockSpec(memory_space=pltpu.VMEM)
    return pl.pallas_call(
        propagate_kernel,
        in_specs=[smem, smem, vmem, vmem, vmem],
        out_specs=[vmem, vmem],
        out_shape=[
            jax.ShapeDtypeStruct((spec_count * comps, chunk * lons), jnp.float32),
            jax.ShapeDtypeStruct((1, chunk * lons), jnp.float32),
        ],
        scratch_shapes=[
            pltpu.VMEM((rows, 128), jnp.float32),
            pltpu.VMEM((rows, 128), jnp.float32),
            pltpu.VMEM((rows, 128), jnp.float32),
            pltpu.VMEM((rows, 128), jnp.float32),
            pltpu.SemaphoreType.DMA((2,)),
            pltpu.SemaphoreType.DMA((2,)),
            pltpu.VMEM((comps * rows, 128), jnp.float32),
            pltpu.VMEM((comps * rows, 128), jnp.float32),
            pltpu.VMEM((spec_count, comps, chunk * lons), jnp.bfloat16),
            pltpu.SemaphoreType.DMA((spec_count,)),
            pltpu.SemaphoreType.DMA((spec_count,)),
            pltpu.VMEM((spec_count, comps, chunk * lons), jnp.bfloat16),
        ],
        compiler_params=pltpu.CompilerParams(
            collective_id=0, has_side_effects=True, vmem_limit_bytes=56 * 1024 * 1024
        ),
        cost_estimate=pl.CostEstimate(
            flops=30 * comps * rows * lons, bytes_accessed=6 * comps * rows * lons, transcendentals=0
        ),
    )(rate_x, rate_y, spectrum, factor, sea_float)


def local(
    spectrum,
    group_speed,
    depth_factor,
    sea_mask,
    interaction,
    wind_speed,
    wind_dir,
    nest_owner,
    nest_point,
    nest_cell,
    weight_index,
    weight_table,
):
    comp_dev = spectrum.shape[0]
    freq_count = group_speed.shape[0]
    comp_total = interaction.shape[0]
    dir_count = comp_total // freq_count
    spec_count = lax.axis_size("spec")
    grid_count = lax.axis_size("grid")
    heading, freq_index = headings(
        lax.axis_index("spec") * comp_dev, comp_dev, freq_count, dir_count
    )
    repeats = -(-(freq_count + comp_dev) // freq_count)
    group_rate = lax.dynamic_slice_in_dim(
        jnp.tile(group_speed, repeats), lax.rem(lax.axis_index("spec") * comp_dev, freq_count), comp_dev
    )
    rate_x = group_rate * jnp.cos(heading)
    rate_y = group_rate * jnp.sin(heading)
    sea_float = sea_mask.astype(jnp.float32)
    factor = depth_factor * sea_float
    lon_count = spectrum.shape[2]
    received, first_sumsq = propagate(spectrum, rate_x, rate_y, depth_factor, sea_mask, spec_count)
    row_count = spectrum.shape[1] // spec_count
    cell_count = row_count * lon_count
    spectra_now = received
    sea_rows = lax.dynamic_slice_in_dim(sea_float, lax.axis_index("spec") * row_count, row_count, 0)
    sea_cells = sea_rows.reshape(-1)
    all_heading, all_freq = headings(0, comp_total, freq_count, dir_count)
    wind_gain = wind_term(
        all_heading, all_freq, freq_count, wind_speed.reshape(-1), wind_dir.reshape(-1)
    )
    for step_number in range(SOURCE_STEPS):
        if step_number == 0:
            spread = jnp.sqrt(first_sumsq[0] / comp_total + EPSILON)
        else:
            spread = jnp.sqrt(jnp.mean(spectra_now * spectra_now, axis=0) + EPSILON)
        rounded = spectra_now.astype(jnp.bfloat16)
        transfer = jnp.dot(interaction, rounded, preferred_element_type=jnp.float32)
        spectra_now = (
            sea_cells[None]
            * (
                spectra_now
                + RATE * (wind_gain * spectra_now + spectra_now * transfer / spread[None])
            )
            / (1.0 + RATE * WHITECAP * spread[None])
        )

    slots = grid_count * CAP
    owners = nest_owner[:, 0]
    member = (owners[:, None] == jnp.arange(grid_count, dtype=jnp.int32)[None]).astype(jnp.int32)
    slot_rank = jnp.sum((jnp.cumsum(member, axis=0) - member) * member, axis=1)
    column = owners * CAP + slot_rank
    weights = jnp.take(weight_table, weight_index)
    pick_slot = (column[:, None] == jnp.arange(slots, dtype=jnp.int32)[None]).astype(jnp.float32)
    pick_cell = (nest_cell[:, None] == jnp.arange(cell_count, dtype=jnp.int32)[None]).astype(jnp.float32)
    slot_cell = jnp.dot(pick_slot.T, pick_cell, precision=HIGHEST, preferred_element_type=jnp.float32)
    slot_weight = jnp.dot(pick_slot.T, weights, precision=HIGHEST, preferred_element_type=jnp.float32)
    slot_label = jnp.dot(
        pick_slot.T, nest_point.astype(jnp.float32) + 1.0, precision=HIGHEST,
        preferred_element_type=jnp.float32,
    ) - 1.0
    gathered = lax.dot_general(
        slot_cell, spectra_now, (((1,), (1,)), ((), ())), precision=lax.Precision.HIGH,
        preferred_element_type=jnp.float32,
    )
    send = jnp.concatenate([gathered * slot_weight[:, None], slot_label[:, None]], axis=1)
    send = send.astype(jnp.bfloat16).reshape(grid_count, CAP, comp_total + 1)
    arrived = lax.all_to_all(send, "grid", split_axis=0, concat_axis=0, tiled=True)
    arrived = arrived.reshape(slots, comp_total + 1)
    select = (arrived[:, comp_total][:, None] == jnp.arange(NB_OWN, dtype=jnp.bfloat16)[None]).astype(
        jnp.bfloat16
    )
    nest_spectra = lax.dot_general(
        arrived[:, :comp_total], select, (((0,), (0,)), ((), ())),
        preferred_element_type=jnp.float32,
    )
    return (spectra_now.reshape(comp_total, row_count, lon_count), nest_spectra)


def solution(mesh):
    in_specs = (
        P("spec", None, "grid"),
        P(),
        P(None, "grid"),
        P(None, "grid"),
        P(),
        P("spec", "grid"),
        P("spec", "grid"),
        P(("spec", "grid"), None),
        P(("spec", "grid")),
        P(("spec", "grid")),
        P(("spec", "grid")),
        P(),
    )
    out_specs = (P(None, "spec", "grid"), P(None, ("spec", "grid")))
    return jax.shard_map(local, mesh=mesh, in_specs=in_specs, out_specs=out_specs, check_vma=False)
```

```python
import functools
import math

import jax
import jax.numpy as jnp
from jax import lax
from jax.experimental import pallas as pl
from jax.experimental.pallas import tpu as pltpu
from jax.sharding import PartitionSpec as P

SOURCE_STEPS = 4
NB_OWN = 128
CAP = 16


TWO_PI = 2.0 * math.pi
RATE = 0.2
WIND_GAIN = 0.8
WHITECAP = 1.0
EPSILON = 1e-06
HIGHEST = lax.Precision.HIGHEST


def headings(offset, number, freq_count, dir_count):
    component = offset + jnp.arange(number, dtype=jnp.int32)
    heading = TWO_PI * ((component // freq_count).astype(jnp.float32) + 0.5) / dir_count
    return (heading, component % freq_count)


def wind_term(heading, freq_index, freq_count, speed_flat, direction_flat):
    alignment = (
        jnp.cos(heading)[:, None] * jnp.cos(direction_flat)[None]
        + jnp.sin(heading)[:, None] * jnp.sin(direction_flat)[None]
    )
    scale_freq = (freq_index + 1).astype(jnp.float32) / freq_count
    return WIND_GAIN * scale_freq[:, None] * speed_flat[None] * jnp.maximum(alignment, 0.0)


def propagate_kernel(
    rx_ref, ry_ref, spec_ref, factor_ref, sea_ref, out_ref, sumsq_ref,
    send_first, send_last, recv_west, recv_east, send_sem, recv_sem,
    result_lo, result_hi, send_buf, a2a_send, a2a_recv, recv_buf,
):
    comps, rows, lons = spec_ref.shape
    spec_count = lax.axis_size("spec")
    grid_count = lax.axis_size("grid")
    chunk = rows // spec_count
    me = lax.axis_index("grid")
    spec = lax.axis_index("spec")
    right = lax.rem(me + 1, grid_count)
    left = lax.rem(me + grid_count - 1, grid_count)
    barrier = pltpu.get_barrier_semaphore()
    for neighbour in (left, right):
        pl.semaphore_signal(barrier, inc=1, device_id=(spec, neighbour), device_id_type=pl.DeviceIdType.MESH)

    def greet(d, carry):
        @pl.when(d != spec)
        def _():
            pl.semaphore_signal(barrier, inc=1, device_id=(d, me), device_id_type=pl.DeviceIdType.MESH)
        return carry

    lax.fori_loop(0, spec_count, greet, 0)
    pl.semaphore_wait(barrier, 2 + spec_count - 1)

    sea = sea_ref[...].astype(jnp.float32)
    factor = factor_ref[...] * sea
    edge_lane = lax.broadcasted_iota(jnp.int32, (rows, 128), 1)
    factor_first = factor[:, 0:1]
    factor_last = factor[:, lons - 1 : lons]

    def edges(kk, carry):
        first, last = carry
        rx = rx_ref[kk]
        s_first = spec_ref[kk, :, 0:128][:, 0:1]
        s_last = spec_ref[kk, :, lons - 128 : lons][:, 127:128]
        first = jnp.where(edge_lane == kk, rx * factor_first * s_first, first)
        last = jnp.where(edge_lane == kk, rx * factor_last * s_last, last)
        return first, last

    zero = jnp.zeros((rows, 128), jnp.float32)
    first, last = lax.fori_loop(0, comps, edges, (zero, zero), unroll=3)
    send_first[...] = first
    send_last[...] = last
    to_right = pltpu.make_async_remote_copy(
        src_ref=send_last, dst_ref=recv_west, send_sem=send_sem.at[0], recv_sem=recv_sem.at[0],
        device_id=(spec, right), device_id_type=pl.DeviceIdType.MESH,
    )
    to_left = pltpu.make_async_remote_copy(
        src_ref=send_first, dst_ref=recv_east, send_sem=send_sem.at[1], recv_sem=recv_sem.at[1],
        device_id=(spec, left), device_id_type=pl.DeviceIdType.MESH,
    )
    to_right.start()
    to_left.start()
    to_right.wait()
    to_left.wait()

    lane = lax.broadcasted_iota(jnp.int32, (rows, lons), 1)
    row = lax.broadcasted_iota(jnp.int32, (rows, lons), 0)

    def one(kk, carry):
        rx = rx_ref[kk]
        ry = ry_ref[kk]
        s = spec_ref[kk]
        west_col = jnp.sum(jnp.where(edge_lane == kk, recv_west[...], 0.0), axis=1, keepdims=True)
        east_col = jnp.sum(jnp.where(edge_lane == kk, recv_east[...], 0.0), axis=1, keepdims=True)
        fx = rx * factor * s
        west = jnp.where(lane == 0, west_col, pltpu.roll(fx, 1, 1))
        east = jnp.where(lane == lons - 1, east_col, pltpu.roll(fx, lons - 1, 1))
        change = jnp.where(rx > 0, fx - west, east - fx)
        ax = sea * (s - change)
        fy = ry * factor * ax
        south = jnp.where(row == 0, 0.0, pltpu.roll(fy, 1, 0))
        north = jnp.where(row == rows - 1, 0.0, pltpu.roll(fy, rows - 1, 0))
        change_y = jnp.where(ry > 0, fy - south, north - fy)
        res = sea * (ax - change_y)
        place = pl.ds(pl.multiple_of(kk * rows, rows), rows)
        result_lo[place, :] = res[:, :128]
        result_hi[place, :] = res[:, 128:]
        return carry

    def copy_to(d, slot, start, size):
        return pltpu.make_async_remote_copy(
            src_ref=send_buf.at[d, pl.ds(start, size)], dst_ref=recv_buf.at[slot, pl.ds(start, size)],
            send_sem=a2a_send.at[d], recv_sem=a2a_recv.at[slot], device_id=(d, me),
            device_id_type=pl.DeviceIdType.MESH,
        )

    tile = 16
    count = comps // tile
    blocks = [(tile * b, tile) for b in range(count - 1)]
    blocks.append((tile * (count - 1), comps - tile * (count - 1)))
    for start, size in blocks:
        lax.fori_loop(start, start + size, one, 0)

        def regroup(t, carry, start=start, size=size):
            d = lax.rem(spec + t, spec_count)
            for r in range(chunk):
                i = start * rows + d * chunk + r
                for half, part in ((0, result_lo), (1, result_hi)):
                    at = r * lons + half * 128
                    send_buf[d, pl.ds(start, size), at : at + 128] = part[
                        pl.ds(i, size, stride=rows), :
                    ].astype(send_buf.dtype)

            @pl.when(d != spec)
            def _():
                copy_to(d, spec, start, size).start()

            @pl.when(d == spec)
            def _():
                recv_buf[d, pl.ds(start, size), :] = send_buf[d, pl.ds(start, size), :]

            return carry

        lax.fori_loop(0, spec_count, regroup, 0)

    def finish(d, carry):
        @pl.when(d != spec)
        def _():
            copy_to(d, d, 0, comps).wait_send()
            copy_to(d, d, 0, comps).wait_recv()

        return carry

    lax.fori_loop(0, spec_count, finish, 0)
    total = jnp.zeros(sumsq_ref.shape, jnp.float32)
    for s in range(spec_count):
        part = recv_buf[s].astype(out_ref.dtype)
        out_ref[s * comps : (s + 1) * comps, :] = part
        total = total + jnp.sum(part * part, axis=0, keepdims=True)
    sumsq_ref[...] = total


def propagate(spectrum, rate_x, rate_y, factor, sea_float, spec_count):
    comps, rows, lons = spectrum.shape
    chunk = rows // spec_count
    smem = pl.BlockSpec(memory_space=pltpu.SMEM)
    vmem = pl.BlockSpec(memory_space=pltpu.VMEM)
    return pl.pallas_call(
        propagate_kernel,
        in_specs=[smem, smem, vmem, vmem, vmem],
        out_specs=[vmem, vmem],
        out_shape=[
            jax.ShapeDtypeStruct((spec_count * comps, chunk * lons), jnp.float32),
            jax.ShapeDtypeStruct((1, chunk * lons), jnp.float32),
        ],
        scratch_shapes=[
            pltpu.VMEM((rows, 128), jnp.float32),
            pltpu.VMEM((rows, 128), jnp.float32),
            pltpu.VMEM((rows, 128), jnp.float32),
            pltpu.VMEM((rows, 128), jnp.float32),
            pltpu.SemaphoreType.DMA((2,)),
            pltpu.SemaphoreType.DMA((2,)),
            pltpu.VMEM((comps * rows, 128), jnp.float32),
            pltpu.VMEM((comps * rows, 128), jnp.float32),
            pltpu.VMEM((spec_count, comps, chunk * lons), jnp.bfloat16),
            pltpu.SemaphoreType.DMA((spec_count,)),
            pltpu.SemaphoreType.DMA((spec_count,)),
            pltpu.VMEM((spec_count, comps, chunk * lons), jnp.bfloat16),
        ],
        compiler_params=pltpu.CompilerParams(
            collective_id=0, has_side_effects=True, vmem_limit_bytes=56 * 1024 * 1024
        ),
        cost_estimate=pl.CostEstimate(
            flops=30 * comps * rows * lons, bytes_accessed=6 * comps * rows * lons, transcendentals=0
        ),
    )(rate_x, rate_y, spectrum, factor, sea_float)


def local(
    spectrum,
    group_speed,
    depth_factor,
    sea_mask,
    interaction,
    wind_speed,
    wind_dir,
    nest_owner,
    nest_point,
    nest_cell,
    weight_index,
    weight_table,
):
    comp_dev = spectrum.shape[0]
    freq_count = group_speed.shape[0]
    comp_total = interaction.shape[0]
    dir_count = comp_total // freq_count
    spec_count = lax.axis_size("spec")
    grid_count = lax.axis_size("grid")
    heading, freq_index = headings(
        lax.axis_index("spec") * comp_dev, comp_dev, freq_count, dir_count
    )
    repeats = -(-(freq_count + comp_dev) // freq_count)
    group_rate = lax.dynamic_slice_in_dim(
        jnp.tile(group_speed, repeats), lax.rem(lax.axis_index("spec") * comp_dev, freq_count), comp_dev
    )
    rate_x = group_rate * jnp.cos(heading)
    rate_y = group_rate * jnp.sin(heading)
    sea_float = sea_mask.astype(jnp.float32)
    factor = depth_factor * sea_float
    lon_count = spectrum.shape[2]
    received, first_sumsq = propagate(spectrum, rate_x, rate_y, depth_factor, sea_mask, spec_count)
    row_count = spectrum.shape[1] // spec_count
    cell_count = row_count * lon_count
    spectra_now = received
    sea_rows = lax.dynamic_slice_in_dim(sea_float, lax.axis_index("spec") * row_count, row_count, 0)
    sea_cells = sea_rows.reshape(-1)
    all_heading, all_freq = headings(0, comp_total, freq_count, dir_count)
    wind_gain = wind_term(
        all_heading, all_freq, freq_count, wind_speed.reshape(-1), wind_dir.reshape(-1)
    )
    for step_number in range(SOURCE_STEPS):
        if step_number == 0:
            spread = jnp.sqrt(first_sumsq[0] / comp_total + EPSILON)
        else:
            spread = jnp.sqrt(jnp.mean(spectra_now * spectra_now, axis=0) + EPSILON)
        rounded = spectra_now.astype(jnp.bfloat16)
        transfer = jnp.dot(interaction, rounded, preferred_element_type=jnp.float32)
        spectra_now = (
            sea_cells[None]
            * (
                spectra_now
                + RATE * (wind_gain * spectra_now + spectra_now * transfer / spread[None])
            )
            / (1.0 + RATE * WHITECAP * spread[None])
        )

    slots = grid_count * CAP
    owners = nest_owner[:, 0]
    member = (owners[:, None] == jnp.arange(grid_count, dtype=jnp.int32)[None]).astype(jnp.int32)
    slot_rank = jnp.sum((jnp.cumsum(member, axis=0) - member) * member, axis=1)
    column = owners * CAP + slot_rank
    table_rows = weight_table.shape[0]
    weights = jnp.sum(
        jnp.where(
            weight_index[:, None] == jnp.arange(table_rows, dtype=jnp.int32)[None], weight_table[None], 0.0
        ),
        axis=1,
    )
    pick_slot = (column[:, None] == jnp.arange(slots, dtype=jnp.int32)[None]).astype(jnp.float32)
    pick_cell = (nest_cell[:, None] == jnp.arange(cell_count, dtype=jnp.int32)[None]).astype(jnp.float32)
    slot_cell = jnp.dot(pick_slot.T, pick_cell, precision=HIGHEST, preferred_element_type=jnp.float32)
    slot_weight = jnp.dot(pick_slot.T, weights, precision=HIGHEST, preferred_element_type=jnp.float32)
    slot_label = jnp.dot(
        pick_slot.T, nest_point.astype(jnp.float32) + 1.0, precision=HIGHEST,
        preferred_element_type=jnp.float32,
    ) - 1.0
    gathered = lax.dot_general(
        slot_cell, spectra_now, (((1,), (1,)), ((), ())), precision=lax.Precision.HIGH,
        preferred_element_type=jnp.float32,
    )
    send = jnp.concatenate([gathered * slot_weight[:, None], slot_label[:, None]], axis=1)
    send = send.astype(jnp.bfloat16).reshape(grid_count, CAP, comp_total + 1)
    arrived = lax.all_to_all(send, "grid", split_axis=0, concat_axis=0, tiled=True)
    arrived = arrived.reshape(slots, comp_total + 1)
    select = (arrived[:, comp_total][:, None] == jnp.arange(NB_OWN, dtype=jnp.bfloat16)[None]).astype(
        jnp.bfloat16
    )
    nest_spectra = lax.dot_general(
        arrived[:, :comp_total], select, (((0,), (0,)), ((), ())),
        preferred_element_type=jnp.float32,
    )
    return (spectra_now.reshape(comp_total, row_count, lon_count), nest_spectra)


def solution(mesh):
    in_specs = (
        P("spec", None, "grid"),
        P(),
        P(None, "grid"),
        P(None, "grid"),
        P(),
        P("spec", "grid"),
        P("spec", "grid"),
        P(("spec", "grid"), None),
        P(("spec", "grid")),
        P(("spec", "grid")),
        P(("spec", "grid")),
        P(),
    )
    out_specs = (P(None, "spec", "grid"), P(None, ("spec", "grid")))
    return jax.shard_map(local, mesh=mesh, in_specs=in_specs, out_specs=out_specs, check_vma=False)
```

```python
import functools
import math

import jax
import jax.numpy as jnp
from jax import lax
from jax.experimental import pallas as pl
from jax.experimental.pallas import tpu as pltpu
from jax.sharding import PartitionSpec as P

SOURCE_STEPS = 4
NB_OWN = 128
CAP = 16


TWO_PI = 2.0 * math.pi
RATE = 0.2
WIND_GAIN = 0.8
WHITECAP = 1.0
EPSILON = 1e-06
HIGHEST = lax.Precision.HIGHEST


def headings(offset, number, freq_count, dir_count):
    component = offset + jnp.arange(number, dtype=jnp.int32)
    heading = TWO_PI * ((component // freq_count).astype(jnp.float32) + 0.5) / dir_count
    return (heading, component % freq_count)


def wind_term(heading, freq_index, freq_count, speed_flat, direction_flat):
    alignment = (
        jnp.cos(heading)[:, None] * jnp.cos(direction_flat)[None]
        + jnp.sin(heading)[:, None] * jnp.sin(direction_flat)[None]
    )
    scale_freq = (freq_index + 1).astype(jnp.float32) / freq_count
    return WIND_GAIN * scale_freq[:, None] * speed_flat[None] * jnp.maximum(alignment, 0.0)


def propagate_kernel(
    rx_ref, ry_ref, spec_ref, factor_ref, sea_ref, out_ref, sumsq_ref,
    send_first, send_last, recv_west, recv_east, send_sem, recv_sem,
    result_lo, result_hi, send_buf, a2a_send, a2a_recv, recv_buf,
):
    comps, rows, lons = spec_ref.shape
    spec_count = lax.axis_size("spec")
    grid_count = lax.axis_size("grid")
    chunk = rows // spec_count
    me = lax.axis_index("grid")
    spec = lax.axis_index("spec")
    right = lax.rem(me + 1, grid_count)
    left = lax.rem(me + grid_count - 1, grid_count)
    barrier = pltpu.get_barrier_semaphore()
    for neighbour in (left, right):
        pl.semaphore_signal(barrier, inc=1, device_id=(spec, neighbour), device_id_type=pl.DeviceIdType.MESH)

    def greet(d, carry):
        @pl.when(d != spec)
        def _():
            pl.semaphore_signal(barrier, inc=1, device_id=(d, me), device_id_type=pl.DeviceIdType.MESH)
        return carry

    lax.fori_loop(0, spec_count, greet, 0)
    pl.semaphore_wait(barrier, 2 + spec_count - 1)

    sea = sea_ref[...].astype(jnp.float32)
    factor = factor_ref[...] * sea
    edge_lane = lax.broadcasted_iota(jnp.int32, (rows, 128), 1)
    factor_first = factor[:, 0:1]
    factor_last = factor[:, lons - 1 : lons]

    def edges(kk, carry):
        first, last = carry
        rx = rx_ref[kk]
        s_first = spec_ref[kk, :, 0:128][:, 0:1]
        s_last = spec_ref[kk, :, lons - 128 : lons][:, 127:128]
        first = jnp.where(edge_lane == kk, rx * factor_first * s_first, first)
        last = jnp.where(edge_lane == kk, rx * factor_last * s_last, last)
        return first, last

    zero = jnp.zeros((rows, 128), jnp.float32)
    first, last = lax.fori_loop(0, comps, edges, (zero, zero), unroll=3)
    send_first[...] = first
    send_last[...] = last
    to_right = pltpu.make_async_remote_copy(
        src_ref=send_last, dst_ref=recv_west, send_sem=send_sem.at[0], recv_sem=recv_sem.at[0],
        device_id=(spec, right), device_id_type=pl.DeviceIdType.MESH,
    )
    to_left = pltpu.make_async_remote_copy(
        src_ref=send_first, dst_ref=recv_east, send_sem=send_sem.at[1], recv_sem=recv_sem.at[1],
        device_id=(spec, left), device_id_type=pl.DeviceIdType.MESH,
    )
    to_right.start()
    to_left.start()
    to_right.wait()
    to_left.wait()

    lane = lax.broadcasted_iota(jnp.int32, (rows, lons), 1)
    row = lax.broadcasted_iota(jnp.int32, (rows, lons), 0)

    def one(kk, carry):
        rx = rx_ref[kk]
        ry = ry_ref[kk]
        s = spec_ref[kk]
        west_col = jnp.sum(jnp.where(edge_lane == kk, recv_west[...], 0.0), axis=1, keepdims=True)
        east_col = jnp.sum(jnp.where(edge_lane == kk, recv_east[...], 0.0), axis=1, keepdims=True)
        fx = rx * factor * s
        west = jnp.where(lane == 0, west_col, pltpu.roll(fx, 1, 1))
        east = jnp.where(lane == lons - 1, east_col, pltpu.roll(fx, lons - 1, 1))
        change = jnp.where(rx > 0, fx - west, east - fx)
        ax = sea * (s - change)
        fy = ry * factor * ax
        south = jnp.where(row == 0, 0.0, pltpu.roll(fy, 1, 0))
        north = jnp.where(row == rows - 1, 0.0, pltpu.roll(fy, rows - 1, 0))
        change_y = jnp.where(ry > 0, fy - south, north - fy)
        res = sea * (ax - change_y)
        place = pl.ds(pl.multiple_of(kk * rows, rows), rows)
        result_lo[place, :] = res[:, :128]
        result_hi[place, :] = res[:, 128:]
        return carry

    def copy_to(d, slot, start, size):
        return pltpu.make_async_remote_copy(
            src_ref=send_buf.at[d, pl.ds(start, size)], dst_ref=recv_buf.at[slot, pl.ds(start, size)],
            send_sem=a2a_send.at[d], recv_sem=a2a_recv.at[slot], device_id=(d, me),
            device_id_type=pl.DeviceIdType.MESH,
        )

    tile = 16
    count = comps // tile
    blocks = [(tile * b, tile) for b in range(count - 1)]
    blocks.append((tile * (count - 1), comps - tile * (count - 1)))
    for start, size in blocks:
        lax.fori_loop(start, start + size, one, 0, unroll=2)

        def regroup(t, carry, start=start, size=size):
            d = lax.rem(spec + t, spec_count)
            for r in range(chunk):
                i = start * rows + d * chunk + r
                for half, part in ((0, result_lo), (1, result_hi)):
                    at = r * lons + half * 128
                    send_buf[d, pl.ds(start, size), at : at + 128] = part[
                        pl.ds(i, size, stride=rows), :
                    ].astype(send_buf.dtype)

            @pl.when(d != spec)
            def _():
                copy_to(d, spec, start, size).start()

            @pl.when(d == spec)
            def _():
                recv_buf[d, pl.ds(start, size), :] = send_buf[d, pl.ds(start, size), :]

            return carry

        lax.fori_loop(0, spec_count, regroup, 0)

    def finish(d, carry):
        @pl.when(d != spec)
        def _():
            copy_to(d, d, 0, comps).wait_send()
            copy_to(d, d, 0, comps).wait_recv()

        return carry

    lax.fori_loop(0, spec_count, finish, 0)
    total = jnp.zeros(sumsq_ref.shape, jnp.float32)
    for s in range(spec_count):
        part = recv_buf[s].astype(out_ref.dtype)
        out_ref[s * comps : (s + 1) * comps, :] = part
        total = total + jnp.sum(part * part, axis=0, keepdims=True)
    sumsq_ref[...] = total


def propagate(spectrum, rate_x, rate_y, factor, sea_float, spec_count):
    comps, rows, lons = spectrum.shape
    chunk = rows // spec_count
    smem = pl.BlockSpec(memory_space=pltpu.SMEM)
    vmem = pl.BlockSpec(memory_space=pltpu.VMEM)
    return pl.pallas_call(
        propagate_kernel,
        in_specs=[smem, smem, vmem, vmem, vmem],
        out_specs=[vmem, vmem],
        out_shape=[
            jax.ShapeDtypeStruct((spec_count * comps, chunk * lons), jnp.float32),
            jax.ShapeDtypeStruct((1, chunk * lons), jnp.float32),
        ],
        scratch_shapes=[
            pltpu.VMEM((rows, 128), jnp.float32),
            pltpu.VMEM((rows, 128), jnp.float32),
            pltpu.VMEM((rows, 128), jnp.float32),
            pltpu.VMEM((rows, 128), jnp.float32),
            pltpu.SemaphoreType.DMA((2,)),
            pltpu.SemaphoreType.DMA((2,)),
            pltpu.VMEM((comps * rows, 128), jnp.float32),
            pltpu.VMEM((comps * rows, 128), jnp.float32),
            pltpu.VMEM((spec_count, comps, chunk * lons), jnp.bfloat16),
            pltpu.SemaphoreType.DMA((spec_count,)),
            pltpu.SemaphoreType.DMA((spec_count,)),
            pltpu.VMEM((spec_count, comps, chunk * lons), jnp.bfloat16),
        ],
        compiler_params=pltpu.CompilerParams(
            collective_id=0, has_side_effects=True, vmem_limit_bytes=56 * 1024 * 1024
        ),
        cost_estimate=pl.CostEstimate(
            flops=30 * comps * rows * lons, bytes_accessed=6 * comps * rows * lons, transcendentals=0
        ),
    )(rate_x, rate_y, spectrum, factor, sea_float)


def local(
    spectrum,
    group_speed,
    depth_factor,
    sea_mask,
    interaction,
    wind_speed,
    wind_dir,
    nest_owner,
    nest_point,
    nest_cell,
    weight_index,
    weight_table,
):
    comp_dev = spectrum.shape[0]
    freq_count = group_speed.shape[0]
    comp_total = interaction.shape[0]
    dir_count = comp_total // freq_count
    spec_count = lax.axis_size("spec")
    grid_count = lax.axis_size("grid")
    heading, freq_index = headings(
        lax.axis_index("spec") * comp_dev, comp_dev, freq_count, dir_count
    )
    repeats = -(-(freq_count + comp_dev) // freq_count)
    group_rate = lax.dynamic_slice_in_dim(
        jnp.tile(group_speed, repeats), lax.rem(lax.axis_index("spec") * comp_dev, freq_count), comp_dev
    )
    rate_x = group_rate * jnp.cos(heading)
    rate_y = group_rate * jnp.sin(heading)
    sea_float = sea_mask.astype(jnp.float32)
    factor = depth_factor * sea_float
    lon_count = spectrum.shape[2]
    received, first_sumsq = propagate(spectrum, rate_x, rate_y, depth_factor, sea_mask, spec_count)
    row_count = spectrum.shape[1] // spec_count
    cell_count = row_count * lon_count
    spectra_now = received
    sea_rows = lax.dynamic_slice_in_dim(sea_float, lax.axis_index("spec") * row_count, row_count, 0)
    sea_cells = sea_rows.reshape(-1)
    all_heading, all_freq = headings(0, comp_total, freq_count, dir_count)
    wind_gain = wind_term(
        all_heading, all_freq, freq_count, wind_speed.reshape(-1), wind_dir.reshape(-1)
    )
    for step_number in range(SOURCE_STEPS):
        if step_number == 0:
            spread = jnp.sqrt(first_sumsq[0] / comp_total + EPSILON)
        else:
            spread = jnp.sqrt(jnp.mean(spectra_now * spectra_now, axis=0) + EPSILON)
        rounded = spectra_now.astype(jnp.bfloat16)
        transfer = jnp.dot(interaction, rounded, preferred_element_type=jnp.float32)
        spectra_now = (
            sea_cells[None]
            * (
                spectra_now
                + RATE * (wind_gain * spectra_now + spectra_now * transfer / spread[None])
            )
            / (1.0 + RATE * WHITECAP * spread[None])
        )

    slots = grid_count * CAP
    owners = nest_owner[:, 0]
    member = (owners[:, None] == jnp.arange(grid_count, dtype=jnp.int32)[None]).astype(jnp.int32)
    slot_rank = jnp.sum((jnp.cumsum(member, axis=0) - member) * member, axis=1)
    column = owners * CAP + slot_rank
    table_rows = weight_table.shape[0]
    weights = jnp.sum(
        jnp.where(
            weight_index[:, None] == jnp.arange(table_rows, dtype=jnp.int32)[None], weight_table[None], 0.0
        ),
        axis=1,
    )
    pick_slot = (column[:, None] == jnp.arange(slots, dtype=jnp.int32)[None]).astype(jnp.float32)
    pick_cell = (nest_cell[:, None] == jnp.arange(cell_count, dtype=jnp.int32)[None]).astype(jnp.float32)
    slot_cell = jnp.dot(pick_slot.T, pick_cell, precision=HIGHEST, preferred_element_type=jnp.float32)
    slot_weight = jnp.dot(pick_slot.T, weights, precision=HIGHEST, preferred_element_type=jnp.float32)
    slot_label = jnp.dot(
        pick_slot.T, nest_point.astype(jnp.float32) + 1.0, precision=HIGHEST,
        preferred_element_type=jnp.float32,
    ) - 1.0
    gathered = lax.dot_general(
        slot_cell, spectra_now, (((1,), (1,)), ((), ())), precision=lax.Precision.HIGH,
        preferred_element_type=jnp.float32,
    )
    send = jnp.concatenate([gathered * slot_weight[:, None], slot_label[:, None]], axis=1)
    send = send.astype(jnp.bfloat16).reshape(grid_count, CAP, comp_total + 1)
    arrived = lax.all_to_all(send, "grid", split_axis=0, concat_axis=0, tiled=True)
    arrived = arrived.reshape(slots, comp_total + 1)
    select = (arrived[:, comp_total][:, None] == jnp.arange(NB_OWN, dtype=jnp.bfloat16)[None]).astype(
        jnp.bfloat16
    )
    nest_spectra = lax.dot_general(
        arrived[:, :comp_total], select, (((0,), (0,)), ((), ())),
        preferred_element_type=jnp.float32,
    )
    return (spectra_now.reshape(comp_total, row_count, lon_count), nest_spectra)


def solution(mesh):
    in_specs = (
        P("spec", None, "grid"),
        P(),
        P(None, "grid"),
        P(None, "grid"),
        P(),
        P("spec", "grid"),
        P("spec", "grid"),
        P(("spec", "grid"), None),
        P(("spec", "grid")),
        P(("spec", "grid")),
        P(("spec", "grid")),
        P(),
    )
    out_specs = (P(None, "spec", "grid"), P(None, ("spec", "grid")))
    return jax.shard_map(local, mesh=mesh, in_specs=in_specs, out_specs=out_specs, check_vma=False)
```

```python
import functools
import math

import jax
import jax.numpy as jnp
from jax import lax
from jax.experimental import pallas as pl
from jax.experimental.pallas import tpu as pltpu
from jax.sharding import PartitionSpec as P

SOURCE_STEPS = 4
NB_OWN = 128
CAP = 16


TWO_PI = 2.0 * math.pi
RATE = 0.2
WIND_GAIN = 0.8
WHITECAP = 1.0
EPSILON = 1e-06
HIGHEST = lax.Precision.HIGHEST


def headings(offset, number, freq_count, dir_count):
    component = offset + jnp.arange(number, dtype=jnp.int32)
    heading = TWO_PI * ((component // freq_count).astype(jnp.float32) + 0.5) / dir_count
    return (heading, component % freq_count)


def wind_term(heading, freq_index, freq_count, speed_flat, direction_flat):
    alignment = (
        jnp.cos(heading)[:, None] * jnp.cos(direction_flat)[None]
        + jnp.sin(heading)[:, None] * jnp.sin(direction_flat)[None]
    )
    scale_freq = (freq_index + 1).astype(jnp.float32) / freq_count
    return WIND_GAIN * scale_freq[:, None] * speed_flat[None] * jnp.maximum(alignment, 0.0)


def propagate_kernel(
    rx_ref, ry_ref, spec_ref, factor_ref, sea_ref, out_ref, sumsq_ref,
    send_first, send_last, recv_west, recv_east, send_sem, recv_sem,
    result_lo, result_hi, send_buf, a2a_send, a2a_recv, recv_buf,
):
    comps, rows, lons = spec_ref.shape
    spec_count = lax.axis_size("spec")
    grid_count = lax.axis_size("grid")
    chunk = rows // spec_count
    me = lax.axis_index("grid")
    spec = lax.axis_index("spec")
    right = lax.rem(me + 1, grid_count)
    left = lax.rem(me + grid_count - 1, grid_count)
    barrier = pltpu.get_barrier_semaphore()
    for neighbour in (left, right):
        pl.semaphore_signal(barrier, inc=1, device_id=(spec, neighbour), device_id_type=pl.DeviceIdType.MESH)

    def greet(d, carry):
        @pl.when(d != spec)
        def _():
            pl.semaphore_signal(barrier, inc=1, device_id=(d, me), device_id_type=pl.DeviceIdType.MESH)
        return carry

    lax.fori_loop(0, spec_count, greet, 0)
    pl.semaphore_wait(barrier, 2 + spec_count - 1)

    sea = sea_ref[...].astype(jnp.float32)
    factor = factor_ref[...] * sea
    edge_lane = lax.broadcasted_iota(jnp.int32, (rows, 128), 1)
    factor_first = factor[:, 0:1]
    factor_last = factor[:, lons - 1 : lons]

    def edges(kk, carry):
        first, last = carry
        rx = rx_ref[kk]
        s_first = spec_ref[kk, :, 0:128][:, 0:1]
        s_last = spec_ref[kk, :, lons - 128 : lons][:, 127:128]
        first = jnp.where(edge_lane == kk, rx * factor_first * s_first, first)
        last = jnp.where(edge_lane == kk, rx * factor_last * s_last, last)
        return first, last

    zero = jnp.zeros((rows, 128), jnp.float32)
    first, last = lax.fori_loop(0, comps, edges, (zero, zero), unroll=3)
    send_first[...] = first
    send_last[...] = last
    to_right = pltpu.make_async_remote_copy(
        src_ref=send_last, dst_ref=recv_west, send_sem=send_sem.at[0], recv_sem=recv_sem.at[0],
        device_id=(spec, right), device_id_type=pl.DeviceIdType.MESH,
    )
    to_left = pltpu.make_async_remote_copy(
        src_ref=send_first, dst_ref=recv_east, send_sem=send_sem.at[1], recv_sem=recv_sem.at[1],
        device_id=(spec, left), device_id_type=pl.DeviceIdType.MESH,
    )
    to_right.start()
    to_left.start()
    to_right.wait()
    to_left.wait()

    lane = lax.broadcasted_iota(jnp.int32, (rows, lons), 1)
    row = lax.broadcasted_iota(jnp.int32, (rows, lons), 0)

    def one(kk, carry):
        rx = rx_ref[kk]
        ry = ry_ref[kk]
        s = spec_ref[kk]
        west_col = jnp.sum(jnp.where(edge_lane == kk, recv_west[...], 0.0), axis=1, keepdims=True)
        east_col = jnp.sum(jnp.where(edge_lane == kk, recv_east[...], 0.0), axis=1, keepdims=True)
        fx = rx * factor * s
        west = jnp.where(lane == 0, west_col, pltpu.roll(fx, 1, 1))
        east = jnp.where(lane == lons - 1, east_col, pltpu.roll(fx, lons - 1, 1))
        change = jnp.where(rx > 0, fx - west, east - fx)
        ax = sea * (s - change)
        fy = ry * factor * ax
        south = jnp.where(row == 0, 0.0, pltpu.roll(fy, 1, 0))
        north = jnp.where(row == rows - 1, 0.0, pltpu.roll(fy, rows - 1, 0))
        change_y = jnp.where(ry > 0, fy - south, north - fy)
        res = sea * (ax - change_y)
        place = pl.ds(pl.multiple_of(kk * rows, rows), rows)
        result_lo[place, :] = res[:, :128]
        result_hi[place, :] = res[:, 128:]
        return carry

    def copy_to(d, slot, start, size):
        return pltpu.make_async_remote_copy(
            src_ref=send_buf.at[d, pl.ds(start, size)], dst_ref=recv_buf.at[slot, pl.ds(start, size)],
            send_sem=a2a_send.at[d], recv_sem=a2a_recv.at[slot], device_id=(d, me),
            device_id_type=pl.DeviceIdType.MESH,
        )

    tile = 16
    count = comps // tile
    blocks = [(tile * b, tile) for b in range(count - 1)]
    blocks.append((tile * (count - 1), comps - tile * (count - 1)))
    for start, size in blocks:
        lax.fori_loop(start, start + size, one, 0, unroll=4)

        def regroup(t, carry, start=start, size=size):
            d = lax.rem(spec + t, spec_count)
            for r in range(chunk):
                i = start * rows + d * chunk + r
                for half, part in ((0, result_lo), (1, result_hi)):
                    at = r * lons + half * 128
                    send_buf[d, pl.ds(start, size), at : at + 128] = part[
                        pl.ds(i, size, stride=rows), :
                    ].astype(send_buf.dtype)

            @pl.when(d != spec)
            def _():
                copy_to(d, spec, start, size).start()

            @pl.when(d == spec)
            def _():
                recv_buf[d, pl.ds(start, size), :] = send_buf[d, pl.ds(start, size), :]

            return carry

        lax.fori_loop(0, spec_count, regroup, 0, unroll=2)

    def finish(d, carry):
        @pl.when(d != spec)
        def _():
            copy_to(d, d, 0, comps).wait_send()
            copy_to(d, d, 0, comps).wait_recv()

        return carry

    lax.fori_loop(0, spec_count, finish, 0)
    total = jnp.zeros(sumsq_ref.shape, jnp.float32)
    for s in range(spec_count):
        part = recv_buf[s].astype(out_ref.dtype)
        out_ref[s * comps : (s + 1) * comps, :] = part
        total = total + jnp.sum(part * part, axis=0, keepdims=True)
    sumsq_ref[...] = total


def propagate(spectrum, rate_x, rate_y, factor, sea_float, spec_count):
    comps, rows, lons = spectrum.shape
    chunk = rows // spec_count
    smem = pl.BlockSpec(memory_space=pltpu.SMEM)
    vmem = pl.BlockSpec(memory_space=pltpu.VMEM)
    return pl.pallas_call(
        propagate_kernel,
        in_specs=[smem, smem, vmem, vmem, vmem],
        out_specs=[vmem, vmem],
        out_shape=[
            jax.ShapeDtypeStruct((spec_count * comps, chunk * lons), jnp.float32),
            jax.ShapeDtypeStruct((1, chunk * lons), jnp.float32),
        ],
        scratch_shapes=[
            pltpu.VMEM((rows, 128), jnp.float32),
            pltpu.VMEM((rows, 128), jnp.float32),
            pltpu.VMEM((rows, 128), jnp.float32),
            pltpu.VMEM((rows, 128), jnp.float32),
            pltpu.SemaphoreType.DMA((2,)),
            pltpu.SemaphoreType.DMA((2,)),
            pltpu.VMEM((comps * rows, 128), jnp.float32),
            pltpu.VMEM((comps * rows, 128), jnp.float32),
            pltpu.VMEM((spec_count, comps, chunk * lons), jnp.bfloat16),
            pltpu.SemaphoreType.DMA((spec_count,)),
            pltpu.SemaphoreType.DMA((spec_count,)),
            pltpu.VMEM((spec_count, comps, chunk * lons), jnp.bfloat16),
        ],
        compiler_params=pltpu.CompilerParams(
            collective_id=0, has_side_effects=True, vmem_limit_bytes=56 * 1024 * 1024
        ),
        cost_estimate=pl.CostEstimate(
            flops=30 * comps * rows * lons, bytes_accessed=6 * comps * rows * lons, transcendentals=0
        ),
    )(rate_x, rate_y, spectrum, factor, sea_float)


def local(
    spectrum,
    group_speed,
    depth_factor,
    sea_mask,
    interaction,
    wind_speed,
    wind_dir,
    nest_owner,
    nest_point,
    nest_cell,
    weight_index,
    weight_table,
):
    comp_dev = spectrum.shape[0]
    freq_count = group_speed.shape[0]
    comp_total = interaction.shape[0]
    dir_count = comp_total // freq_count
    spec_count = lax.axis_size("spec")
    grid_count = lax.axis_size("grid")
    heading, freq_index = headings(
        lax.axis_index("spec") * comp_dev, comp_dev, freq_count, dir_count
    )
    repeats = -(-(freq_count + comp_dev) // freq_count)
    group_rate = lax.dynamic_slice_in_dim(
        jnp.tile(group_speed, repeats), lax.rem(lax.axis_index("spec") * comp_dev, freq_count), comp_dev
    )
    rate_x = group_rate * jnp.cos(heading)
    rate_y = group_rate * jnp.sin(heading)
    sea_float = sea_mask.astype(jnp.float32)
    factor = depth_factor * sea_float
    lon_count = spectrum.shape[2]
    received, first_sumsq = propagate(spectrum, rate_x, rate_y, depth_factor, sea_mask, spec_count)
    row_count = spectrum.shape[1] // spec_count
    cell_count = row_count * lon_count
    spectra_now = received
    sea_rows = lax.dynamic_slice_in_dim(sea_float, lax.axis_index("spec") * row_count, row_count, 0)
    sea_cells = sea_rows.reshape(-1)
    all_heading, all_freq = headings(0, comp_total, freq_count, dir_count)
    wind_gain = wind_term(
        all_heading, all_freq, freq_count, wind_speed.reshape(-1), wind_dir.reshape(-1)
    )
    for step_number in range(SOURCE_STEPS):
        if step_number == 0:
            spread = jnp.sqrt(first_sumsq[0] / comp_total + EPSILON)
        else:
            spread = jnp.sqrt(jnp.mean(spectra_now * spectra_now, axis=0) + EPSILON)
        rounded = spectra_now.astype(jnp.bfloat16)
        transfer = jnp.dot(interaction, rounded, preferred_element_type=jnp.float32)
        spectra_now = (
            sea_cells[None]
            * (
                spectra_now
                + RATE * (wind_gain * spectra_now + spectra_now * transfer / spread[None])
            )
            / (1.0 + RATE * WHITECAP * spread[None])
        )

    slots = grid_count * CAP
    owners = nest_owner[:, 0]
    member = (owners[:, None] == jnp.arange(grid_count, dtype=jnp.int32)[None]).astype(jnp.int32)
    slot_rank = jnp.sum((jnp.cumsum(member, axis=0) - member) * member, axis=1)
    column = owners * CAP + slot_rank
    table_rows = weight_table.shape[0]
    weights = jnp.sum(
        jnp.where(
            weight_index[:, None] == jnp.arange(table_rows, dtype=jnp.int32)[None], weight_table[None], 0.0
        ),
        axis=1,
    )
    pick_slot = (column[:, None] == jnp.arange(slots, dtype=jnp.int32)[None]).astype(jnp.float32)
    pick_cell = (nest_cell[:, None] == jnp.arange(cell_count, dtype=jnp.int32)[None]).astype(jnp.float32)
    slot_cell = jnp.dot(pick_slot.T, pick_cell, precision=HIGHEST, preferred_element_type=jnp.float32)
    slot_weight = jnp.dot(pick_slot.T, weights, precision=HIGHEST, preferred_element_type=jnp.float32)
    slot_label = jnp.dot(
        pick_slot.T, nest_point.astype(jnp.float32) + 1.0, precision=HIGHEST,
        preferred_element_type=jnp.float32,
    ) - 1.0
    gathered = lax.dot_general(
        slot_cell, spectra_now, (((1,), (1,)), ((), ())), precision=lax.Precision.HIGH,
        preferred_element_type=jnp.float32,
    )
    send = jnp.concatenate([gathered * slot_weight[:, None], slot_label[:, None]], axis=1)
    send = send.astype(jnp.bfloat16).reshape(grid_count, CAP, comp_total + 1)
    arrived = lax.all_to_all(send, "grid", split_axis=0, concat_axis=0, tiled=True)
    arrived = arrived.reshape(slots, comp_total + 1)
    select = (arrived[:, comp_total][:, None] == jnp.arange(NB_OWN, dtype=jnp.bfloat16)[None]).astype(
        jnp.bfloat16
    )
    nest_spectra = lax.dot_general(
        arrived[:, :comp_total], select, (((0,), (0,)), ((), ())),
        preferred_element_type=jnp.float32,
    )
    return (spectra_now.reshape(comp_total, row_count, lon_count), nest_spectra)


def solution(mesh):
    in_specs = (
        P("spec", None, "grid"),
        P(),
        P(None, "grid"),
        P(None, "grid"),
        P(),
        P("spec", "grid"),
        P("spec", "grid"),
        P(("spec", "grid"), None),
        P(("spec", "grid")),
        P(("spec", "grid")),
        P(("spec", "grid")),
        P(),
    )
    out_specs = (P(None, "spec", "grid"), P(None, ("spec", "grid")))
    return jax.shard_map(local, mesh=mesh, in_specs=in_specs, out_specs=out_specs, check_vma=False)
```

```python
import functools
import math

import jax
import jax.numpy as jnp
from jax import lax
from jax.experimental import pallas as pl
from jax.experimental.pallas import tpu as pltpu
from jax.sharding import PartitionSpec as P

SOURCE_STEPS = 4
NB_OWN = 128
CAP = 16


TWO_PI = 2.0 * math.pi
RATE = 0.2
WIND_GAIN = 0.8
WHITECAP = 1.0
EPSILON = 1e-06
HIGHEST = lax.Precision.HIGHEST


def headings(offset, number, freq_count, dir_count):
    component = offset + jnp.arange(number, dtype=jnp.int32)
    heading = TWO_PI * ((component // freq_count).astype(jnp.float32) + 0.5) / dir_count
    return (heading, component % freq_count)


def wind_term(heading, freq_index, freq_count, speed_flat, direction_flat):
    alignment = (
        jnp.cos(heading)[:, None] * jnp.cos(direction_flat)[None]
        + jnp.sin(heading)[:, None] * jnp.sin(direction_flat)[None]
    )
    scale_freq = (freq_index + 1).astype(jnp.float32) / freq_count
    return WIND_GAIN * scale_freq[:, None] * speed_flat[None] * jnp.maximum(alignment, 0.0)


def propagate_kernel(
    rx_ref, ry_ref, spec_ref, factor_ref, sea_ref, out_ref, sumsq_ref,
    send_first, send_last, recv_west, recv_east, send_sem, recv_sem,
    result_lo, result_hi, send_buf, a2a_send, a2a_recv, recv_buf,
):
    comps, rows, lons = spec_ref.shape
    spec_count = lax.axis_size("spec")
    grid_count = lax.axis_size("grid")
    chunk = rows // spec_count
    me = lax.axis_index("grid")
    spec = lax.axis_index("spec")
    right = lax.rem(me + 1, grid_count)
    left = lax.rem(me + grid_count - 1, grid_count)
    barrier = pltpu.get_barrier_semaphore()
    for neighbour in (left, right):
        pl.semaphore_signal(barrier, inc=1, device_id=(spec, neighbour), device_id_type=pl.DeviceIdType.MESH)

    def greet(d, carry):
        @pl.when(d != spec)
        def _():
            pl.semaphore_signal(barrier, inc=1, device_id=(d, me), device_id_type=pl.DeviceIdType.MESH)
        return carry

    lax.fori_loop(0, spec_count, greet, 0)
    pl.semaphore_wait(barrier, 2 + spec_count - 1)

    sea = sea_ref[...].astype(jnp.float32)
    factor = factor_ref[...] * sea
    edge_lane = lax.broadcasted_iota(jnp.int32, (rows, 128), 1)
    factor_first = factor[:, 0:1]
    factor_last = factor[:, lons - 1 : lons]

    def edges(kk, carry):
        first, last = carry
        rx = rx_ref[kk]
        s_first = spec_ref[kk, :, 0:128][:, 0:1]
        s_last = spec_ref[kk, :, lons - 128 : lons][:, 127:128]
        first = jnp.where(edge_lane == kk, rx * factor_first * s_first, first)
        last = jnp.where(edge_lane == kk, rx * factor_last * s_last, last)
        return first, last

    zero = jnp.zeros((rows, 128), jnp.float32)
    first, last = lax.fori_loop(0, comps, edges, (zero, zero), unroll=3)
    send_first[...] = first
    send_last[...] = last
    to_right = pltpu.make_async_remote_copy(
        src_ref=send_last, dst_ref=recv_west, send_sem=send_sem.at[0], recv_sem=recv_sem.at[0],
        device_id=(spec, right), device_id_type=pl.DeviceIdType.MESH,
    )
    to_left = pltpu.make_async_remote_copy(
        src_ref=send_first, dst_ref=recv_east, send_sem=send_sem.at[1], recv_sem=recv_sem.at[1],
        device_id=(spec, left), device_id_type=pl.DeviceIdType.MESH,
    )
    to_right.start()
    to_left.start()
    to_right.wait()
    to_left.wait()

    lane = lax.broadcasted_iota(jnp.int32, (rows, lons), 1)
    row = lax.broadcasted_iota(jnp.int32, (rows, lons), 0)

    def one(kk, carry):
        rx = rx_ref[kk]
        ry = ry_ref[kk]
        s = spec_ref[kk]
        west_col = jnp.sum(jnp.where(edge_lane == kk, recv_west[...], 0.0), axis=1, keepdims=True)
        east_col = jnp.sum(jnp.where(edge_lane == kk, recv_east[...], 0.0), axis=1, keepdims=True)
        fx = rx * factor * s
        west = jnp.where(lane == 0, west_col, pltpu.roll(fx, 1, 1))
        east = jnp.where(lane == lons - 1, east_col, pltpu.roll(fx, lons - 1, 1))
        change = jnp.where(rx > 0, fx - west, east - fx)
        ax = sea * (s - change)
        fy = ry * factor * ax
        south = jnp.where(row == 0, 0.0, pltpu.roll(fy, 1, 0))
        north = jnp.where(row == rows - 1, 0.0, pltpu.roll(fy, rows - 1, 0))
        change_y = jnp.where(ry > 0, fy - south, north - fy)
        res = sea * (ax - change_y)
        place = pl.ds(pl.multiple_of(kk * rows, rows), rows)
        result_lo[place, :] = res[:, :128]
        result_hi[place, :] = res[:, 128:]
        return carry

    def copy_to(d, slot, start, size):
        return pltpu.make_async_remote_copy(
            src_ref=send_buf.at[d, pl.ds(start, size)], dst_ref=recv_buf.at[slot, pl.ds(start, size)],
            send_sem=a2a_send.at[d], recv_sem=a2a_recv.at[slot], device_id=(d, me),
            device_id_type=pl.DeviceIdType.MESH,
        )

    tile = 16
    count = comps // tile
    blocks = [(tile * b, tile) for b in range(count - 1)]
    blocks.append((tile * (count - 1), comps - tile * (count - 1)))
    for start, size in blocks:
        lax.fori_loop(start, start + size, one, 0, unroll=4)

        def regroup(t, carry, start=start, size=size):
            d = lax.rem(spec + t, spec_count)
            for r in range(chunk):
                i = start * rows + d * chunk + r
                for half, part in ((0, result_lo), (1, result_hi)):
                    at = r * lons + half * 128
                    send_buf[d, pl.ds(start, size), at : at + 128] = part[
                        pl.ds(i, size, stride=rows), :
                    ].astype(send_buf.dtype)

            @pl.when(d != spec)
            def _():
                copy_to(d, spec, start, size).start()

            @pl.when(d == spec)
            def _():
                recv_buf[d, pl.ds(start, size), :] = send_buf[d, pl.ds(start, size), :]

            return carry

        lax.fori_loop(0, spec_count, regroup, 0, unroll=2)

    total = jnp.zeros(sumsq_ref.shape, jnp.float32)
    for s in range(spec_count):

        @pl.when(s != spec)
        def _():
            copy_to(s, s, 0, comps).wait_send()
            copy_to(s, s, 0, comps).wait_recv()

        part = recv_buf[s].astype(out_ref.dtype)
        out_ref[s * comps : (s + 1) * comps, :] = part
        total = total + jnp.sum(part * part, axis=0, keepdims=True)
    sumsq_ref[...] = total


def propagate(spectrum, rate_x, rate_y, factor, sea_float, spec_count):
    comps, rows, lons = spectrum.shape
    chunk = rows // spec_count
    smem = pl.BlockSpec(memory_space=pltpu.SMEM)
    vmem = pl.BlockSpec(memory_space=pltpu.VMEM)
    return pl.pallas_call(
        propagate_kernel,
        in_specs=[smem, smem, vmem, vmem, vmem],
        out_specs=[vmem, vmem],
        out_shape=[
            jax.ShapeDtypeStruct((spec_count * comps, chunk * lons), jnp.float32),
            jax.ShapeDtypeStruct((1, chunk * lons), jnp.float32),
        ],
        scratch_shapes=[
            pltpu.VMEM((rows, 128), jnp.float32),
            pltpu.VMEM((rows, 128), jnp.float32),
            pltpu.VMEM((rows, 128), jnp.float32),
            pltpu.VMEM((rows, 128), jnp.float32),
            pltpu.SemaphoreType.DMA((2,)),
            pltpu.SemaphoreType.DMA((2,)),
            pltpu.VMEM((comps * rows, 128), jnp.float32),
            pltpu.VMEM((comps * rows, 128), jnp.float32),
            pltpu.VMEM((spec_count, comps, chunk * lons), jnp.bfloat16),
            pltpu.SemaphoreType.DMA((spec_count,)),
            pltpu.SemaphoreType.DMA((spec_count,)),
            pltpu.VMEM((spec_count, comps, chunk * lons), jnp.bfloat16),
        ],
        compiler_params=pltpu.CompilerParams(
            collective_id=0, has_side_effects=True, vmem_limit_bytes=56 * 1024 * 1024
        ),
        cost_estimate=pl.CostEstimate(
            flops=30 * comps * rows * lons, bytes_accessed=6 * comps * rows * lons, transcendentals=0
        ),
    )(rate_x, rate_y, spectrum, factor, sea_float)


def local(
    spectrum,
    group_speed,
    depth_factor,
    sea_mask,
    interaction,
    wind_speed,
    wind_dir,
    nest_owner,
    nest_point,
    nest_cell,
    weight_index,
    weight_table,
):
    comp_dev = spectrum.shape[0]
    freq_count = group_speed.shape[0]
    comp_total = interaction.shape[0]
    dir_count = comp_total // freq_count
    spec_count = lax.axis_size("spec")
    grid_count = lax.axis_size("grid")
    heading, freq_index = headings(
        lax.axis_index("spec") * comp_dev, comp_dev, freq_count, dir_count
    )
    repeats = -(-(freq_count + comp_dev) // freq_count)
    group_rate = lax.dynamic_slice_in_dim(
        jnp.tile(group_speed, repeats), lax.rem(lax.axis_index("spec") * comp_dev, freq_count), comp_dev
    )
    rate_x = group_rate * jnp.cos(heading)
    rate_y = group_rate * jnp.sin(heading)
    sea_float = sea_mask.astype(jnp.float32)
    factor = depth_factor * sea_float
    lon_count = spectrum.shape[2]
    received, first_sumsq = propagate(spectrum, rate_x, rate_y, depth_factor, sea_mask, spec_count)
    row_count = spectrum.shape[1] // spec_count
    cell_count = row_count * lon_count
    spectra_now = received
    sea_rows = lax.dynamic_slice_in_dim(sea_float, lax.axis_index("spec") * row_count, row_count, 0)
    sea_cells = sea_rows.reshape(-1)
    all_heading, all_freq = headings(0, comp_total, freq_count, dir_count)
    wind_gain = wind_term(
        all_heading, all_freq, freq_count, wind_speed.reshape(-1), wind_dir.reshape(-1)
    )
    for step_number in range(SOURCE_STEPS):
        if step_number == 0:
            spread = jnp.sqrt(first_sumsq[0] / comp_total + EPSILON)
        else:
            spread = jnp.sqrt(jnp.mean(spectra_now * spectra_now, axis=0) + EPSILON)
        rounded = spectra_now.astype(jnp.bfloat16)
        transfer = jnp.dot(interaction, rounded, preferred_element_type=jnp.float32)
        spectra_now = (
            sea_cells[None]
            * (
                spectra_now
                + RATE * (wind_gain * spectra_now + spectra_now * transfer / spread[None])
            )
            / (1.0 + RATE * WHITECAP * spread[None])
        )

    slots = grid_count * CAP
    owners = nest_owner[:, 0]
    member = (owners[:, None] == jnp.arange(grid_count, dtype=jnp.int32)[None]).astype(jnp.int32)
    slot_rank = jnp.sum((jnp.cumsum(member, axis=0) - member) * member, axis=1)
    column = owners * CAP + slot_rank
    table_rows = weight_table.shape[0]
    weights = jnp.sum(
        jnp.where(
            weight_index[:, None] == jnp.arange(table_rows, dtype=jnp.int32)[None], weight_table[None], 0.0
        ),
        axis=1,
    )
    pick_slot = (column[:, None] == jnp.arange(slots, dtype=jnp.int32)[None]).astype(jnp.float32)
    pick_cell = (nest_cell[:, None] == jnp.arange(cell_count, dtype=jnp.int32)[None]).astype(jnp.float32)
    slot_cell = jnp.dot(pick_slot.T, pick_cell, precision=HIGHEST, preferred_element_type=jnp.float32)
    slot_weight = jnp.dot(pick_slot.T, weights, precision=HIGHEST, preferred_element_type=jnp.float32)
    slot_label = jnp.dot(
        pick_slot.T, nest_point.astype(jnp.float32) + 1.0, precision=HIGHEST,
        preferred_element_type=jnp.float32,
    ) - 1.0
    gathered = lax.dot_general(
        slot_cell, spectra_now, (((1,), (1,)), ((), ())), precision=lax.Precision.HIGH,
        preferred_element_type=jnp.float32,
    )
    send = jnp.concatenate([gathered * slot_weight[:, None], slot_label[:, None]], axis=1)
    send = send.astype(jnp.bfloat16).reshape(grid_count, CAP, comp_total + 1)
    arrived = lax.all_to_all(send, "grid", split_axis=0, concat_axis=0, tiled=True)
    arrived = arrived.reshape(slots, comp_total + 1)
    select = (arrived[:, comp_total][:, None] == jnp.arange(NB_OWN, dtype=jnp.bfloat16)[None]).astype(
        jnp.bfloat16
    )
    nest_spectra = lax.dot_general(
        arrived[:, :comp_total], select, (((0,), (0,)), ((), ())),
        preferred_element_type=jnp.float32,
    )
    return (spectra_now.reshape(comp_total, row_count, lon_count), nest_spectra)


def solution(mesh):
    in_specs = (
        P("spec", None, "grid"),
        P(),
        P(None, "grid"),
        P(None, "grid"),
        P(),
        P("spec", "grid"),
        P("spec", "grid"),
        P(("spec", "grid"), None),
        P(("spec", "grid")),
        P(("spec", "grid")),
        P(("spec", "grid")),
        P(),
    )
    out_specs = (P(None, "spec", "grid"), P(None, ("spec", "grid")))
    return jax.shard_map(local, mesh=mesh, in_specs=in_specs, out_specs=out_specs, check_vma=False)
```

```python
import functools
import math

import jax
import jax.numpy as jnp
from jax import lax
from jax.experimental import pallas as pl
from jax.experimental.pallas import tpu as pltpu
from jax.sharding import PartitionSpec as P

SOURCE_STEPS = 4
NB_OWN = 128
CAP = 16


TWO_PI = 2.0 * math.pi
RATE = 0.2
WIND_GAIN = 0.8
WHITECAP = 1.0
EPSILON = 1e-06
HIGHEST = lax.Precision.HIGHEST


def headings(offset, number, freq_count, dir_count):
    component = offset + jnp.arange(number, dtype=jnp.int32)
    heading = TWO_PI * ((component // freq_count).astype(jnp.float32) + 0.5) / dir_count
    return (heading, component % freq_count)


def wind_term(heading, freq_index, freq_count, speed_flat, direction_flat):
    alignment = (
        jnp.cos(heading)[:, None] * jnp.cos(direction_flat)[None]
        + jnp.sin(heading)[:, None] * jnp.sin(direction_flat)[None]
    )
    scale_freq = (freq_index + 1).astype(jnp.float32) / freq_count
    return WIND_GAIN * scale_freq[:, None] * speed_flat[None] * jnp.maximum(alignment, 0.0)


def propagate_kernel(
    rx_ref, ry_ref, spec_ref, factor_ref, sea_ref, out_ref, sumsq_ref,
    send_first, send_last, recv_west, recv_east, send_sem, recv_sem,
    result_lo, result_hi, send_buf, a2a_send, a2a_recv, recv_buf,
):
    comps, rows, lons = spec_ref.shape
    spec_count = lax.axis_size("spec")
    grid_count = lax.axis_size("grid")
    chunk = rows // spec_count
    me = lax.axis_index("grid")
    spec = lax.axis_index("spec")
    right = lax.rem(me + 1, grid_count)
    left = lax.rem(me + grid_count - 1, grid_count)
    barrier = pltpu.get_barrier_semaphore()
    for neighbour in (left, right):
        pl.semaphore_signal(barrier, inc=1, device_id=(spec, neighbour), device_id_type=pl.DeviceIdType.MESH)

    def greet(d, carry):
        @pl.when(d != spec)
        def _():
            pl.semaphore_signal(barrier, inc=1, device_id=(d, me), device_id_type=pl.DeviceIdType.MESH)
        return carry

    lax.fori_loop(0, spec_count, greet, 0)

    sea = sea_ref[...].astype(jnp.float32)
    factor = factor_ref[...] * sea
    edge_lane = lax.broadcasted_iota(jnp.int32, (rows, 128), 1)
    factor_first = factor[:, 0:1]
    factor_last = factor[:, lons - 1 : lons]

    def edges(kk, carry):
        first, last = carry
        rx = rx_ref[kk]
        s_first = spec_ref[kk, :, 0:128][:, 0:1]
        s_last = spec_ref[kk, :, lons - 128 : lons][:, 127:128]
        first = jnp.where(edge_lane == kk, rx * factor_first * s_first, first)
        last = jnp.where(edge_lane == kk, rx * factor_last * s_last, last)
        return first, last

    zero = jnp.zeros((rows, 128), jnp.float32)
    first, last = lax.fori_loop(0, comps, edges, (zero, zero), unroll=3)
    send_first[...] = first
    send_last[...] = last
    pl.semaphore_wait(barrier, 2 + spec_count - 1)
    to_right = pltpu.make_async_remote_copy(
        src_ref=send_last, dst_ref=recv_west, send_sem=send_sem.at[0], recv_sem=recv_sem.at[0],
        device_id=(spec, right), device_id_type=pl.DeviceIdType.MESH,
    )
    to_left = pltpu.make_async_remote_copy(
        src_ref=send_first, dst_ref=recv_east, send_sem=send_sem.at[1], recv_sem=recv_sem.at[1],
        device_id=(spec, left), device_id_type=pl.DeviceIdType.MESH,
    )
    to_right.start()
    to_left.start()
    to_right.wait()
    to_left.wait()

    lane = lax.broadcasted_iota(jnp.int32, (rows, lons), 1)
    row = lax.broadcasted_iota(jnp.int32, (rows, lons), 0)

    def one(kk, carry):
        rx = rx_ref[kk]
        ry = ry_ref[kk]
        s = spec_ref[kk]
        west_col = jnp.sum(jnp.where(edge_lane == kk, recv_west[...], 0.0), axis=1, keepdims=True)
        east_col = jnp.sum(jnp.where(edge_lane == kk, recv_east[...], 0.0), axis=1, keepdims=True)
        fx = rx * factor * s
        west = jnp.where(lane == 0, west_col, pltpu.roll(fx, 1, 1))
        east = jnp.where(lane == lons - 1, east_col, pltpu.roll(fx, lons - 1, 1))
        change = jnp.where(rx > 0, fx - west, east - fx)
        ax = sea * (s - change)
        fy = ry * factor * ax
        south = jnp.where(row == 0, 0.0, pltpu.roll(fy, 1, 0))
        north = jnp.where(row == rows - 1, 0.0, pltpu.roll(fy, rows - 1, 0))
        change_y = jnp.where(ry > 0, fy - south, north - fy)
        res = sea * (ax - change_y)
        place = pl.ds(pl.multiple_of(kk * rows, rows), rows)
        result_lo[place, :] = res[:, :128]
        result_hi[place, :] = res[:, 128:]
        return carry

    def copy_to(d, slot, start, size):
        return pltpu.make_async_remote_copy(
            src_ref=send_buf.at[d, pl.ds(start, size)], dst_ref=recv_buf.at[slot, pl.ds(start, size)],
            send_sem=a2a_send.at[d], recv_sem=a2a_recv.at[slot], device_id=(d, me),
            device_id_type=pl.DeviceIdType.MESH,
        )

    tile = 16
    count = comps // tile
    blocks = [(tile * b, tile) for b in range(count - 1)]
    blocks.append((tile * (count - 1), comps - tile * (count - 1)))
    for start, size in blocks:
        lax.fori_loop(start, start + size, one, 0, unroll=4)

        def regroup(t, carry, start=start, size=size):
            d = lax.rem(spec + t, spec_count)
            for r in range(chunk):
                i = start * rows + d * chunk + r
                for half, part in ((0, result_lo), (1, result_hi)):
                    at = r * lons + half * 128
                    send_buf[d, pl.ds(start, size), at : at + 128] = part[
                        pl.ds(i, size, stride=rows), :
                    ].astype(send_buf.dtype)

            @pl.when(d != spec)
            def _():
                copy_to(d, spec, start, size).start()

            @pl.when(d == spec)
            def _():
                recv_buf[d, pl.ds(start, size), :] = send_buf[d, pl.ds(start, size), :]

            return carry

        lax.fori_loop(0, spec_count, regroup, 0, unroll=2)

    def finish(d, carry):
        @pl.when(d != spec)
        def _():
            copy_to(d, d, 0, comps).wait_send()
            copy_to(d, d, 0, comps).wait_recv()

        return carry

    lax.fori_loop(0, spec_count, finish, 0)
    total = jnp.zeros(sumsq_ref.shape, jnp.float32)
    for s in range(spec_count):
        part = recv_buf[s].astype(out_ref.dtype)
        out_ref[s * comps : (s + 1) * comps, :] = part
        total = total + jnp.sum(part * part, axis=0, keepdims=True)
    sumsq_ref[...] = total


def propagate(spectrum, rate_x, rate_y, factor, sea_float, spec_count):
    comps, rows, lons = spectrum.shape
    chunk = rows // spec_count
    smem = pl.BlockSpec(memory_space=pltpu.SMEM)
    vmem = pl.BlockSpec(memory_space=pltpu.VMEM)
    return pl.pallas_call(
        propagate_kernel,
        in_specs=[smem, smem, vmem, vmem, vmem],
        out_specs=[vmem, vmem],
        out_shape=[
            jax.ShapeDtypeStruct((spec_count * comps, chunk * lons), jnp.float32),
            jax.ShapeDtypeStruct((1, chunk * lons), jnp.float32),
        ],
        scratch_shapes=[
            pltpu.VMEM((rows, 128), jnp.float32),
            pltpu.VMEM((rows, 128), jnp.float32),
            pltpu.VMEM((rows, 128), jnp.float32),
            pltpu.VMEM((rows, 128), jnp.float32),
            pltpu.SemaphoreType.DMA((2,)),
            pltpu.SemaphoreType.DMA((2,)),
            pltpu.VMEM((comps * rows, 128), jnp.float32),
            pltpu.VMEM((comps * rows, 128), jnp.float32),
            pltpu.VMEM((spec_count, comps, chunk * lons), jnp.bfloat16),
            pltpu.SemaphoreType.DMA((spec_count,)),
            pltpu.SemaphoreType.DMA((spec_count,)),
            pltpu.VMEM((spec_count, comps, chunk * lons), jnp.bfloat16),
        ],
        compiler_params=pltpu.CompilerParams(
            collective_id=0, has_side_effects=True, vmem_limit_bytes=56 * 1024 * 1024
        ),
        cost_estimate=pl.CostEstimate(
            flops=30 * comps * rows * lons, bytes_accessed=6 * comps * rows * lons, transcendentals=0
        ),
    )(rate_x, rate_y, spectrum, factor, sea_float)


def local(
    spectrum,
    group_speed,
    depth_factor,
    sea_mask,
    interaction,
    wind_speed,
    wind_dir,
    nest_owner,
    nest_point,
    nest_cell,
    weight_index,
    weight_table,
):
    comp_dev = spectrum.shape[0]
    freq_count = group_speed.shape[0]
    comp_total = interaction.shape[0]
    dir_count = comp_total // freq_count
    spec_count = lax.axis_size("spec")
    grid_count = lax.axis_size("grid")
    heading, freq_index = headings(
        lax.axis_index("spec") * comp_dev, comp_dev, freq_count, dir_count
    )
    repeats = -(-(freq_count + comp_dev) // freq_count)
    group_rate = lax.dynamic_slice_in_dim(
        jnp.tile(group_speed, repeats), lax.rem(lax.axis_index("spec") * comp_dev, freq_count), comp_dev
    )
    rate_x = group_rate * jnp.cos(heading)
    rate_y = group_rate * jnp.sin(heading)
    sea_float = sea_mask.astype(jnp.float32)
    factor = depth_factor * sea_float
    lon_count = spectrum.shape[2]
    received, first_sumsq = propagate(spectrum, rate_x, rate_y, depth_factor, sea_mask, spec_count)
    row_count = spectrum.shape[1] // spec_count
    cell_count = row_count * lon_count
    spectra_now = received
    sea_rows = lax.dynamic_slice_in_dim(sea_float, lax.axis_index("spec") * row_count, row_count, 0)
    sea_cells = sea_rows.reshape(-1)
    all_heading, all_freq = headings(0, comp_total, freq_count, dir_count)
    wind_gain = wind_term(
        all_heading, all_freq, freq_count, wind_speed.reshape(-1), wind_dir.reshape(-1)
    )
    for step_number in range(SOURCE_STEPS):
        if step_number == 0:
            spread = jnp.sqrt(first_sumsq[0] / comp_total + EPSILON)
        else:
            spread = jnp.sqrt(jnp.mean(spectra_now * spectra_now, axis=0) + EPSILON)
        rounded = spectra_now.astype(jnp.bfloat16)
        transfer = jnp.dot(interaction, rounded, preferred_element_type=jnp.float32)
        spectra_now = (
            sea_cells[None]
            * (
                spectra_now
                + RATE * (wind_gain * spectra_now + spectra_now * transfer / spread[None])
            )
            / (1.0 + RATE * WHITECAP * spread[None])
        )

    slots = grid_count * CAP
    owners = nest_owner[:, 0]
    member = (owners[:, None] == jnp.arange(grid_count, dtype=jnp.int32)[None]).astype(jnp.int32)
    slot_rank = jnp.sum((jnp.cumsum(member, axis=0) - member) * member, axis=1)
    column = owners * CAP + slot_rank
    table_rows = weight_table.shape[0]
    weights = jnp.sum(
        jnp.where(
            weight_index[:, None] == jnp.arange(table_rows, dtype=jnp.int32)[None], weight_table[None], 0.0
        ),
        axis=1,
    )
    pick_slot = (column[:, None] == jnp.arange(slots, dtype=jnp.int32)[None]).astype(jnp.float32)
    pick_cell = (nest_cell[:, None] == jnp.arange(cell_count, dtype=jnp.int32)[None]).astype(jnp.float32)
    slot_cell = jnp.dot(pick_slot.T, pick_cell, precision=HIGHEST, preferred_element_type=jnp.float32)
    slot_weight = jnp.dot(pick_slot.T, weights, precision=HIGHEST, preferred_element_type=jnp.float32)
    slot_label = jnp.dot(
        pick_slot.T, nest_point.astype(jnp.float32) + 1.0, precision=HIGHEST,
        preferred_element_type=jnp.float32,
    ) - 1.0
    gathered = lax.dot_general(
        slot_cell, spectra_now, (((1,), (1,)), ((), ())), precision=lax.Precision.HIGH,
        preferred_element_type=jnp.float32,
    )
    send = jnp.concatenate([gathered * slot_weight[:, None], slot_label[:, None]], axis=1)
    send = send.astype(jnp.bfloat16).reshape(grid_count, CAP, comp_total + 1)
    arrived = lax.all_to_all(send, "grid", split_axis=0, concat_axis=0, tiled=True)
    arrived = arrived.reshape(slots, comp_total + 1)
    select = (arrived[:, comp_total][:, None] == jnp.arange(NB_OWN, dtype=jnp.bfloat16)[None]).astype(
        jnp.bfloat16
    )
    nest_spectra = lax.dot_general(
        arrived[:, :comp_total], select, (((0,), (0,)), ((), ())),
        preferred_element_type=jnp.float32,
    )
    return (spectra_now.reshape(comp_total, row_count, lon_count), nest_spectra)


def solution(mesh):
    in_specs = (
        P("spec", None, "grid"),
        P(),
        P(None, "grid"),
        P(None, "grid"),
        P(),
        P("spec", "grid"),
        P("spec", "grid"),
        P(("spec", "grid"), None),
        P(("spec", "grid")),
        P(("spec", "grid")),
        P(("spec", "grid")),
        P(),
    )
    out_specs = (P(None, "spec", "grid"), P(None, ("spec", "grid")))
    return jax.shard_map(local, mesh=mesh, in_specs=in_specs, out_specs=out_specs, check_vma=False)
```

```python
import functools
import math

import jax
import jax.numpy as jnp
from jax import lax
from jax.experimental import pallas as pl
from jax.experimental.pallas import tpu as pltpu
from jax.sharding import PartitionSpec as P

SOURCE_STEPS = 4
NB_OWN = 128
CAP = 16


TWO_PI = 2.0 * math.pi
RATE = 0.2
WIND_GAIN = 0.8
WHITECAP = 1.0
EPSILON = 1e-06
HIGHEST = lax.Precision.HIGHEST


def headings(offset, number, freq_count, dir_count):
    component = offset + jnp.arange(number, dtype=jnp.int32)
    heading = TWO_PI * ((component // freq_count).astype(jnp.float32) + 0.5) / dir_count
    return (heading, component % freq_count)


def wind_term(heading, freq_index, freq_count, speed_flat, direction_flat):
    alignment = (
        jnp.cos(heading)[:, None] * jnp.cos(direction_flat)[None]
        + jnp.sin(heading)[:, None] * jnp.sin(direction_flat)[None]
    )
    scale_freq = (freq_index + 1).astype(jnp.float32) / freq_count
    return WIND_GAIN * scale_freq[:, None] * speed_flat[None] * jnp.maximum(alignment, 0.0)


def propagate_kernel(
    rx_ref, ry_ref, spec_ref, factor_ref, sea_ref, out_ref, sumsq_ref,
    send_first, send_last, recv_west, recv_east, send_sem, recv_sem,
    result_lo, result_hi, send_buf, a2a_send, a2a_recv, recv_buf,
):
    comps, rows, lons = spec_ref.shape
    spec_count = lax.axis_size("spec")
    grid_count = lax.axis_size("grid")
    chunk = rows // spec_count
    me = lax.axis_index("grid")
    spec = lax.axis_index("spec")
    right = lax.rem(me + 1, grid_count)
    left = lax.rem(me + grid_count - 1, grid_count)
    barrier = pltpu.get_barrier_semaphore()
    for neighbour in (left, right):
        pl.semaphore_signal(barrier, inc=1, device_id=(spec, neighbour), device_id_type=pl.DeviceIdType.MESH)

    def greet(d, carry):
        @pl.when(d != spec)
        def _():
            pl.semaphore_signal(barrier, inc=1, device_id=(d, me), device_id_type=pl.DeviceIdType.MESH)
        return carry

    lax.fori_loop(0, spec_count, greet, 0)

    sea = sea_ref[...].astype(jnp.float32)
    factor = factor_ref[...] * sea
    edge_lane = lax.broadcasted_iota(jnp.int32, (rows, 128), 1)
    factor_first = factor[:, 0:1]
    factor_last = factor[:, lons - 1 : lons]

    def edges(kk, carry):
        first, last = carry
        rx = rx_ref[kk]
        s_first = spec_ref[kk, :, 0:128][:, 0:1]
        s_last = spec_ref[kk, :, lons - 128 : lons][:, 127:128]
        first = jnp.where(edge_lane == kk, rx * factor_first * s_first, first)
        last = jnp.where(edge_lane == kk, rx * factor_last * s_last, last)
        return first, last

    zero = jnp.zeros((rows, 128), jnp.float32)
    first, last = lax.fori_loop(0, comps, edges, (zero, zero), unroll=3)
    send_first[...] = first
    send_last[...] = last
    pl.semaphore_wait(barrier, 2 + spec_count - 1)
    to_right = pltpu.make_async_remote_copy(
        src_ref=send_last, dst_ref=recv_west, send_sem=send_sem.at[0], recv_sem=recv_sem.at[0],
        device_id=(spec, right), device_id_type=pl.DeviceIdType.MESH,
    )
    to_left = pltpu.make_async_remote_copy(
        src_ref=send_first, dst_ref=recv_east, send_sem=send_sem.at[1], recv_sem=recv_sem.at[1],
        device_id=(spec, left), device_id_type=pl.DeviceIdType.MESH,
    )
    to_right.start()
    to_left.start()
    to_right.wait()
    to_left.wait()

    lane = lax.broadcasted_iota(jnp.int32, (rows, lons), 1)
    row = lax.broadcasted_iota(jnp.int32, (rows, lons), 0)

    def one(kk, carry):
        rx = rx_ref[kk]
        ry = ry_ref[kk]
        s = spec_ref[kk]
        west_col = jnp.sum(jnp.where(edge_lane == kk, recv_west[...], 0.0), axis=1, keepdims=True)
        east_col = jnp.sum(jnp.where(edge_lane == kk, recv_east[...], 0.0), axis=1, keepdims=True)
        fx = rx * factor * s
        west = jnp.where(lane == 0, west_col, pltpu.roll(fx, 1, 1))
        east = jnp.where(lane == lons - 1, east_col, pltpu.roll(fx, lons - 1, 1))
        change = jnp.where(rx > 0, fx - west, east - fx)
        ax = sea * (s - change)
        fy = ry * factor * ax
        south = jnp.where(row == 0, 0.0, pltpu.roll(fy, 1, 0))
        north = jnp.where(row == rows - 1, 0.0, pltpu.roll(fy, rows - 1, 0))
        change_y = jnp.where(ry > 0, fy - south, north - fy)
        res = sea * (ax - change_y)
        place = pl.ds(pl.multiple_of(kk * rows, rows), rows)
        result_lo[place, :] = res[:, :128]
        result_hi[place, :] = res[:, 128:]
        return carry

    def copy_to(d, slot, start, size):
        return pltpu.make_async_remote_copy(
            src_ref=send_buf.at[d, pl.ds(start, size)], dst_ref=recv_buf.at[slot, pl.ds(start, size)],
            send_sem=a2a_send.at[d], recv_sem=a2a_recv.at[slot], device_id=(d, me),
            device_id_type=pl.DeviceIdType.MESH,
        )

    tile = 16
    count = comps // tile
    blocks = [(tile * b, tile) for b in range(count - 1)]
    blocks.append((tile * (count - 1), comps - tile * (count - 1)))
    for start, size in blocks:
        lax.fori_loop(start, start + size, one, 0, unroll=8)

        def regroup(t, carry, start=start, size=size):
            d = lax.rem(spec + t, spec_count)
            for r in range(chunk):
                i = start * rows + d * chunk + r
                for half, part in ((0, result_lo), (1, result_hi)):
                    at = r * lons + half * 128
                    send_buf[d, pl.ds(start, size), at : at + 128] = part[
                        pl.ds(i, size, stride=rows), :
                    ].astype(send_buf.dtype)

            @pl.when(d != spec)
            def _():
                copy_to(d, spec, start, size).start()

            @pl.when(d == spec)
            def _():
                recv_buf[d, pl.ds(start, size), :] = send_buf[d, pl.ds(start, size), :]

            return carry

        lax.fori_loop(0, spec_count, regroup, 0, unroll=2)

    def finish(d, carry):
        @pl.when(d != spec)
        def _():
            copy_to(d, d, 0, comps).wait_send()
            copy_to(d, d, 0, comps).wait_recv()

        return carry

    lax.fori_loop(0, spec_count, finish, 0)
    total = jnp.zeros(sumsq_ref.shape, jnp.float32)
    for s in range(spec_count):
        part = recv_buf[s].astype(out_ref.dtype)
        out_ref[s * comps : (s + 1) * comps, :] = part
        total = total + jnp.sum(part * part, axis=0, keepdims=True)
    sumsq_ref[...] = total


def propagate(spectrum, rate_x, rate_y, factor, sea_float, spec_count):
    comps, rows, lons = spectrum.shape
    chunk = rows // spec_count
    smem = pl.BlockSpec(memory_space=pltpu.SMEM)
    vmem = pl.BlockSpec(memory_space=pltpu.VMEM)
    return pl.pallas_call(
        propagate_kernel,
        in_specs=[smem, smem, vmem, vmem, vmem],
        out_specs=[vmem, vmem],
        out_shape=[
            jax.ShapeDtypeStruct((spec_count * comps, chunk * lons), jnp.float32),
            jax.ShapeDtypeStruct((1, chunk * lons), jnp.float32),
        ],
        scratch_shapes=[
            pltpu.VMEM((rows, 128), jnp.float32),
            pltpu.VMEM((rows, 128), jnp.float32),
            pltpu.VMEM((rows, 128), jnp.float32),
            pltpu.VMEM((rows, 128), jnp.float32),
            pltpu.SemaphoreType.DMA((2,)),
            pltpu.SemaphoreType.DMA((2,)),
            pltpu.VMEM((comps * rows, 128), jnp.float32),
            pltpu.VMEM((comps * rows, 128), jnp.float32),
            pltpu.VMEM((spec_count, comps, chunk * lons), jnp.bfloat16),
            pltpu.SemaphoreType.DMA((spec_count,)),
            pltpu.SemaphoreType.DMA((spec_count,)),
            pltpu.VMEM((spec_count, comps, chunk * lons), jnp.bfloat16),
        ],
        compiler_params=pltpu.CompilerParams(
            collective_id=0, has_side_effects=True, vmem_limit_bytes=56 * 1024 * 1024
        ),
        cost_estimate=pl.CostEstimate(
            flops=30 * comps * rows * lons, bytes_accessed=6 * comps * rows * lons, transcendentals=0
        ),
    )(rate_x, rate_y, spectrum, factor, sea_float)


def local(
    spectrum,
    group_speed,
    depth_factor,
    sea_mask,
    interaction,
    wind_speed,
    wind_dir,
    nest_owner,
    nest_point,
    nest_cell,
    weight_index,
    weight_table,
):
    comp_dev = spectrum.shape[0]
    freq_count = group_speed.shape[0]
    comp_total = interaction.shape[0]
    dir_count = comp_total // freq_count
    spec_count = lax.axis_size("spec")
    grid_count = lax.axis_size("grid")
    heading, freq_index = headings(
        lax.axis_index("spec") * comp_dev, comp_dev, freq_count, dir_count
    )
    repeats = -(-(freq_count + comp_dev) // freq_count)
    group_rate = lax.dynamic_slice_in_dim(
        jnp.tile(group_speed, repeats), lax.rem(lax.axis_index("spec") * comp_dev, freq_count), comp_dev
    )
    rate_x = group_rate * jnp.cos(heading)
    rate_y = group_rate * jnp.sin(heading)
    sea_float = sea_mask.astype(jnp.float32)
    factor = depth_factor * sea_float
    lon_count = spectrum.shape[2]
    received, first_sumsq = propagate(spectrum, rate_x, rate_y, depth_factor, sea_mask, spec_count)
    row_count = spectrum.shape[1] // spec_count
    cell_count = row_count * lon_count
    spectra_now = received
    sea_rows = lax.dynamic_slice_in_dim(sea_float, lax.axis_index("spec") * row_count, row_count, 0)
    sea_cells = sea_rows.reshape(-1)
    all_heading, all_freq = headings(0, comp_total, freq_count, dir_count)
    wind_gain = wind_term(
        all_heading, all_freq, freq_count, wind_speed.reshape(-1), wind_dir.reshape(-1)
    )
    for step_number in range(SOURCE_STEPS):
        if step_number == 0:
            spread = jnp.sqrt(first_sumsq[0] / comp_total + EPSILON)
        else:
            spread = jnp.sqrt(jnp.mean(spectra_now * spectra_now, axis=0) + EPSILON)
        rounded = spectra_now.astype(jnp.bfloat16)
        transfer = jnp.dot(interaction, rounded, preferred_element_type=jnp.float32)
        spectra_now = (
            sea_cells[None]
            * (
                spectra_now
                + RATE * (wind_gain * spectra_now + spectra_now * transfer / spread[None])
            )
            / (1.0 + RATE * WHITECAP * spread[None])
        )

    slots = grid_count * CAP
    owners = nest_owner[:, 0]
    member = (owners[:, None] == jnp.arange(grid_count, dtype=jnp.int32)[None]).astype(jnp.int32)
    slot_rank = jnp.sum((jnp.cumsum(member, axis=0) - member) * member, axis=1)
    column = owners * CAP + slot_rank
    table_rows = weight_table.shape[0]
    weights = jnp.sum(
        jnp.where(
            weight_index[:, None] == jnp.arange(table_rows, dtype=jnp.int32)[None], weight_table[None], 0.0
        ),
        axis=1,
    )
    pick_slot = (column[:, None] == jnp.arange(slots, dtype=jnp.int32)[None]).astype(jnp.float32)
    pick_cell = (nest_cell[:, None] == jnp.arange(cell_count, dtype=jnp.int32)[None]).astype(jnp.float32)
    slot_cell = jnp.dot(pick_slot.T, pick_cell, precision=HIGHEST, preferred_element_type=jnp.float32)
    slot_weight = jnp.dot(pick_slot.T, weights, precision=HIGHEST, preferred_element_type=jnp.float32)
    slot_label = jnp.dot(
        pick_slot.T, nest_point.astype(jnp.float32) + 1.0, precision=HIGHEST,
        preferred_element_type=jnp.float32,
    ) - 1.0
    gathered = lax.dot_general(
        slot_cell, spectra_now, (((1,), (1,)), ((), ())), precision=lax.Precision.HIGH,
        preferred_element_type=jnp.float32,
    )
    send = jnp.concatenate([gathered * slot_weight[:, None], slot_label[:, None]], axis=1)
    send = send.astype(jnp.bfloat16).reshape(grid_count, CAP, comp_total + 1)
    arrived = lax.all_to_all(send, "grid", split_axis=0, concat_axis=0, tiled=True)
    arrived = arrived.reshape(slots, comp_total + 1)
    select = (arrived[:, comp_total][:, None] == jnp.arange(NB_OWN, dtype=jnp.bfloat16)[None]).astype(
        jnp.bfloat16
    )
    nest_spectra = lax.dot_general(
        arrived[:, :comp_total], select, (((0,), (0,)), ((), ())),
        preferred_element_type=jnp.float32,
    )
    return (spectra_now.reshape(comp_total, row_count, lon_count), nest_spectra)


def solution(mesh):
    in_specs = (
        P("spec", None, "grid"),
        P(),
        P(None, "grid"),
        P(None, "grid"),
        P(),
        P("spec", "grid"),
        P("spec", "grid"),
        P(("spec", "grid"), None),
        P(("spec", "grid")),
        P(("spec", "grid")),
        P(("spec", "grid")),
        P(),
    )
    out_specs = (P(None, "spec", "grid"), P(None, ("spec", "grid")))
    return jax.shard_map(local, mesh=mesh, in_specs=in_specs, out_specs=out_specs, check_vma=False)
```

```python
import functools
import math

import jax
import jax.numpy as jnp
from jax import lax
from jax.experimental import pallas as pl
from jax.experimental.pallas import tpu as pltpu
from jax.sharding import PartitionSpec as P

SOURCE_STEPS = 4
NB_OWN = 128
CAP = 16


TWO_PI = 2.0 * math.pi
RATE = 0.2
WIND_GAIN = 0.8
WHITECAP = 1.0
EPSILON = 1e-06
HIGHEST = lax.Precision.HIGHEST


def headings(offset, number, freq_count, dir_count):
    component = offset + jnp.arange(number, dtype=jnp.int32)
    heading = TWO_PI * ((component // freq_count).astype(jnp.float32) + 0.5) / dir_count
    return (heading, component % freq_count)


def wind_term(heading, freq_index, freq_count, speed_flat, direction_flat):
    alignment = (
        jnp.cos(heading)[:, None] * jnp.cos(direction_flat)[None]
        + jnp.sin(heading)[:, None] * jnp.sin(direction_flat)[None]
    )
    scale_freq = (freq_index + 1).astype(jnp.float32) / freq_count
    return WIND_GAIN * scale_freq[:, None] * speed_flat[None] * jnp.maximum(alignment, 0.0)


def propagate_kernel(
    rx_ref, ry_ref, spec_ref, factor_ref, sea_ref, out_ref, sumsq_ref,
    send_first, send_last, recv_west, recv_east, send_sem, recv_sem,
    result_lo, result_hi, send_buf, a2a_send, a2a_recv, recv_buf,
):
    comps, rows, lons = spec_ref.shape
    spec_count = lax.axis_size("spec")
    grid_count = lax.axis_size("grid")
    chunk = rows // spec_count
    me = lax.axis_index("grid")
    spec = lax.axis_index("spec")
    right = lax.rem(me + 1, grid_count)
    left = lax.rem(me + grid_count - 1, grid_count)
    barrier = pltpu.get_barrier_semaphore()
    for neighbour in (left, right):
        pl.semaphore_signal(barrier, inc=1, device_id=(spec, neighbour), device_id_type=pl.DeviceIdType.MESH)

    def greet(d, carry):
        @pl.when(d != spec)
        def _():
            pl.semaphore_signal(barrier, inc=1, device_id=(d, me), device_id_type=pl.DeviceIdType.MESH)
        return carry

    lax.fori_loop(0, spec_count, greet, 0)

    sea = sea_ref[...].astype(jnp.float32)
    factor = factor_ref[...] * sea
    edge_lane = lax.broadcasted_iota(jnp.int32, (rows, 128), 1)
    factor_first = factor[:, 0:1]
    factor_last = factor[:, lons - 1 : lons]

    def edges(kk, carry):
        first, last = carry
        rx = rx_ref[kk]
        s_first = spec_ref[kk, :, 0:128][:, 0:1]
        s_last = spec_ref[kk, :, lons - 128 : lons][:, 127:128]
        first = jnp.where(edge_lane == kk, rx * factor_first * s_first, first)
        last = jnp.where(edge_lane == kk, rx * factor_last * s_last, last)
        return first, last

    zero = jnp.zeros((rows, 128), jnp.float32)
    first, last = lax.fori_loop(0, comps, edges, (zero, zero), unroll=3)
    send_first[...] = first
    send_last[...] = last
    pl.semaphore_wait(barrier, 2 + spec_count - 1)
    to_right = pltpu.make_async_remote_copy(
        src_ref=send_last, dst_ref=recv_west, send_sem=send_sem.at[0], recv_sem=recv_sem.at[0],
        device_id=(spec, right), device_id_type=pl.DeviceIdType.MESH,
    )
    to_left = pltpu.make_async_remote_copy(
        src_ref=send_first, dst_ref=recv_east, send_sem=send_sem.at[1], recv_sem=recv_sem.at[1],
        device_id=(spec, left), device_id_type=pl.DeviceIdType.MESH,
    )
    to_right.start()
    to_left.start()
    to_right.wait()
    to_left.wait()

    lane = lax.broadcasted_iota(jnp.int32, (rows, lons), 1)
    row = lax.broadcasted_iota(jnp.int32, (rows, lons), 0)

    def one(kk, carry):
        rx = rx_ref[kk]
        ry = ry_ref[kk]
        s = spec_ref[kk]
        west_col = jnp.sum(jnp.where(edge_lane == kk, recv_west[...], 0.0), axis=1, keepdims=True)
        east_col = jnp.sum(jnp.where(edge_lane == kk, recv_east[...], 0.0), axis=1, keepdims=True)
        fx = rx * factor * s
        west = jnp.where(lane == 0, west_col, pltpu.roll(fx, 1, 1))
        east = jnp.where(lane == lons - 1, east_col, pltpu.roll(fx, lons - 1, 1))
        change = jnp.where(rx > 0, fx - west, east - fx)
        ax = sea * (s - change)
        fy = ry * factor * ax
        south = jnp.where(row == 0, 0.0, pltpu.roll(fy, 1, 0))
        north = jnp.where(row == rows - 1, 0.0, pltpu.roll(fy, rows - 1, 0))
        change_y = jnp.where(ry > 0, fy - south, north - fy)
        res = sea * (ax - change_y)
        place = pl.ds(pl.multiple_of(kk * rows, rows), rows)
        result_lo[place, :] = res[:, :128]
        result_hi[place, :] = res[:, 128:]
        return carry

    def copy_to(d, slot, start, size):
        return pltpu.make_async_remote_copy(
            src_ref=send_buf.at[d, pl.ds(start, size)], dst_ref=recv_buf.at[slot, pl.ds(start, size)],
            send_sem=a2a_send.at[d], recv_sem=a2a_recv.at[slot], device_id=(d, me),
            device_id_type=pl.DeviceIdType.MESH,
        )

    tile = 16
    count = comps // tile
    blocks = [(tile * b, tile) for b in range(count - 1)]
    blocks.append((tile * (count - 1), comps - tile * (count - 1)))
    for start, size in blocks:
        lax.fori_loop(start, start + size, one, 0, unroll=4)

        def regroup(t, carry, start=start, size=size):
            d = lax.rem(spec + t, spec_count)
            for r in range(chunk):
                i = start * rows + d * chunk + r
                for half, part in ((0, result_lo), (1, result_hi)):
                    at = r * lons + half * 128
                    send_buf[d, pl.ds(start, size), at : at + 128] = part[
                        pl.ds(i, size, stride=rows), :
                    ].astype(send_buf.dtype)

            @pl.when(d != spec)
            def _():
                copy_to(d, spec, start, size).start()

            @pl.when(d == spec)
            def _():
                recv_buf[d, pl.ds(start, size), :] = send_buf[d, pl.ds(start, size), :]

            return carry

        lax.fori_loop(0, spec_count, regroup, 0, unroll=4)

    def finish(d, carry):
        @pl.when(d != spec)
        def _():
            copy_to(d, d, 0, comps).wait_send()
            copy_to(d, d, 0, comps).wait_recv()

        return carry

    lax.fori_loop(0, spec_count, finish, 0)
    total = jnp.zeros(sumsq_ref.shape, jnp.float32)
    for s in range(spec_count):
        part = recv_buf[s].astype(out_ref.dtype)
        out_ref[s * comps : (s + 1) * comps, :] = part
        total = total + jnp.sum(part * part, axis=0, keepdims=True)
    sumsq_ref[...] = total


def propagate(spectrum, rate_x, rate_y, factor, sea_float, spec_count):
    comps, rows, lons = spectrum.shape
    chunk = rows // spec_count
    smem = pl.BlockSpec(memory_space=pltpu.SMEM)
    vmem = pl.BlockSpec(memory_space=pltpu.VMEM)
    return pl.pallas_call(
        propagate_kernel,
        in_specs=[smem, smem, vmem, vmem, vmem],
        out_specs=[vmem, vmem],
        out_shape=[
            jax.ShapeDtypeStruct((spec_count * comps, chunk * lons), jnp.float32),
            jax.ShapeDtypeStruct((1, chunk * lons), jnp.float32),
        ],
        scratch_shapes=[
            pltpu.VMEM((rows, 128), jnp.float32),
            pltpu.VMEM((rows, 128), jnp.float32),
            pltpu.VMEM((rows, 128), jnp.float32),
            pltpu.VMEM((rows, 128), jnp.float32),
            pltpu.SemaphoreType.DMA((2,)),
            pltpu.SemaphoreType.DMA((2,)),
            pltpu.VMEM((comps * rows, 128), jnp.float32),
            pltpu.VMEM((comps * rows, 128), jnp.float32),
            pltpu.VMEM((spec_count, comps, chunk * lons), jnp.bfloat16),
            pltpu.SemaphoreType.DMA((spec_count,)),
            pltpu.SemaphoreType.DMA((spec_count,)),
            pltpu.VMEM((spec_count, comps, chunk * lons), jnp.bfloat16),
        ],
        compiler_params=pltpu.CompilerParams(
            collective_id=0, has_side_effects=True, vmem_limit_bytes=56 * 1024 * 1024
        ),
        cost_estimate=pl.CostEstimate(
            flops=30 * comps * rows * lons, bytes_accessed=6 * comps * rows * lons, transcendentals=0
        ),
    )(rate_x, rate_y, spectrum, factor, sea_float)


def local(
    spectrum,
    group_speed,
    depth_factor,
    sea_mask,
    interaction,
    wind_speed,
    wind_dir,
    nest_owner,
    nest_point,
    nest_cell,
    weight_index,
    weight_table,
):
    comp_dev = spectrum.shape[0]
    freq_count = group_speed.shape[0]
    comp_total = interaction.shape[0]
    dir_count = comp_total // freq_count
    spec_count = lax.axis_size("spec")
    grid_count = lax.axis_size("grid")
    heading, freq_index = headings(
        lax.axis_index("spec") * comp_dev, comp_dev, freq_count, dir_count
    )
    repeats = -(-(freq_count + comp_dev) // freq_count)
    group_rate = lax.dynamic_slice_in_dim(
        jnp.tile(group_speed, repeats), lax.rem(lax.axis_index("spec") * comp_dev, freq_count), comp_dev
    )
    rate_x = group_rate * jnp.cos(heading)
    rate_y = group_rate * jnp.sin(heading)
    sea_float = sea_mask.astype(jnp.float32)
    factor = depth_factor * sea_float
    lon_count = spectrum.shape[2]
    received, first_sumsq = propagate(spectrum, rate_x, rate_y, depth_factor, sea_mask, spec_count)
    row_count = spectrum.shape[1] // spec_count
    cell_count = row_count * lon_count
    spectra_now = received
    sea_rows = lax.dynamic_slice_in_dim(sea_float, lax.axis_index("spec") * row_count, row_count, 0)
    sea_cells = sea_rows.reshape(-1)
    all_heading, all_freq = headings(0, comp_total, freq_count, dir_count)
    wind_gain = wind_term(
        all_heading, all_freq, freq_count, wind_speed.reshape(-1), wind_dir.reshape(-1)
    )
    for step_number in range(SOURCE_STEPS):
        if step_number == 0:
            spread = jnp.sqrt(first_sumsq[0] / comp_total + EPSILON)
        else:
            spread = jnp.sqrt(jnp.mean(spectra_now * spectra_now, axis=0) + EPSILON)
        rounded = spectra_now.astype(jnp.bfloat16)
        transfer = jnp.dot(interaction, rounded, preferred_element_type=jnp.float32)
        spectra_now = (
            sea_cells[None]
            * (
                spectra_now
                + RATE * (wind_gain * spectra_now + spectra_now * transfer / spread[None])
            )
            / (1.0 + RATE * WHITECAP * spread[None])
        )

    slots = grid_count * CAP
    owners = nest_owner[:, 0]
    member = (owners[:, None] == jnp.arange(grid_count, dtype=jnp.int32)[None]).astype(jnp.int32)
    slot_rank = jnp.sum((jnp.cumsum(member, axis=0) - member) * member, axis=1)
    column = owners * CAP + slot_rank
    table_rows = weight_table.shape[0]
    weights = jnp.sum(
        jnp.where(
            weight_index[:, None] == jnp.arange(table_rows, dtype=jnp.int32)[None], weight_table[None], 0.0
        ),
        axis=1,
    )
    pick_slot = (column[:, None] == jnp.arange(slots, dtype=jnp.int32)[None]).astype(jnp.float32)
    pick_cell = (nest_cell[:, None] == jnp.arange(cell_count, dtype=jnp.int32)[None]).astype(jnp.float32)
    slot_cell = jnp.dot(pick_slot.T, pick_cell, precision=HIGHEST, preferred_element_type=jnp.float32)
    slot_weight = jnp.dot(pick_slot.T, weights, precision=HIGHEST, preferred_element_type=jnp.float32)
    slot_label = jnp.dot(
        pick_slot.T, nest_point.astype(jnp.float32) + 1.0, precision=HIGHEST,
        preferred_element_type=jnp.float32,
    ) - 1.0
    gathered = lax.dot_general(
        slot_cell, spectra_now, (((1,), (1,)), ((), ())), precision=lax.Precision.HIGH,
        preferred_element_type=jnp.float32,
    )
    send = jnp.concatenate([gathered * slot_weight[:, None], slot_label[:, None]], axis=1)
    send = send.astype(jnp.bfloat16).reshape(grid_count, CAP, comp_total + 1)
    arrived = lax.all_to_all(send, "grid", split_axis=0, concat_axis=0, tiled=True)
    arrived = arrived.reshape(slots, comp_total + 1)
    select = (arrived[:, comp_total][:, None] == jnp.arange(NB_OWN, dtype=jnp.bfloat16)[None]).astype(
        jnp.bfloat16
    )
    nest_spectra = lax.dot_general(
        arrived[:, :comp_total], select, (((0,), (0,)), ((), ())),
        preferred_element_type=jnp.float32,
    )
    return (spectra_now.reshape(comp_total, row_count, lon_count), nest_spectra)


def solution(mesh):
    in_specs = (
        P("spec", None, "grid"),
        P(),
        P(None, "grid"),
        P(None, "grid"),
        P(),
        P("spec", "grid"),
        P("spec", "grid"),
        P(("spec", "grid"), None),
        P(("spec", "grid")),
        P(("spec", "grid")),
        P(("spec", "grid")),
        P(),
    )
    out_specs = (P(None, "spec", "grid"), P(None, ("spec", "grid")))
    return jax.shard_map(local, mesh=mesh, in_specs=in_specs, out_specs=out_specs, check_vma=False)
```
